32 devices in a mesh: groups: 2 (over y), patch: 4 (over z), sub: 4 (over x, core).
Axes of the slice: x: 2, y: 2, z: 4, core: 2. Of those that a mesh axis runs over, the one named last changes fastest.
Arguments:
- fine_nodes: float32 [32768, 128], P(('groups', 'patch', 'sub')), parts along dimension 0, may hold values from -6 to 6
- fine_edges: float32 [32768, 6, 128], P(('groups', 'patch', 'sub')), parts along dimension 0, may hold values from -6 to 6
- fine_senders: int32 [32768, 6], P(('groups', 'patch', 'sub')), parts along dimension 0, may hold values from 0 to 1279
- fine_halo: int32 [64, 128], P(('groups', 'patch', 'sub')), parts along dimension 0, may hold values from 0 to 1023
- fine_pool: int32 [32768], P(('groups', 'patch', 'sub')), parts along dimension 0, may hold values from 0 to 1023, as said below
- quarter_edges: float32 [8192, 4, 128], P(('groups', 'patch')), parts along dimension 0, may hold values from -6 to 6
- quarter_senders: int32 [8192, 4], P(('groups', 'patch')), parts along dimension 0, may hold values from 0 to 1279
- quarter_halo: int32 [16, 128], P(('groups', 'patch')), parts along dimension 0, may hold values from 0 to 1023
- quarter_pool: int32 [8192], P(('groups', 'patch')), parts along dimension 0, may hold values from 0 to 255, as said below
- coarse_edges: float32 [2048, 4, 128], P(('groups', 'patch', 'sub')), parts along dimension 0, may hold values from -6 to 6
- coarse_senders: int32 [2048, 4], P('groups'), parts along dimension 0, may hold values from 0 to 1023
- edge_in: float32 [3, 384, 128], replicated, may hold values from -0.3125 to 0.3125
- edge_out: float32 [3, 128, 128], replicated, may hold values from -0.5 to 0.5
- node_in: float32 [3, 256, 128], replicated, may hold values from -0.375 to 0.375
- node_out: float32 [3, 128, 128], replicated, may hold values from -0.5 to 0.5
Outputs:
- fine_out: float32 [32768, 128], P(('groups', 'patch', 'sub')), parts along dimension 0
The draws below stay inside these ranges and needn't reach their ends.
There are 2 independent parts, one for each index of `groups`. The reference program is written for one: setup_inputs(seed, part) draws one part's arguments, and reference() takes and returns one part's arrays. A program takes and returns all parts, laid end to end along the dimension named above; an argument that names none is the same for every part. Nothing has to cross between parts.
Inputs may be any that keep to these rules, and one draw needn't show every extreme that they name: `fine_pool`: every one of a patch's 1024 quarter nodes is the target of at least one fine node of that patch. `quarter_pool`: every one of a patch's 256 sixteenth nodes is the target of at least one quarter node of that patch.
All inputs are finite; a program needn't handle non-finite values.
Results may differ from the reference program's by a relative error of at most 0.00005.
Values sent between devices are 32-bit elements; how exact they have to be, the bound alone decides.
No kernel may reach another device: no remote copies, remote signals or barrier semaphores. Data moves between devices by JAX's collectives and lax.ppermute only.
A program may use at most 128 MiB of HBM per device.

```python
import jax
import jax.numpy as jnp
from jax import lax

W = 128
NF_DEV = 1024
K_F = 6
K_Q = 4
K_S = 4
HALO = 128
HALO_Q = 128
QUARTER_PATCH = 1024
SIXTEENTH_PATCH = 256
NF = 16384
NQ = 4096
NS = 1024
N_PATCH = 4
N_SUB = 4


def covering(key, blocks, block_size, targets):

    def one_block(block_key):
        first_key, second_key = jax.random.split(block_key)
        extra = jax.random.randint(first_key, (block_size - targets,), 0, targets, dtype=jnp.int32)
        labels = jnp.concatenate([jnp.arange(targets, dtype=jnp.int32), extra])
        return jax.random.permutation(second_key, labels)
    block_keys = jax.random.split(key, blocks)
    return jax.vmap(one_block)(block_keys).reshape(-1)


def draw_fine_pool(key, part):
    return covering(jax.random.fold_in(key, 11), NF // (4 * QUARTER_PATCH), 4 * QUARTER_PATCH, QUARTER_PATCH)


def draw_quarter_pool(key, part):
    return covering(jax.random.fold_in(key, 23), NQ // (4 * SIXTEENTH_PATCH), 4 * SIXTEENTH_PATCH, SIXTEENTH_PATCH)


def plant(entries, rng, low, largest):
    shape = entries.shape
    index_at = [jax.random.randint(jax.random.fold_in(rng, axis), (), 0, shape[axis]) for axis in range(len(shape))]
    entries = entries.at[tuple(index_at)].set(low)
    longest = shape.index(max(shape))
    index_at[longest] = (index_at[longest] + 1) % shape[longest]
    return entries.at[tuple(index_at)].set(largest)


def block_scale(stream_key, extent, shards, low, largest):
    level = 1.0
    for position, parts in shards:
        heights = jax.random.uniform(jax.random.fold_in(jax.random.fold_in(stream_key, 6), position), (parts,), jnp.float32, low / len(shards), largest / len(shards))
        level = level * jnp.repeat(jnp.exp(heights), extent[position] // parts).reshape((-1,) + (1,) * (len(extent) - 1 - position))
    return level


def gaussian(key, shape, scale, limit, pieces=(), kind=jnp.bfloat16):
    loudness = block_scale(key, shape, pieces, -0.22, 0.18) if pieces else 1.0
    values = jax.random.normal(key, shape, jnp.float32) * scale * loudness
    return jnp.minimum(jnp.maximum(values, -limit), limit).astype(kind)


def setup_inputs(seed: int = 0, part: int = 0) -> dict:
    streams_of = jax.random.split(jax.random.key(seed), 16)
    part_splits = jax.random.split(jax.random.fold_in(streams_of[15], part), 16)
    return {
        "fine_nodes": gaussian(part_splits[0], (NF, W), 1.0, 6.0, ((0, 16),), jnp.float32),
        "fine_edges": gaussian(part_splits[1], (NF, K_F, W), 1.0, 6.0, ((0, 16),), jnp.float32),
        "fine_senders": plant(jax.random.randint(part_splits[2], (NF, K_F), 0, NF_DEV + 2 * HALO), jax.random.fold_in(part_splits[2], 1), 0, (NF_DEV + 2 * HALO) - 1).astype(jnp.int32),
        "fine_halo": plant(jax.random.randint(part_splits[3], (2 * N_PATCH * N_SUB, HALO), 0, NF_DEV), jax.random.fold_in(part_splits[3], 1), 0, NF_DEV - 1).astype(jnp.int32),
        "fine_pool": draw_fine_pool(jax.random.fold_in(jax.random.fold_in(streams_of[15], part), 71), part),
        "quarter_edges": gaussian(part_splits[5], (NQ, K_Q, W), 1.0, 6.0, ((0, 4),), jnp.float32),
        "quarter_senders": plant(jax.random.randint(part_splits[6], (NQ, K_Q), 0, QUARTER_PATCH + 2 * HALO_Q), jax.random.fold_in(part_splits[6], 1), 0, (QUARTER_PATCH + 2 * HALO_Q) - 1).astype(jnp.int32),
        "quarter_halo": plant(jax.random.randint(part_splits[7], (2 * N_PATCH, HALO_Q), 0, QUARTER_PATCH), jax.random.fold_in(part_splits[7], 1), 0, QUARTER_PATCH - 1).astype(jnp.int32),
        "quarter_pool": draw_quarter_pool(jax.random.fold_in(jax.random.fold_in(streams_of[15], part), 71), part),
        "coarse_edges": gaussian(part_splits[9], (NS, K_S, W), 1.0, 6.0, ((0, 16),), jnp.float32),
        "coarse_senders": plant(jax.random.randint(part_splits[10], (NS, K_S), 0, NS), jax.random.fold_in(part_splits[10], 1), 0, NS - 1).astype(jnp.int32),
        "edge_in": gaussian(streams_of[11], (3, 3 * W, W), (3 * W) ** -0.5, 0.3125, (), jnp.float32),
        "edge_out": gaussian(streams_of[12], (3, W, W), W ** -0.5, 0.5, (), jnp.float32),
        "node_in": gaussian(streams_of[13], (3, 2 * W, W), (2 * W) ** -0.5, 0.375, (), jnp.float32),
        "node_out": gaussian(streams_of[14], (3, W, W), W ** -0.5, 0.5, (), jnp.float32),
    }


exact_mode = lax.Precision.HIGHEST

def product(left, right):
    return jnp.dot(left, right, precision=exact_mode)

def normalize(values):
    centred = values - lax.optimization_barrier(jnp.mean(values, axis=-1, keepdims=True))
    spread = lax.optimization_barrier(jnp.mean(centred * centred, axis=-1, keepdims=True))
    return centred * lax.rsqrt(spread + 1e-05)

def process_level(receivers, sources, senders, edge_feats, edge_in, edge_out, node_in, node_out):
    rows_count, degree, width = edge_feats.shape
    sender_proj = product(sources, edge_in[:width])
    receiver_proj = product(receivers, edge_in[width:2 * width])
    edge_proj = product(edge_feats.reshape(rows_count * degree, width), edge_in[2 * width:]).reshape(rows_count, degree, width)
    hidden = jax.nn.relu(sender_proj[senders] + receiver_proj[:, None, :] + edge_proj)
    message = product(hidden.reshape(rows_count * degree, width), edge_out).reshape(rows_count, degree, width)
    summed = lax.optimization_barrier(jnp.sum(edge_feats + normalize(message), axis=1))
    node_hidden = jax.nn.relu(product(receivers, node_in[:width]) + product(summed, node_in[width:]))
    return receivers + normalize(product(node_hidden, node_out))

def halo_rows_global(halo_lists, blocks, block_size, margin):
    lists = halo_lists.reshape(blocks, 2, margin)
    starts = jnp.arange(blocks, dtype=jnp.int32) * block_size
    own_rows = starts[:, None] + jnp.arange(block_size, dtype=jnp.int32)[None, :]
    from_left = jnp.roll(starts, 1)[:, None] + jnp.roll(lists[:, 0], 1, axis=0)
    from_right = jnp.roll(starts, -1)[:, None] + jnp.roll(lists[:, 1], -1, axis=0)
    return jnp.concatenate([own_rows, from_left, from_right], axis=1)

def global_senders(senders, lookup):
    blocks = lookup.shape[0]
    local_ids = senders.reshape(blocks, -1, senders.shape[1])
    picked = jax.vmap(lambda rows_here, picks: rows_here[picks])(lookup, local_ids)
    return picked.reshape(senders.shape)

def pool_mean(values, targets, segments):
    sums = jax.ops.segment_sum(values, targets, num_segments=segments)
    counts = jax.ops.segment_sum(jnp.ones((values.shape[0],), jnp.float32), targets, num_segments=segments)
    return sums / counts[:, None]

def reference(fine_nodes, fine_edges, fine_senders, fine_halo, fine_pool, quarter_edges, quarter_senders, quarter_halo, quarter_pool, coarse_edges, coarse_senders, edge_in, edge_out, node_in, node_out):
    fine_lookup = halo_rows_global(fine_halo, N_PATCH * N_SUB, NF_DEV, HALO)
    fine_new = process_level(fine_nodes, fine_nodes, global_senders(fine_senders, fine_lookup), fine_edges, edge_in[0], edge_out[0], node_in[0], node_out[0])
    fine_owner = jnp.arange(NF, dtype=jnp.int32) // (NF_DEV * N_SUB)
    fine_target = fine_owner * QUARTER_PATCH + fine_pool
    quarter_nodes = pool_mean(fine_new, fine_target, NQ)
    quarter_lookup = halo_rows_global(quarter_halo, N_PATCH, QUARTER_PATCH, HALO_Q)
    quarter_new = process_level(quarter_nodes, quarter_nodes, global_senders(quarter_senders, quarter_lookup), quarter_edges, edge_in[1], edge_out[1], node_in[1], node_out[1])
    quarter_owner = jnp.arange(NQ, dtype=jnp.int32) // QUARTER_PATCH
    quarter_target = quarter_owner * SIXTEENTH_PATCH + quarter_pool
    coarse_nodes = pool_mean(quarter_new, quarter_target, NS)
    coarse_new = process_level(coarse_nodes, coarse_nodes, coarse_senders, coarse_edges, edge_in[2], edge_out[2], node_in[2], node_out[2])
    quarter_out = quarter_new + coarse_new[quarter_target]
    return fine_new + quarter_out[fine_target]
```

```python
import functools

import jax
import jax.numpy as jnp
from jax import lax
from jax.experimental import pallas as pl
from jax.experimental.pallas import tpu as pltpu
from jax.sharding import PartitionSpec as P

f32 = jnp.float32
half = jnp.bfloat16
LANES = 128
EPS = 1e-05


def side(x):
    high = x.astype(half)
    low = (x - high.astype(f32)).astype(half)
    return jnp.concatenate([high, low], axis=1)


def packed(w):
    row = side(w)
    return jnp.concatenate([row, row], axis=0)


def folded(y):
    w = y.shape[1] // 2
    return y[:, :w] + y[:, w:]


def times(a, b):
    return lax.dot_general(a, b, (((1,), (0,)), ((), ())), preferred_element_type=f32)


def centred_columns(w):
    return w - jnp.mean(w, axis=1, keepdims=True)


def inverse_spread(v):
    return lax.rsqrt(jnp.mean(v * v, axis=1, keepdims=True) + EPS)


def down(row):
    n = row.shape[1]
    parts = []
    for start in range(0, n, LANES):
        wide = jnp.broadcast_to(row[:, start : start + LANES], (LANES, LANES))
        parts.append(jnp.transpose(wide).astype(jnp.int16))
    return parts[0] if len(parts) == 1 else jnp.concatenate(parts, axis=0)


def picks(column, size):
    n = column.shape[0]
    lane = lax.broadcasted_iota(jnp.int32, (n, LANES), 1)
    one, zero = jnp.ones((n, LANES), half), jnp.zeros((n, LANES), half)
    parts = [
        jnp.where(column == (lane + start).astype(jnp.int16), one, zero)
        for start in range(0, size, LANES)
    ]
    return jnp.concatenate(parts, axis=1)


def members(row, size):
    n = row.shape[1]
    line = lax.broadcasted_iota(jnp.int32, (size, n), 0).astype(jnp.int16)
    entry = jnp.broadcast_to(row, (size, n)).astype(jnp.int16)
    return jnp.where(entry == line, jnp.ones((size, n), half), jnp.zeros((size, n), half))


def level_tile(degree, tile, sources, lhs, wide, rhs_message, rhs_node, rhs_out, receivers, column, edge, reach):
    for k in range(degree):
        lhs[k * tile : (k + 1) * tile, :sources] = picks(column(k), sources)
        lhs[k * tile : (k + 1) * tile, sources:] = side(edge(k))
    before = folded(times(lhs[...], wide[...])).reshape(degree, tile, -1)
    hidden = jnp.maximum(before + reach[None], 0.0)
    message = folded(times(side(hidden.reshape(degree * tile, -1)), rhs_message))
    message = (message * inverse_spread(message)).reshape(degree, tile, -1)
    total = message[0] + edge(0)
    for k in range(1, degree):
        total = total + (message[k] + edge(k))
    node = jnp.concatenate([side(receivers), side(total)], axis=1)
    node_hidden = jnp.maximum(folded(times(node, rhs_node)), 0.0)
    update = folded(times(side(node_hidden), rhs_out))
    return receivers + update * inverse_spread(update)


def prepare(edge_in, edge_out, node_in, node_out, wide, weights, sources):
    w = edge_out.shape[1]
    wide[sources:, :] = packed(edge_in[2 * w : 3 * w])
    weights[0] = packed(edge_in[w : 2 * w])
    weights[1] = packed(centred_columns(edge_out[...]))
    weights[2] = packed(node_in[0:w])
    weights[3] = packed(node_in[w : 2 * w])
    weights[4] = packed(centred_columns(node_out[...]))
    return packed(edge_in[0:w])


def node_rhs(weights):
    return jnp.concatenate([weights[2], weights[3]], axis=0)


def halo_kernel(lists, nodes, to_next, to_previous):
    both = side(nodes[...])
    size = nodes.shape[0]
    for i, out in enumerate((to_next, to_previous)):
        out[...] = folded(times(picks(down(lists[i : i + 1, :]), size), both))


def fine_kernel(
    tile, flip, senders, pool, nodes, left, right, edges, edge_in, edge_out, node_in, node_out,
    new, keep, send, wide, weights, lhs,
):
    degree = edges.shape[0]
    rows, w = nodes.shape
    margin = left.shape[0]
    sources = rows + 2 * margin
    i = pl.program_id(0)

    @pl.when(i == 0)
    def _():
        sender = prepare(edge_in.at[0], edge_out.at[0], node_in.at[0], node_out.at[0], wide, weights, sources)
        wide[:rows, :] = side(folded(times(side(nodes[...]), sender)))
        wide[rows : rows + margin, :] = side(folded(times(side(left[...]), sender)))
        wide[rows + margin : sources, :] = side(folded(times(side(right[...]), sender)))
        keep[...] = jnp.zeros_like(keep)
        send[...] = jnp.zeros_like(send)

    receivers = nodes[pl.ds(pl.multiple_of(i * tile, tile), tile), :]
    reach = folded(times(side(receivers), weights[0]))
    updated = level_tile(
        degree, tile, sources, lhs, wide, weights[1], node_rhs(weights), weights[4], receivers,
        lambda k: down(senders[k : k + 1, :]), lambda k: edges[k], reach,
    )
    new[...] = updated
    both = side(updated)
    part = keep.shape[0]
    per = tile // LANES
    target = jnp.concatenate([pool[pl.ds(i * per + j, 1), :] for j in range(per)], axis=1)
    target = jnp.where(target < part, target + flip[0] * part, target - flip[0] * part)
    target = jnp.where(target < 0, target + 2 * part, target)
    target = jnp.where(target >= 2 * part, target - 2 * part, target)
    keep[...] += folded(times(members(target, part), both))
    send[...] += folded(times(members(target - part, part), both))


def count_kernel(*refs):
    pools, out = refs[:-1], refs[-1]
    size = out.shape[0]
    line = lax.broadcasted_iota(jnp.int32, (size, LANES), 0).astype(jnp.int16)
    one, zero = jnp.ones((size, LANES), half), jnp.zeros((size, LANES), half)
    total = zero
    for pool in pools:
        for r in range(pool.shape[0]):
            entry = jnp.broadcast_to(pool[r : r + 1, :], (size, LANES)).astype(jnp.int16)
            total = total + jnp.where(entry == line, one, zero)
    out[...] = 1.0 / times(total, jnp.ones((LANES, LANES), half))


def quarter_nodes_kernel(flip, mine, other, share, lists, nodes, to_next, to_previous):
    part = mine.shape[0]
    first = pl.multiple_of(flip[0] * part, part)
    second = pl.multiple_of((1 - flip[0]) * part, part)
    nodes[pl.ds(first, part), :] = mine[...] * share[pl.ds(first, part), :]
    nodes[pl.ds(second, part), :] = other[...] * share[pl.ds(second, part), :]
    halo_kernel(lists, nodes, to_next, to_previous)


def quarter_kernel(
    tile, degree, senders, pool, nodes, left, right, edges, edge_in, edge_out, node_in, node_out,
    new, coarse, wide, weights, lhs,
):
    rows, w = nodes.shape
    margin = left.shape[0]
    sources = rows + 2 * margin
    i = pl.program_id(0)

    @pl.when(i == 0)
    def _():
        sender = prepare(edge_in.at[1], edge_out.at[1], node_in.at[1], node_out.at[1], wide, weights, sources)
        wide[:rows, :] = side(folded(times(side(nodes[...]), sender)))
        wide[rows : rows + margin, :] = side(folded(times(side(left[...]), sender)))
        wide[rows + margin : sources, :] = side(folded(times(side(right[...]), sender)))
        coarse[...] = jnp.zeros_like(coarse)

    receivers = nodes[pl.ds(pl.multiple_of(i * tile, tile), tile), :]
    reach = folded(times(side(receivers), weights[0]))
    updated = level_tile(
        degree, tile, sources, lhs, wide, weights[1], node_rhs(weights), weights[4], receivers,
        lambda k: down(senders[k : k + 1, :]), lambda k: edges[pl.ds(k, tile, stride=degree), :], reach,
    )
    new[...] = updated
    per = tile // LANES
    target = jnp.concatenate([pool[pl.ds(i * per + j, 1), :] for j in range(per)], axis=1)
    coarse[...] += folded(times(members(target, coarse.shape[0]), side(updated)))

    @pl.when(i == pl.num_programs(0) - 1)
    def _():
        size = coarse.shape[0]
        line = lax.broadcasted_iota(jnp.int32, (size, LANES), 0).astype(jnp.int16)
        one, zero = jnp.ones((size, LANES), half), jnp.zeros((size, LANES), half)
        total = zero
        for r in range(pool.shape[0]):
            entry = jnp.broadcast_to(pool[r : r + 1, :], (size, LANES)).astype(jnp.int16)
            total = total + jnp.where(entry == line, one, zero)
        coarse[...] = coarse[...] / times(total, jnp.ones((LANES, LANES), half))


def coarse_kernel(n_patch, n_sub, degree, tile, place, *refs):
    pieces, refs = refs[:n_patch], refs[n_patch:]
    shares, refs = refs[:n_sub], refs[n_sub:]
    (senders, quarter_pool, fine_pool, quarter_new, fine_new, edge_in, edge_out, node_in, node_out,
     out, nodes, edges, wide, weights, lhs, coarse_new) = refs
    block = pieces[0].shape[0]
    piece = shares[0].shape[0]
    sources = nodes.shape[0]
    for j in range(n_patch):
        at = lax.rem(place[0] + j, n_patch)
        nodes[pl.ds(pl.multiple_of(at * block, block), block), :] = pieces[j][...]
    for j in range(n_sub):
        at = lax.rem(place[1] + j, n_sub)
        edges[pl.ds(pl.multiple_of(at * piece, piece), piece), :] = shares[j][...]
    sender = prepare(edge_in.at[2], edge_out.at[2], node_in.at[2], node_out.at[2], wide, weights, sources)
    wide[:sources, :] = side(folded(times(side(nodes[...]), sender)))
    for t in range(block // tile):
        receivers = pieces[0][t * tile : (t + 1) * tile, :]
        reach = folded(times(side(receivers), weights[0]))
        coarse_new[t * tile : (t + 1) * tile, :] = level_tile(
            degree, tile, sources, lhs, wide, weights[1], node_rhs(weights), weights[4], receivers,
            lambda k: down(senders[k : k + 1, t * tile : (t + 1) * tile]),
            lambda k: edges[pl.ds(k + t * tile * degree, tile, stride=degree), :], reach,
        )
    column = jnp.concatenate([down(quarter_pool[r : r + 1, :]) for r in range(quarter_pool.shape[0])], axis=0)
    quarter_out = quarter_new[...] + folded(times(picks(column, block), side(coarse_new[...])))
    both = side(quarter_out)
    for r in range(fine_pool.shape[0]):
        rows = slice(r * LANES, (r + 1) * LANES)
        chosen = picks(down(fine_pool[r : r + 1, :]), both.shape[0])
        out[rows, :] = fine_new[rows, :] + folded(times(chosen, both))


def whole(shape):
    return pl.BlockSpec(shape, lambda *_: (0,) * len(shape))


def shaped(rows, w):
    return jax.ShapeDtypeStruct((rows, w), f32)


def run(kernel, grid, scalars, in_specs, operands, outs, out_specs, scratch, flops=10**9):
    return pl.pallas_call(
        kernel,
        out_shape=outs,
        grid_spec=pltpu.PrefetchScalarGridSpec(
            num_scalar_prefetch=len(scalars), grid=grid, in_specs=in_specs, out_specs=out_specs,
            scratch_shapes=scratch,
        ),
        compiler_params=pltpu.CompilerParams(vmem_limit_bytes=60 * 1024 * 1024),
        cost_estimate=pl.CostEstimate(flops=flops, bytes_accessed=4 * 10**6, transcendentals=0),
    )(*scalars, *operands)


def passed(value, axis, steps):
    count = lax.axis_size(axis)
    return lax.ppermute(value, axis, [(s, (s + steps) % count) for s in range(count)])


def swapped(value, axis, bit):
    count = lax.axis_size(axis)
    return lax.ppermute(value, axis, [(s, s ^ bit) for s in range(count)])


def on_device(
    fine_nodes, fine_edges, fine_senders, fine_halo, fine_pool, quarter_edges, quarter_senders,
    quarter_halo, quarter_pool, coarse_edges, coarse_senders, edge_in, edge_out, node_in, node_out,
):
    n_sub, n_patch = lax.axis_size("sub"), lax.axis_size("patch")
    sub, patch = lax.axis_index("sub"), lax.axis_index("patch")
    rows, degree, w = fine_edges.shape
    q_rows, q_degree, _ = quarter_edges.shape
    margin, q_margin = fine_halo.shape[1], quarter_halo.shape[1]
    piece_rows, c_degree, _ = coarse_edges.shape
    total = coarse_senders.shape[0]
    block = total // n_patch
    layers = (edge_in, edge_out, node_in, node_out)
    layer_specs = [whole(x.shape) for x in layers]

    to_next, to_previous = run(
        halo_kernel, (), (), [whole((2, margin)), whole((rows, w))], (fine_halo, fine_nodes),
        (shaped(margin, w),) * 2, [whole((margin, w))] * 2, [],
    )
    left = passed(to_next, ("patch", "sub"), 1)
    right = passed(to_previous, ("patch", "sub"), -1)

    pool_rows = fine_pool.reshape(rows // LANES, LANES)
    pools = [pool_rows] + [passed(pool_rows, "sub", -j) for j in range(1, n_sub)]
    own_share = coarse_edges.reshape(piece_rows * c_degree, w)
    shares = [own_share] + [passed(own_share, "sub", -j) for j in range(1, n_sub)]
    inverse = run(
        count_kernel, (), (), [whole(pool_rows.shape)] * n_sub, pools, shaped(q_rows, w), whole((q_rows, w)), [],
    )

    tile = 256
    sources = rows + 2 * margin
    flip = (sub % 2).astype(jnp.int32).reshape(1)
    part = q_rows // 2
    fine_new, keep, send = run(
        functools.partial(fine_kernel, tile), (rows // tile,), (flip,),
        [
            pl.BlockSpec((degree, tile), lambda i, *_: (0, i)), whole(pool_rows.shape), whole((rows, w)),
            whole((margin, w)), whole((margin, w)), pl.BlockSpec((degree, tile, w), lambda i, *_: (0, i, 0)),
            *layer_specs,
        ],
        (fine_senders.T, pool_rows, fine_nodes, left, right, fine_edges.transpose(1, 0, 2), *layers),
        (shaped(rows, w), shaped(part, w), shaped(part, w)),
        [pl.BlockSpec((tile, w), lambda i, *_: (i, 0)), whole((part, w)), whole((part, w))],
        [
            pltpu.VMEM((sources + 2 * w, 2 * w), half), pltpu.VMEM((5, 2 * w, 2 * w), half),
            pltpu.VMEM((degree * tile, sources + 2 * w), half),
        ],
        6 * 10**9,
    )

    mine = keep + swapped(send, "sub", 1)
    bit = 2
    while bit < n_sub:
        mine = mine + swapped(mine, "sub", bit)
        bit *= 2
    other = swapped(mine, "sub", 1)
    quarter_nodes, to_next, to_previous = run(
        quarter_nodes_kernel, (), (flip,),
        [whole((part, w)), whole((part, w)), whole((q_rows, w)), whole((2, q_margin))],
        (mine, other, inverse, quarter_halo),
        (shaped(q_rows, w), shaped(q_margin, w), shaped(q_margin, w)),
        [whole((q_rows, w)), whole((q_margin, w)), whole((q_margin, w))], [],
    )
    left = passed(to_next, "patch", 1)
    right = passed(to_previous, "patch", -1)

    sources = q_rows + 2 * q_margin
    quarter_pool_rows = quarter_pool.reshape(q_rows // LANES, LANES)
    quarter_new, coarse_block = run(
        functools.partial(quarter_kernel, tile, q_degree), (q_rows // tile,), (),
        [
            pl.BlockSpec((q_degree, tile), lambda i, *_: (0, i)), whole(quarter_pool_rows.shape), whole((q_rows, w)),
            whole((q_margin, w)), whole((q_margin, w)), pl.BlockSpec((q_degree * tile, w), lambda i, *_: (i, 0)),
            *layer_specs,
        ],
        (quarter_senders.T, quarter_pool_rows, quarter_nodes, left, right,
         quarter_edges.reshape(q_rows * q_degree, w), *layers),
        (shaped(q_rows, w), shaped(block, w)),
        [pl.BlockSpec((tile, w), lambda i, *_: (i, 0)), whole((block, w))],
        [
            pltpu.VMEM((sources + 2 * w, 2 * w), half), pltpu.VMEM((5, 2 * w, 2 * w), half),
            pltpu.VMEM((q_degree * tile, sources + 2 * w), half),
        ],
        4 * 10**9,
    )

    pieces = [coarse_block] + [passed(coarse_block, "patch", -j) for j in range(1, n_patch)]
    place = jnp.stack([patch, sub]).astype(jnp.int32)
    c_tile = min(block, tile)
    return run(
        functools.partial(coarse_kernel, n_patch, n_sub, c_degree, c_tile), (1,), (place,),
        [
            *[whole((block, w))] * n_patch, *[whole(own_share.shape)] * n_sub,
            pl.BlockSpec((c_degree, block), lambda i, place: (0, place[0])), whole(quarter_pool_rows.shape),
            whole(pool_rows.shape), whole((q_rows, w)), whole((rows, w)), *layer_specs,
        ],
        (*pieces, *shares, coarse_senders.T, quarter_pool_rows, pool_rows, quarter_new, fine_new, *layers),
        shaped(rows, w), whole((rows, w)),
        [
            pltpu.VMEM((total, w), f32), pltpu.VMEM((block * c_degree, w), f32),
            pltpu.VMEM((total + 2 * w, 2 * w), half), pltpu.VMEM((5, 2 * w, 2 * w), half),
            pltpu.VMEM((c_degree * c_tile, total + 2 * w), half), pltpu.VMEM((block, w), f32),
        ],
        2 * 10**9,
    )


def solution(mesh):
    split = P(("groups", "patch", "sub"))
    patches = P(("groups", "patch"))
    return jax.shard_map(
        on_device,
        mesh=mesh,
        in_specs=(
            split, split, split, split, split, patches, patches, patches, patches, split, P("groups"),
            P(), P(), P(), P(),
        ),
        out_specs=split,
        check_vma=False,
    )
```

```python
import functools

import jax
import jax.numpy as jnp
from jax import lax
from jax.experimental import pallas as pl
from jax.experimental.pallas import tpu as pltpu
from jax.sharding import PartitionSpec as P

f32 = jnp.float32
half = jnp.bfloat16
LANES = 128
EPS = 1e-05


def side(x):
    high = x.astype(half)
    low = (x - high.astype(f32)).astype(half)
    return jnp.concatenate([high, low], axis=1)


def packed(w):
    row = side(w)
    return jnp.concatenate([row, row], axis=0)


def folded(y):
    w = y.shape[1] // 2
    return y[:, :w] + y[:, w:]


def times(a, b):
    return lax.dot_general(a, b, (((1,), (0,)), ((), ())), preferred_element_type=f32)


def centred_columns(w):
    return w - jnp.mean(w, axis=1, keepdims=True)


def inverse_spread(v):
    return lax.rsqrt(jnp.mean(v * v, axis=1, keepdims=True) + EPS)


def down(row):
    n = row.shape[1]
    parts = []
    for start in range(0, n, LANES):
        wide = jnp.broadcast_to(row[:, start : start + LANES], (LANES, LANES))
        parts.append(jnp.transpose(wide).astype(jnp.int16))
    return parts[0] if len(parts) == 1 else jnp.concatenate(parts, axis=0)


def picks(column, size):
    n = column.shape[0]
    lane = lax.broadcasted_iota(jnp.int32, (n, LANES), 1)
    one, zero = jnp.ones((n, LANES), half), jnp.zeros((n, LANES), half)
    parts = [
        jnp.where(column == (lane + start).astype(jnp.int16), one, zero)
        for start in range(0, size, LANES)
    ]
    return jnp.concatenate(parts, axis=1)


def members(row, size):
    n = row.shape[1]
    line = lax.broadcasted_iota(jnp.int32, (size, n), 0).astype(jnp.int16)
    entry = jnp.broadcast_to(row, (size, n)).astype(jnp.int16)
    return jnp.where(entry == line, jnp.ones((size, n), half), jnp.zeros((size, n), half))


def share_of_each(pools, first, size):
    line = (lax.broadcasted_iota(jnp.int32, (size, LANES), 0) + first).astype(jnp.int16)
    one, zero = jnp.ones((size, LANES), half), jnp.zeros((size, LANES), half)
    total = zero
    for pool in pools:
        for r in range(pool.shape[0]):
            entry = jnp.broadcast_to(pool[r : r + 1, :], (size, LANES)).astype(jnp.int16)
            total = total + jnp.where(entry == line, one, zero)
    return 1.0 / times(total, jnp.ones((LANES, LANES), half))


def first_part(degree, tile, sources, lhs, wide, column, edge, reach, before, extra=None):
    for k in range(degree):
        lhs[k * tile : (k + 1) * tile, :sources] = picks(column(k), sources)
        if edge is not None:
            lhs[k * tile : (k + 1) * tile, sources:] = side(edge(k))
    sums = folded(times(lhs[...], wide[...])).reshape(degree, tile, -1)
    for k in range(degree):
        part = sums[k] + reach
        before[k] = part if extra is None else part + extra[k]


def second_part(degree, tile, hidden, edge_sum, receivers, rhs_message, rhs_node, rhs_out):
    message = folded(times(side(hidden), rhs_message))
    message = (message * inverse_spread(message)).reshape(degree, tile, -1)
    total = edge_sum
    for k in range(degree):
        total = total + message[k]
    node = jnp.concatenate([side(receivers), side(total)], axis=1)
    node_hidden = jnp.maximum(folded(times(node, rhs_node)), 0.0)
    update = folded(times(side(node_hidden), rhs_out))
    return receivers + update * inverse_spread(update)


def pack_second(edge_out, node_in, node_out, weights):
    w = edge_out.shape[1]
    weights[0] = packed(centred_columns(edge_out[...]))
    weights[1] = packed(node_in[0:w])
    weights[2] = packed(node_in[w : 2 * w])
    weights[3] = packed(centred_columns(node_out[...]))


def with_halo(degree, tile, rows, margin, beyond, column, before):
    chosen = [picks(column(k) - jnp.int16(rows), 2 * margin) for k in range(degree)]
    sums = folded(times(jnp.concatenate(chosen, axis=0), beyond[...])).reshape(degree, tile, -1)
    parts = [jnp.maximum(sums[k] + before[k], 0.0) for k in range(degree)]
    return jnp.concatenate(parts, axis=0)


def gather_halo(lists, nodes, to_next, to_previous):
    both = side(nodes[...])
    for i, out in enumerate((to_next, to_previous)):
        out[...] = folded(times(picks(down(lists[i : i + 1, :]), nodes.shape[0]), both))


def start_kernel(lists, nodes, edges, pool, to_next, to_previous, early):
    gather_halo(lists, nodes, to_next, to_previous)
    count = edges.shape[0]
    early[:count, :] = edges[...]
    early[count:, :] = pool[...].astype(f32)


def fine_first_kernel(tile, senders, nodes, edges, edge_in, before, edge_sum, wide, reach_rhs, lhs):
    degree = edges.shape[0]
    rows, w = nodes.shape
    i = pl.program_id(0)

    @pl.when(i == 0)
    def _():
        wide[:rows, :] = side(folded(times(side(nodes[...]), packed(edge_in[0, 0:w]))))
        wide[rows:, :] = packed(edge_in[0, 2 * w : 3 * w])
        reach_rhs[...] = packed(edge_in[0, w : 2 * w])

    receivers = nodes[pl.ds(pl.multiple_of(i * tile, tile), tile), :]
    reach = folded(times(side(receivers), reach_rhs[...]))
    total = edges[0]
    for k in range(1, degree):
        total = total + edges[k]
    edge_sum[...] = total
    first_part(
        degree, tile, rows, lhs, wide, lambda k: down(senders[k : k + 1, :]), lambda k: edges[k], reach, before
    )


def rotated(target, flip, part):
    return jnp.where(target < part, target + flip * part, target - flip * part)


def fine_second_kernel(
    tile, flip, senders, pool, nodes, left, right, before, edge_sum, edge_in, edge_out, node_in, node_out,
    new, keep, send, beyond, weights,
):
    degree = before.shape[0]
    rows, w = nodes.shape
    margin = left.shape[0]
    i = pl.program_id(0)

    @pl.when(i == 0)
    def _():
        sender = packed(edge_in[0, 0:w])
        beyond[:margin, :] = side(folded(times(side(left[...]), sender)))
        beyond[margin:, :] = side(folded(times(side(right[...]), sender)))
        pack_second(edge_out.at[0], node_in.at[0], node_out.at[0], weights)
        keep[...] = jnp.zeros_like(keep)
        send[...] = jnp.zeros_like(send)

    receivers = nodes[pl.ds(pl.multiple_of(i * tile, tile), tile), :]
    hidden = with_halo(degree, tile, rows, margin, beyond, lambda k: down(senders[k : k + 1, :]), before)
    updated = second_part(
        degree, tile, hidden, edge_sum[...], receivers, weights[0],
        jnp.concatenate([weights[1], weights[2]], axis=0), weights[3],
    )
    new[...] = updated
    both = side(updated)
    part = keep.shape[0]
    per = tile // LANES
    target = jnp.concatenate([pool[pl.ds(i * per + j, 1), :] for j in range(per)], axis=1)
    target = rotated(target, flip[0], part)
    keep[...] += folded(times(members(target, part), both))
    send[...] += folded(times(members(target - part, part), both))


def window_kernel(n_sub, place, *refs):
    early, refs = refs[:n_sub], refs[n_sub:]
    (quarter_pool, fine_pool, quarter_edges, edge_in, _, share, coarse_share, chosen, quarter_before,
     quarter_sum, coarse_before, coarse_sum, edges) = refs
    w = edge_in.shape[2]
    piece = early[0].shape[0] - fine_pool.shape[0]
    pools = [block[piece:, :].astype(jnp.int32) for block in early]
    share[...] = share_of_each(pools, 0, share.shape[0])
    coarse_part = coarse_share.shape[0]
    coarse_share[...] = share_of_each([quarter_pool[...]], place[1] * coarse_part, coarse_part)

    degree, rows, _ = quarter_before.shape
    rhs = packed(edge_in[1, 2 * w : 3 * w])
    total = None
    for k in range(degree):
        edge = quarter_edges[pl.ds(k, rows, stride=degree), :]
        total = edge if total is None else total + edge
        quarter_before[k] = folded(times(side(edge), rhs))
    quarter_sum[...] = total

    for j in range(n_sub):
        at = lax.rem(place[0] + j, n_sub)
        edges[pl.ds(pl.multiple_of(at * piece, piece), piece), :] = early[j][:piece, :]
    degree, rows, _ = coarse_before.shape
    rhs = packed(edge_in[2, 2 * w : 3 * w])
    total = None
    for k in range(degree):
        edge = edges[pl.ds(k, rows, stride=degree), :]
        total = edge if total is None else total + edge
        coarse_before[k] = folded(times(side(edge), rhs))
    coarse_sum[...] = total

    parent = [down(quarter_pool[r : r + 1, :]) for r in range(quarter_pool.shape[0])]
    parent = side(jnp.concatenate(parent, axis=0).astype(jnp.int32).astype(f32))
    for r in range(fine_pool.shape[0]):
        rows = slice(r * LANES, (r + 1) * LANES)
        named = folded(times(picks(down(fine_pool[r : r + 1, :]), parent.shape[0]), parent))
        chosen[rows, :] = picks(named.astype(jnp.int32).astype(jnp.int16), chosen.shape[1])


def quarter_nodes_kernel(flip, mine, other, share, lists, nodes, to_next, to_previous):
    part = mine.shape[0]
    first = pl.multiple_of(flip[0] * part, part)
    second = pl.multiple_of((1 - flip[0]) * part, part)
    nodes[pl.ds(first, part), :] = mine[...] * share[pl.ds(first, part), :]
    nodes[pl.ds(second, part), :] = other[...] * share[pl.ds(second, part), :]
    gather_halo(lists, nodes, to_next, to_previous)


def quarter_first_kernel(tile, flip, senders, nodes, extra, edge_in, before, wide, lhs):
    degree, part, w = before.shape
    rows = nodes.shape[0]
    wide[...] = side(folded(times(side(nodes[...]), packed(edge_in[1, 0:w]))))
    reach_rhs = packed(edge_in[1, w : 2 * w])
    for t in range(part // tile):
        span = slice(t * tile, (t + 1) * tile)
        receivers = nodes[pl.ds(pl.multiple_of(flip[0] * part + t * tile, tile), tile), :]
        reach = folded(times(side(receivers), reach_rhs))
        first_part(
            degree, tile, rows, lhs, wide, lambda k: down(senders[k : k + 1, span]), None, reach,
            before.at[:, span, :], extra.at[:, span, :],
        )


def quarter_second_kernel(
    tile, flip, senders, pool, nodes, left, right, before, edge_sum, edge_in, edge_out, node_in, node_out,
    new, keep, send, beyond, weights,
):
    degree, part, w = before.shape
    rows = nodes.shape[0]
    margin = left.shape[0]
    sender = packed(edge_in[1, 0:w])
    beyond[:margin, :] = side(folded(times(side(left[...]), sender)))
    beyond[margin:, :] = side(folded(times(side(right[...]), sender)))
    pack_second(edge_out.at[1], node_in.at[1], node_out.at[1], weights)
    per = tile // LANES
    coarse_part = keep.shape[0]
    for t in range(part // tile):
        span = slice(t * tile, (t + 1) * tile)
        receivers = nodes[pl.ds(pl.multiple_of(flip[0] * part + t * tile, tile), tile), :]
        hidden = with_halo(
            degree, tile, rows, margin, beyond, lambda k: down(senders[k : k + 1, span]), before.at[:, span, :]
        )
        updated = second_part(
            degree, tile, hidden, edge_sum[span, :], receivers, weights[0],
            jnp.concatenate([weights[1], weights[2]], axis=0), weights[3],
        )
        new[span, :] = updated
        at = flip[0] * (part // LANES) + t * per
        target = jnp.concatenate([pool[pl.ds(at + j, 1), :] for j in range(per)], axis=1)
        target = rotated(target, flip[0], coarse_part)
        both = side(updated)
        kept = folded(times(members(target, coarse_part), both))
        sent = folded(times(members(target - coarse_part, coarse_part), both))
        keep[...] = kept if t == 0 else keep[...] + kept
        send[...] = sent if t == 0 else send[...] + sent


def fine_out_kernel(flip, pool, mine, other, fine_new, out, nodes):
    part = mine.shape[0]
    nodes[pl.ds(pl.multiple_of(flip[0] * part, part), part), :] = mine[...]
    nodes[pl.ds(pl.multiple_of((1 - flip[0]) * part, part), part), :] = other[...]
    both = side(nodes[...])
    for r in range(pool.shape[0]):
        rows = slice(r * LANES, (r + 1) * LANES)
        out[rows, :] = fine_new[rows, :] + folded(times(picks(down(pool[r : r + 1, :]), both.shape[0]), both))


def coarse_kernel(n_patch, tile, place, *refs):
    mine, refs = refs[:n_patch], refs[n_patch:]
    other, refs = refs[:n_patch], refs[n_patch:]
    (senders, extra, edge_sum, chosen, base, edge_in, edge_out, node_in, node_out,
     out, nodes, wide, weights, lhs, before, new) = refs
    part, w = mine[0].shape
    block = 2 * part
    degree = extra.shape[0]
    sources = nodes.shape[0]
    for j in range(n_patch):
        at = lax.rem(place[0] + j, n_patch) * block
        nodes[pl.ds(pl.multiple_of(at + place[1] * part, part), part), :] = mine[j][...]
        nodes[pl.ds(pl.multiple_of(at + (1 - place[1]) * part, part), part), :] = other[j][...]
    wide[...] = side(folded(times(side(nodes[...]), packed(edge_in[2, 0:w]))))
    reach_rhs = packed(edge_in[2, w : 2 * w])
    pack_second(edge_out.at[2], node_in.at[2], node_out.at[2], weights)
    for t in range(block // tile):
        span = slice(t * tile, (t + 1) * tile)
        receivers = nodes[pl.ds(pl.multiple_of(place[0] * block + t * tile, tile), tile), :]
        reach = folded(times(side(receivers), reach_rhs))
        first_part(
            degree, tile, sources, lhs, wide, lambda k: down(senders[k : k + 1, span]), None, reach, before,
            extra.at[:, span, :],
        )
        hidden = jnp.maximum(before[...], 0.0).reshape(degree * tile, w)
        new[span, :] = second_part(
            degree, tile, hidden, edge_sum[span, :], receivers, weights[0],
            jnp.concatenate([weights[1], weights[2]], axis=0), weights[3],
        )
    out[...] = base[...] + folded(times(chosen[...], side(new[...])))


def whole(*shape):
    return pl.BlockSpec(shape, lambda *_: (0,) * len(shape))


def shaped(*shape, dtype=f32):
    return jax.ShapeDtypeStruct(shape, dtype)


def run(kernel, grid, scalars, in_specs, operands, outs, out_specs, scratch, mega, flops):
    return pl.pallas_call(
        kernel,
        out_shape=outs,
        grid_spec=pltpu.PrefetchScalarGridSpec(
            num_scalar_prefetch=len(scalars), grid=grid, in_specs=in_specs, out_specs=out_specs,
            scratch_shapes=scratch,
        ),
        compiler_params=pltpu.CompilerParams(vmem_limit_bytes=mega * 1024 * 1024),
        cost_estimate=pl.CostEstimate(flops=flops, bytes_accessed=10**6, transcendentals=0),
    )(*scalars, *operands)


def passed(value, axis, steps):
    count = lax.axis_size(axis)
    return lax.ppermute(value, axis, [(s, (s + steps) % count) for s in range(count)])


def swapped(value, axis, bit):
    count = lax.axis_size(axis)
    return lax.ppermute(value, axis, [(s, s ^ bit) for s in range(count)])


def on_device(
    fine_nodes, fine_edges, fine_senders, fine_halo, fine_pool, quarter_edges, quarter_senders,
    quarter_halo, quarter_pool, coarse_edges, coarse_senders, edge_in, edge_out, node_in, node_out,
):
    n_sub, n_patch = lax.axis_size("sub"), lax.axis_size("patch")
    sub, patch = lax.axis_index("sub").astype(jnp.int32), lax.axis_index("patch").astype(jnp.int32)
    rows, degree, w = fine_edges.shape
    q_rows, q_degree, _ = quarter_edges.shape
    margin, q_margin = fine_halo.shape[1], quarter_halo.shape[1]
    piece, c_degree, _ = coarse_edges.shape
    total = coarse_senders.shape[0]
    block = total // n_patch
    part, c_part = q_rows // 2, block // 2
    tile = 256
    c_tile = min(block, tile)
    core = sub % 2
    flip = core.reshape(1)
    sub_core = jnp.stack([sub, core])
    patch_core = jnp.stack([patch, core])
    layers = (edge_in, edge_out, node_in, node_out)
    layer_specs = [whole(*x.shape) for x in layers]
    pool_rows = fine_pool.reshape(rows // LANES, LANES)
    quarter_pool_rows = quarter_pool.reshape(q_rows // LANES, LANES)
    fine_senders, quarter_senders, coarse_senders = fine_senders.T, quarter_senders.T, coarse_senders.T
    own_edges = coarse_edges.reshape(piece * c_degree, w)
    early_rows = piece * c_degree + pool_rows.shape[0]
    big = 24 if total <= 2048 else 60

    to_next, to_previous, early = run(
        start_kernel, (), (), [whole(2, margin), whole(rows, w), whole(*own_edges.shape), whole(*pool_rows.shape)],
        (fine_halo, fine_nodes, own_edges, pool_rows),
        (shaped(margin, w), shaped(margin, w), shaped(early_rows, w)),
        [whole(margin, w), whole(margin, w), whole(early_rows, w)], [], 16, 10**8,
    )
    left = passed(to_next, ("patch", "sub"), 1)
    right = passed(to_previous, ("patch", "sub"), -1)
    all_early = [early] + [passed(early, "sub", -j) for j in range(1, n_sub)]

    before, edge_sum = run(
        functools.partial(fine_first_kernel, tile), (rows // tile,), (),
        [
            pl.BlockSpec((degree, tile), lambda i: (0, i)), whole(rows, w),
            pl.BlockSpec((degree, tile, w), lambda i: (0, i, 0)), whole(*edge_in.shape),
        ],
        (fine_senders, fine_nodes, fine_edges.transpose(1, 0, 2), edge_in),
        (shaped(degree, rows, w), shaped(rows, w)),
        [pl.BlockSpec((degree, tile, w), lambda i: (0, i, 0)), pl.BlockSpec((tile, w), lambda i: (i, 0))],
        [
            pltpu.VMEM((rows + 2 * w, 2 * w), half), pltpu.VMEM((2 * w, 2 * w), half),
            pltpu.VMEM((degree * tile, rows + 2 * w), half),
        ],
        24, 8 * 10**9,
    )
    fine_new, keep, send = run(
        functools.partial(fine_second_kernel, tile), (rows // tile,), (flip,),
        [
            pl.BlockSpec((degree, tile), lambda i, *_: (0, i)), whole(*pool_rows.shape), whole(rows, w),
            whole(margin, w), whole(margin, w), pl.BlockSpec((degree, tile, w), lambda i, *_: (0, i, 0)),
            pl.BlockSpec((tile, w), lambda i, *_: (i, 0)), *layer_specs,
        ],
        (fine_senders, pool_rows, fine_nodes, left, right, before, edge_sum, *layers),
        (shaped(rows, w), shaped(part, w), shaped(part, w)),
        [pl.BlockSpec((tile, w), lambda i, *_: (i, 0)), whole(part, w), whole(part, w)],
        [pltpu.VMEM((2 * margin, 2 * w), half), pltpu.VMEM((4, 2 * w, 2 * w), half)],
        24, 4 * 10**9,
    )

    mine = keep + swapped(send, "sub", 1)
    after = mine
    bit = 2
    while bit < n_sub:
        mine = mine + swapped(mine, "sub", bit)
        bit *= 2
    share, coarse_share, chosen, quarter_before, quarter_sum, coarse_before, coarse_sum = run(
        functools.partial(window_kernel, n_sub), (1,), (sub_core,),
        [
            *[whole(early_rows, w)] * n_sub, whole(*quarter_pool_rows.shape), whole(*pool_rows.shape),
            pl.BlockSpec((part * q_degree, w), lambda i, place: (place[1], 0)), whole(*edge_in.shape),
            pl.BlockSpec(memory_space=pl.ANY),
        ],
        (*all_early, quarter_pool_rows, pool_rows, quarter_edges.reshape(q_rows * q_degree, w), edge_in, after),
        (
            shaped(q_rows, w), shaped(c_part, w), shaped(rows, block, dtype=half), shaped(q_degree, part, w),
            shaped(part, w), shaped(c_degree, block, w), shaped(block, w),
        ),
        [
            whole(q_rows, w), whole(c_part, w), whole(rows, block), whole(q_degree, part, w), whole(part, w),
            whole(c_degree, block, w), whole(block, w),
        ],
        [pltpu.VMEM((block * c_degree, w), f32)], 24, 10**9,
    )
    other = swapped(mine, "sub", 1)

    quarter_nodes, to_next, to_previous = run(
        quarter_nodes_kernel, (), (flip,),
        [whole(part, w), whole(part, w), whole(q_rows, w), whole(2, q_margin)],
        (mine, other, share, quarter_halo),
        (shaped(q_rows, w), shaped(q_margin, w), shaped(q_margin, w)),
        [whole(q_rows, w), whole(q_margin, w), whole(q_margin, w)], [], 16, 10**8,
    )
    left = passed(to_next, "patch", 1)
    right = passed(to_previous, "patch", -1)
    sender_spec = pl.BlockSpec((q_degree, part), lambda i, flip: (0, flip[0]))
    quarter_first = run(
        functools.partial(quarter_first_kernel, tile), (1,), (flip,),
        [sender_spec, whole(q_rows, w), whole(q_degree, part, w), whole(*edge_in.shape)],
        (quarter_senders, quarter_nodes, quarter_before, edge_in),
        shaped(q_degree, part, w), whole(q_degree, part, w),
        [pltpu.VMEM((q_rows, 2 * w), half), pltpu.VMEM((q_degree * tile, q_rows), half)], 24, 3 * 10**9,
    )
    quarter_mine, keep, send = run(
        functools.partial(quarter_second_kernel, tile), (1,), (flip,),
        [
            sender_spec, whole(*quarter_pool_rows.shape), whole(q_rows, w), whole(q_margin, w), whole(q_margin, w),
            whole(q_degree, part, w), whole(part, w), *layer_specs,
        ],
        (quarter_senders, quarter_pool_rows, quarter_nodes, left, right, quarter_first, quarter_sum, *layers),
        (shaped(part, w), shaped(c_part, w), shaped(c_part, w)),
        [whole(part, w), whole(c_part, w), whole(c_part, w)],
        [pltpu.VMEM((2 * q_margin, 2 * w), half), pltpu.VMEM((4, 2 * w, 2 * w), half)], 24, 2 * 10**9,
    )

    own = (keep + swapped(send, "sub", 1)) * coarse_share
    quarter_other = swapped(quarter_mine, "sub", 1)
    pieces = [own] + [passed(own, "patch", -j) for j in range(1, n_patch)]
    partner = [swapped(value, "sub", 1) for value in pieces]
    base = run(
        fine_out_kernel, (), (flip,), [whole(*pool_rows.shape), whole(part, w), whole(part, w), whole(rows, w)],
        (pool_rows, quarter_mine, quarter_other, fine_new), shaped(rows, w), whole(rows, w),
        [pltpu.VMEM((q_rows, w), f32)], 24, 10**9,
    )
    return run(
        functools.partial(coarse_kernel, n_patch, c_tile), (1,), (patch_core,),
        [
            *[whole(c_part, w)] * (2 * n_patch), pl.BlockSpec((c_degree, block), lambda i, place: (0, place[0])),
            whole(c_degree, block, w), whole(block, w), whole(rows, block), whole(rows, w), *layer_specs,
        ],
        (*pieces, *partner, coarse_senders, coarse_before, coarse_sum, chosen, base, *layers),
        shaped(rows, w), whole(rows, w),
        [
            pltpu.VMEM((total, w), f32), pltpu.VMEM((total, 2 * w), half), pltpu.VMEM((4, 2 * w, 2 * w), half),
            pltpu.VMEM((c_degree * c_tile, total), half), pltpu.VMEM((c_degree, c_tile, w), f32),
            pltpu.VMEM((block, w), f32),
        ],
        big, 2 * 10**9,
    )


def solution(mesh):
    split = P(("groups", "patch", "sub"))
    patches = P(("groups", "patch"))
    return jax.shard_map(
        on_device,
        mesh=mesh,
        in_specs=(
            split, split, split, split, split, patches, patches, patches, patches, split, P("groups"),
            P(), P(), P(), P(),
        ),
        out_specs=split,
        check_vma=False,
    )
```

```python
import functools

import jax
import jax.numpy as jnp
from jax import lax
from jax.experimental import pallas as pl
from jax.experimental.pallas import tpu as pltpu
from jax.sharding import PartitionSpec as P


f32 = jnp.float32
half = jnp.bfloat16
LANES = 128
EPS = 1e-05


def side(x):
    high = x.astype(half)
    low = (x - high.astype(f32)).astype(half)
    return jnp.concatenate([high, low], axis=1)


def packed(w):
    row = side(w)
    return jnp.concatenate([row, row], axis=0)


def folded(y):
    w = y.shape[1] // 2
    return y[:, :w] + y[:, w:]


def times(a, b):
    return lax.dot_general(a, b, (((1,), (0,)), ((), ())), preferred_element_type=f32)


def centred_columns(w):
    return w - jnp.mean(w, axis=1, keepdims=True)


def inverse_spread(v):
    return lax.rsqrt(jnp.mean(v * v, axis=1, keepdims=True) + EPS)


def down(row):
    n = row.shape[1]
    parts = []
    for start in range(0, n, LANES):
        wide = jnp.broadcast_to(row[:, start : start + LANES], (LANES, LANES))
        parts.append(jnp.transpose(wide).astype(jnp.int16))
    return parts[0] if len(parts) == 1 else jnp.concatenate(parts, axis=0)


def picks(column, size):
    n = column.shape[0]
    lane = lax.broadcasted_iota(jnp.int32, (n, LANES), 1)
    one, zero = jnp.ones((n, LANES), half), jnp.zeros((n, LANES), half)
    parts = [
        jnp.where(column == (lane + start).astype(jnp.int16), one, zero)
        for start in range(0, size, LANES)
    ]
    return jnp.concatenate(parts, axis=1)


def members(row, size):
    n = row.shape[1]
    line = lax.broadcasted_iota(jnp.int32, (size, n), 0).astype(jnp.int16)
    entry = jnp.broadcast_to(row, (size, n)).astype(jnp.int16)
    return jnp.where(entry == line, jnp.ones((size, n), half), jnp.zeros((size, n), half))


def share_of_each(pools, first, size):
    line = (lax.broadcasted_iota(jnp.int32, (size, LANES), 0) + first).astype(jnp.int16)
    one, zero = jnp.ones((size, LANES), half), jnp.zeros((size, LANES), half)
    total = zero
    for pool in pools:
        for r in range(pool.shape[0]):
            entry = jnp.broadcast_to(pool[r : r + 1, :], (size, LANES)).astype(jnp.int16)
            total = total + jnp.where(entry == line, one, zero)
    return 1.0 / times(total, jnp.ones((LANES, LANES), half))


def first_part(degree, tile, sources, lhs, wide, column, edge, reach, before, extra=None):
    for k in range(degree):
        lhs[k * tile : (k + 1) * tile, :sources] = picks(column(k), sources)
        if edge is not None:
            lhs[k * tile : (k + 1) * tile, sources:] = side(edge(k))
    sums = folded(times(lhs[...], wide[...])).reshape(degree, tile, -1)
    for k in range(degree):
        part = sums[k] + reach
        before[k] = part if extra is None else part + extra[k]


def second_part(degree, tile, hidden, edge_sum, receivers, rhs_message, rhs_node, rhs_out):
    message = folded(times(side(hidden), rhs_message))
    message = (message * inverse_spread(message)).reshape(degree, tile, -1)
    total = edge_sum
    for k in range(degree):
        total = total + message[k]
    node = jnp.concatenate([side(receivers), side(total)], axis=1)
    node_hidden = jnp.maximum(folded(times(node, rhs_node)), 0.0)
    update = folded(times(side(node_hidden), rhs_out))
    return receivers + update * inverse_spread(update)


def pack_second(edge_out, node_in, node_out, weights):
    w = edge_out.shape[1]
    weights[0] = packed(centred_columns(edge_out[...]))
    weights[1] = packed(node_in[0:w])
    weights[2] = packed(node_in[w : 2 * w])
    weights[3] = packed(centred_columns(node_out[...]))


def with_halo(degree, tile, rows, margin, beyond, column, before):
    chosen = [picks(column(k) - jnp.int16(rows), 2 * margin) for k in range(degree)]
    sums = folded(times(jnp.concatenate(chosen, axis=0), beyond[...])).reshape(degree, tile, -1)
    parts = [jnp.maximum(sums[k] + before[k], 0.0) for k in range(degree)]
    return jnp.concatenate(parts, axis=0)


def gather_halo(lists, nodes, to_next, to_previous):
    both = side(nodes[...])
    for i, out in enumerate((to_next, to_previous)):
        out[...] = folded(times(picks(down(lists[i : i + 1, :]), nodes.shape[0]), both))


def start_kernel(lists, nodes, edges, pool, to_next, to_previous, early):
    gather_halo(lists, nodes, to_next, to_previous)
    count = edges.shape[0]
    early[:count, :] = edges[...]
    early[count:, :] = pool[...].astype(f32)


def fine_first_kernel(tile, senders, nodes, edges, edge_in, before, edge_sum, wide, reach_rhs, lhs):
    degree = edges.shape[0]
    rows, w = nodes.shape
    i = pl.program_id(0)

    @pl.when(i == 0)
    def _():
        wide[:rows, :] = side(folded(times(side(nodes[...]), packed(edge_in[0, 0:w]))))
        wide[rows:, :] = packed(edge_in[0, 2 * w : 3 * w])
        reach_rhs[...] = packed(edge_in[0, w : 2 * w])

    receivers = nodes[pl.ds(pl.multiple_of(i * tile, tile), tile), :]
    reach = folded(times(side(receivers), reach_rhs[...]))
    total = edges[0]
    for k in range(1, degree):
        total = total + edges[k]
    edge_sum[...] = total
    first_part(
        degree, tile, rows, lhs, wide, lambda k: down(senders[k : k + 1, :]), lambda k: edges[k], reach, before
    )


def rotated(target, flip, part):
    return jnp.where(target < part, target + flip * part, target - flip * part)


def fine_second_kernel(
    tile, flip, senders, pool, nodes, left, right, before, edge_sum, edge_in, edge_out, node_in, node_out,
    new, keep, send, beyond, weights,
):
    degree = before.shape[0]
    rows, w = nodes.shape
    margin = left.shape[0]
    i = pl.program_id(0)

    @pl.when(i == 0)
    def _():
        sender = packed(edge_in[0, 0:w])
        beyond[:margin, :] = side(folded(times(side(left[...]), sender)))
        beyond[margin:, :] = side(folded(times(side(right[...]), sender)))
        pack_second(edge_out.at[0], node_in.at[0], node_out.at[0], weights)
        keep[...] = jnp.zeros_like(keep)
        send[...] = jnp.zeros_like(send)

    receivers = nodes[pl.ds(pl.multiple_of(i * tile, tile), tile), :]
    hidden = with_halo(degree, tile, rows, margin, beyond, lambda k: down(senders[k : k + 1, :]), before)
    updated = second_part(
        degree, tile, hidden, edge_sum[...], receivers, weights[0],
        jnp.concatenate([weights[1], weights[2]], axis=0), weights[3],
    )
    new[...] = updated
    both = side(updated)
    part = keep.shape[0]
    per = tile // LANES
    target = jnp.concatenate([pool[pl.ds(i * per + j, 1), :] for j in range(per)], axis=1)
    target = rotated(target, flip[0], part)
    keep[...] += folded(times(members(target, part), both))
    send[...] += folded(times(members(target - part, part), both))


def window_kernel(n_sub, place, *refs):
    early, refs = refs[:n_sub], refs[n_sub:]
    (quarter_pool, fine_pool, quarter_edges, edge_in, _, share, coarse_share, chosen, quarter_before,
     quarter_sum, coarse_before, coarse_sum, edges) = refs
    w = edge_in.shape[2]
    piece = early[0].shape[0] - fine_pool.shape[0]
    pools = [block[piece:, :].astype(jnp.int32) for block in early]
    share[...] = share_of_each(pools, 0, share.shape[0])
    coarse_part = coarse_share.shape[0]
    coarse_share[...] = share_of_each([quarter_pool[...]], place[1] * coarse_part, coarse_part)

    degree, rows, _ = quarter_before.shape
    rhs = packed(edge_in[1, 2 * w : 3 * w])
    total = None
    for k in range(degree):
        edge = quarter_edges[pl.ds(k, rows, stride=degree), :]
        total = edge if total is None else total + edge
        quarter_before[k] = folded(times(side(edge), rhs))
    quarter_sum[...] = total

    for j in range(n_sub):
        at = lax.rem(place[0] + j, n_sub)
        edges[pl.ds(pl.multiple_of(at * piece, piece), piece), :] = early[j][:piece, :]
    degree, rows, _ = coarse_before.shape
    rhs = packed(edge_in[2, 2 * w : 3 * w])
    total = None
    for k in range(degree):
        edge = edges[pl.ds(k, rows, stride=degree), :]
        total = edge if total is None else total + edge
        coarse_before[k] = folded(times(side(edge), rhs))
    coarse_sum[...] = total

    parent = [down(quarter_pool[r : r + 1, :]) for r in range(quarter_pool.shape[0])]
    parent = side(jnp.concatenate(parent, axis=0).astype(jnp.int32).astype(f32))
    for r in range(fine_pool.shape[0]):
        rows = slice(r * LANES, (r + 1) * LANES)
        named = folded(times(picks(down(fine_pool[r : r + 1, :]), parent.shape[0]), parent))
        chosen[rows, :] = picks(named.astype(jnp.int32).astype(jnp.int16), chosen.shape[1])


def quarter_nodes_kernel(flip, mine, other, share, lists, nodes, to_next, to_previous):
    part = mine.shape[0]
    first = pl.multiple_of(flip[0] * part, part)
    second = pl.multiple_of((1 - flip[0]) * part, part)
    nodes[pl.ds(first, part), :] = mine[...] * share[pl.ds(first, part), :]
    nodes[pl.ds(second, part), :] = other[...] * share[pl.ds(second, part), :]
    gather_halo(lists, nodes, to_next, to_previous)


def quarter_first_kernel(tile, flip, senders, nodes, extra, edge_in, before, wide, lhs):
    degree, part, w = before.shape
    rows = nodes.shape[0]
    wide[...] = side(folded(times(side(nodes[...]), packed(edge_in[1, 0:w]))))
    reach_rhs = packed(edge_in[1, w : 2 * w])
    for t in range(part // tile):
        span = slice(t * tile, (t + 1) * tile)
        receivers = nodes[pl.ds(pl.multiple_of(flip[0] * part + t * tile, tile), tile), :]
        reach = folded(times(side(receivers), reach_rhs))
        first_part(
            degree, tile, rows, lhs, wide, lambda k: down(senders[k : k + 1, span]), None, reach,
            before.at[:, span, :], extra.at[:, span, :],
        )


def quarter_second_kernel(
    tile, flip, senders, pool, nodes, left, right, before, edge_sum, edge_in, edge_out, node_in, node_out,
    new, keep, send, beyond, weights,
):
    degree, part, w = before.shape
    rows = nodes.shape[0]
    margin = left.shape[0]
    sender = packed(edge_in[1, 0:w])
    beyond[:margin, :] = side(folded(times(side(left[...]), sender)))
    beyond[margin:, :] = side(folded(times(side(right[...]), sender)))
    pack_second(edge_out.at[1], node_in.at[1], node_out.at[1], weights)
    per = tile // LANES
    coarse_part = keep.shape[0]
    for t in range(part // tile):
        span = slice(t * tile, (t + 1) * tile)
        receivers = nodes[pl.ds(pl.multiple_of(flip[0] * part + t * tile, tile), tile), :]
        hidden = with_halo(
            degree, tile, rows, margin, beyond, lambda k: down(senders[k : k + 1, span]), before.at[:, span, :]
        )
        updated = second_part(
            degree, tile, hidden, edge_sum[span, :], receivers, weights[0],
            jnp.concatenate([weights[1], weights[2]], axis=0), weights[3],
        )
        new[span, :] = updated
        at = flip[0] * (part // LANES) + t * per
        target = jnp.concatenate([pool[pl.ds(at + j, 1), :] for j in range(per)], axis=1)
        target = rotated(target, flip[0], coarse_part)
        both = side(updated)
        kept = folded(times(members(target, coarse_part), both))
        sent = folded(times(members(target - coarse_part, coarse_part), both))
        keep[...] = kept if t == 0 else keep[...] + kept
        send[...] = sent if t == 0 else send[...] + sent


def fine_out_kernel(flip, pool, mine, other, fine_new, out, nodes):
    part = mine.shape[0]
    nodes[pl.ds(pl.multiple_of(flip[0] * part, part), part), :] = mine[...]
    nodes[pl.ds(pl.multiple_of((1 - flip[0]) * part, part), part), :] = other[...]
    both = side(nodes[...])
    for r in range(pool.shape[0]):
        rows = slice(r * LANES, (r + 1) * LANES)
        out[rows, :] = fine_new[rows, :] + folded(times(picks(down(pool[r : r + 1, :]), both.shape[0]), both))


def coarse_kernel(n_patch, tile, place, *refs):
    mine, refs = refs[:n_patch], refs[n_patch:]
    other, refs = refs[:n_patch], refs[n_patch:]
    (senders, extra, edge_sum, chosen, base, edge_in, edge_out, node_in, node_out,
     out, nodes, wide, weights, lhs, before, new) = refs
    part, w = mine[0].shape
    block = 2 * part
    degree = extra.shape[0]
    sources = nodes.shape[0]
    for j in range(n_patch):
        at = lax.rem(place[0] + j, n_patch) * block
        nodes[pl.ds(pl.multiple_of(at + place[1] * part, part), part), :] = mine[j][...]
        nodes[pl.ds(pl.multiple_of(at + (1 - place[1]) * part, part), part), :] = other[j][...]
    wide[...] = side(folded(times(side(nodes[...]), packed(edge_in[2, 0:w]))))
    reach_rhs = packed(edge_in[2, w : 2 * w])
    pack_second(edge_out.at[2], node_in.at[2], node_out.at[2], weights)
    for t in range(block // tile):
        span = slice(t * tile, (t + 1) * tile)
        receivers = nodes[pl.ds(pl.multiple_of(place[0] * block + t * tile, tile), tile), :]
        reach = folded(times(side(receivers), reach_rhs))
        first_part(
            degree, tile, sources, lhs, wide, lambda k: down(senders[k : k + 1, span]), None, reach, before,
            extra.at[:, span, :],
        )
        hidden = jnp.maximum(before[...], 0.0).reshape(degree * tile, w)
        new[span, :] = second_part(
            degree, tile, hidden, edge_sum[span, :], receivers, weights[0],
            jnp.concatenate([weights[1], weights[2]], axis=0), weights[3],
        )
    out[...] = base[...] + folded(times(chosen[...], side(new[...])))


def whole(*shape):
    return pl.BlockSpec(shape, lambda *_: (0,) * len(shape))


def shaped(*shape, dtype=f32):
    return jax.ShapeDtypeStruct(shape, dtype)


def run(kernel, grid, scalars, in_specs, operands, outs, out_specs, scratch, mega, flops):
    return pl.pallas_call(
        kernel,
        out_shape=outs,
        grid_spec=pltpu.PrefetchScalarGridSpec(
            num_scalar_prefetch=len(scalars), grid=grid, in_specs=in_specs, out_specs=out_specs,
            scratch_shapes=scratch,
        ),
        compiler_params=pltpu.CompilerParams(vmem_limit_bytes=mega * 1024 * 1024),
        cost_estimate=pl.CostEstimate(flops=flops, bytes_accessed=10**6, transcendentals=0),
    )(*scalars, *operands)


def passed(value, axis, steps):
    count = lax.axis_size(axis)
    return lax.ppermute(value, axis, [(s, (s + steps) % count) for s in range(count)])


def swapped(value, axis, bit):
    count = lax.axis_size(axis)
    return lax.ppermute(value, axis, [(s, s ^ bit) for s in range(count)])


def on_device(
    fine_nodes, fine_edges, fine_senders, fine_halo, fine_pool, quarter_edges, quarter_senders,
    quarter_halo, quarter_pool, coarse_edges, coarse_senders, edge_in, edge_out, node_in, node_out,
):
    n_sub, n_patch = lax.axis_size("sub"), lax.axis_size("patch")
    sub, patch = lax.axis_index("sub").astype(jnp.int32), lax.axis_index("patch").astype(jnp.int32)
    rows, degree, w = fine_edges.shape
    q_rows, q_degree, _ = quarter_edges.shape
    margin, q_margin = fine_halo.shape[1], quarter_halo.shape[1]
    piece, c_degree, _ = coarse_edges.shape
    total = coarse_senders.shape[0]
    block = total // n_patch
    part, c_part = q_rows // 2, block // 2
    tile = 256
    c_tile = min(block, tile)
    core = sub % 2
    flip = core.reshape(1)
    sub_core = jnp.stack([sub, core])
    patch_core = jnp.stack([patch, core])
    layers = (edge_in, edge_out, node_in, node_out)
    layer_specs = [whole(*x.shape) for x in layers]
    pool_rows = fine_pool.reshape(rows // LANES, LANES)
    quarter_pool_rows = quarter_pool.reshape(q_rows // LANES, LANES)
    fine_senders, quarter_senders, coarse_senders = fine_senders.T, quarter_senders.T, coarse_senders.T
    own_edges = coarse_edges.reshape(piece * c_degree, w)
    early_rows = piece * c_degree + pool_rows.shape[0]
    big = 14 if total <= 2048 else 60

    hbm = lambda x: pltpu.with_memory_space_constraint(x, pltpu.HBM)
    to_next, to_previous, early = run(
        start_kernel, (), (), [whole(2, margin), whole(rows, w), whole(*own_edges.shape), whole(*pool_rows.shape)],
        (hbm(fine_halo), hbm(fine_nodes), hbm(own_edges), hbm(pool_rows)),
        (shaped(margin, w), shaped(margin, w), shaped(early_rows, w)),
        [whole(margin, w), whole(margin, w), whole(early_rows, w)], [], 8, 10**8,
    )
    left = passed(to_next, ("patch", "sub"), 1)
    right = passed(to_previous, ("patch", "sub"), -1)
    all_early = [early] + [passed(early, "sub", -j) for j in range(1, n_sub)]

    before, edge_sum = run(
        functools.partial(fine_first_kernel, tile), (rows // tile,), (),
        [
            pl.BlockSpec((degree, tile), lambda i: (0, i)), whole(rows, w),
            pl.BlockSpec((degree, tile, w), lambda i: (0, i, 0)), whole(*edge_in.shape),
        ],
        (hbm(fine_senders), hbm(fine_nodes), hbm(fine_edges.transpose(1, 0, 2)), hbm(edge_in)),
        (pltpu.HBM((degree, rows, w), f32), pltpu.HBM((rows, w), f32)),
        [pl.BlockSpec((degree, tile, w), lambda i: (0, i, 0)), pl.BlockSpec((tile, w), lambda i: (i, 0))],
        [
            pltpu.VMEM((rows + 2 * w, 2 * w), half), pltpu.VMEM((2 * w, 2 * w), half),
            pltpu.VMEM((degree * tile, rows + 2 * w), half),
        ],
        16, 8 * 10**9,
    )
    fine_new, keep, send = run(
        functools.partial(fine_second_kernel, tile), (rows // tile,), (flip,),
        [
            pl.BlockSpec((degree, tile), lambda i, *_: (0, i)), whole(*pool_rows.shape), whole(rows, w),
            whole(margin, w), whole(margin, w), pl.BlockSpec((degree, tile, w), lambda i, *_: (0, i, 0)),
            pl.BlockSpec((tile, w), lambda i, *_: (i, 0)), *layer_specs,
        ],
        (fine_senders, pool_rows, fine_nodes, left, right, hbm(before), hbm(edge_sum), *layers),
        (pltpu.HBM((rows, w), f32), shaped(part, w), shaped(part, w)),
        [pl.BlockSpec((tile, w), lambda i, *_: (i, 0)), whole(part, w), whole(part, w)],
        [pltpu.VMEM((2 * margin, 2 * w), half), pltpu.VMEM((4, 2 * w, 2 * w), half)],
        12, 4 * 10**9,
    )

    mine = keep + swapped(send, "sub", 1)
    after = mine
    bit = 2
    while bit < n_sub:
        mine = mine + swapped(mine, "sub", bit)
        bit *= 2
    share, coarse_share, chosen, quarter_before, quarter_sum, coarse_before, coarse_sum = run(
        functools.partial(window_kernel, n_sub), (1,), (sub_core,),
        [
            *[whole(early_rows, w)] * n_sub, whole(*quarter_pool_rows.shape), whole(*pool_rows.shape),
            pl.BlockSpec((part * q_degree, w), lambda i, place: (place[1], 0)), whole(*edge_in.shape),
            pl.BlockSpec(memory_space=pl.ANY),
        ],
        (*all_early, quarter_pool_rows, pool_rows, quarter_edges.reshape(q_rows * q_degree, w), edge_in, after),
        (
            shaped(q_rows, w), shaped(c_part, w), shaped(rows, block, dtype=half), shaped(q_degree, part, w),
            shaped(part, w), shaped(c_degree, block, w), shaped(block, w),
        ),
        [
            whole(q_rows, w), whole(c_part, w), whole(rows, block), whole(q_degree, part, w), whole(part, w),
            whole(c_degree, block, w), whole(block, w),
        ],
        [pltpu.VMEM((block * c_degree, w), f32)], 12, 10**9,
    )
    other = swapped(mine, "sub", 1)

    quarter_nodes, to_next, to_previous = run(
        quarter_nodes_kernel, (), (flip,),
        [whole(part, w), whole(part, w), whole(q_rows, w), whole(2, q_margin)],
        (mine, other, share, quarter_halo),
        (shaped(q_rows, w), shaped(q_margin, w), shaped(q_margin, w)),
        [whole(q_rows, w), whole(q_margin, w), whole(q_margin, w)], [], 8, 10**8,
    )
    left = passed(to_next, "patch", 1)
    right = passed(to_previous, "patch", -1)
    sender_spec = pl.BlockSpec((q_degree, part), lambda i, flip: (0, flip[0]))
    quarter_first = run(
        functools.partial(quarter_first_kernel, tile), (1,), (flip,),
        [sender_spec, whole(q_rows, w), whole(q_degree, part, w), whole(*edge_in.shape)],
        (quarter_senders, quarter_nodes, quarter_before, edge_in),
        shaped(q_degree, part, w), whole(q_degree, part, w),
        [pltpu.VMEM((q_rows, 2 * w), half), pltpu.VMEM((q_degree * tile, q_rows), half)], 12, 3 * 10**9,
    )
    quarter_mine, keep, send = run(
        functools.partial(quarter_second_kernel, tile), (1,), (flip,),
        [
            sender_spec, whole(*quarter_pool_rows.shape), whole(q_rows, w), whole(q_margin, w), whole(q_margin, w),
            whole(q_degree, part, w), whole(part, w), *layer_specs,
        ],
        (quarter_senders, quarter_pool_rows, quarter_nodes, left, right, quarter_first, quarter_sum, *layers),
        (shaped(part, w), shaped(c_part, w), shaped(c_part, w)),
        [whole(part, w), whole(c_part, w), whole(c_part, w)],
        [pltpu.VMEM((2 * q_margin, 2 * w), half), pltpu.VMEM((4, 2 * w, 2 * w), half)], 12, 2 * 10**9,
    )

    own = (keep + swapped(send, "sub", 1)) * coarse_share
    quarter_other = swapped(quarter_mine, "sub", 1)
    pieces = [own] + [passed(own, "patch", -j) for j in range(1, n_patch)]
    partner = [swapped(value, "sub", 1) for value in pieces]
    base = run(
        fine_out_kernel, (), (flip,), [whole(*pool_rows.shape), whole(part, w), whole(part, w), whole(rows, w)],
        (pool_rows, quarter_mine, quarter_other, hbm(fine_new)), shaped(rows, w), whole(rows, w),
        [pltpu.VMEM((q_rows, w), f32)], 12, 10**9,
    )
    return run(
        functools.partial(coarse_kernel, n_patch, c_tile), (1,), (patch_core,),
        [
            *[whole(c_part, w)] * (2 * n_patch), pl.BlockSpec((c_degree, block), lambda i, place: (0, place[0])),
            whole(c_degree, block, w), whole(block, w), whole(rows, block), whole(rows, w), *layer_specs,
        ],
        (*pieces, *partner, coarse_senders, coarse_before, coarse_sum, chosen, base, *layers),
        shaped(rows, w), whole(rows, w),
        [
            pltpu.VMEM((total, w), f32), pltpu.VMEM((total, 2 * w), half), pltpu.VMEM((4, 2 * w, 2 * w), half),
            pltpu.VMEM((c_degree * c_tile, total), half), pltpu.VMEM((c_degree, c_tile, w), f32),
            pltpu.VMEM((block, w), f32),
        ],
        big, 2 * 10**9,
    )


def solution(mesh):
    split = P(("groups", "patch", "sub"))
    patches = P(("groups", "patch"))
    return jax.shard_map(
        on_device,
        mesh=mesh,
        in_specs=(
            split, split, split, split, split, patches, patches, patches, patches, split, P("groups"),
            P(), P(), P(), P(),
        ),
        out_specs=split,
        check_vma=False,
    )
```

```python
import functools

import jax
import jax.numpy as jnp
from jax import lax
from jax.experimental import pallas as pl
from jax.experimental.pallas import tpu as pltpu
from jax.sharding import PartitionSpec as P


f32 = jnp.float32
half = jnp.bfloat16
LANES = 128
EPS = 1e-05


def side(x):
    high = x.astype(half)
    low = (x - high.astype(f32)).astype(half)
    return jnp.concatenate([high, low], axis=1)


def packed(w):
    row = side(w)
    return jnp.concatenate([row, row], axis=0)


def folded(y):
    w = y.shape[1] // 2
    return y[:, :w] + y[:, w:]


def times(a, b):
    return lax.dot_general(a, b, (((1,), (0,)), ((), ())), preferred_element_type=f32)


def centred_columns(w):
    return w - jnp.mean(w, axis=1, keepdims=True)


def inverse_spread(v):
    return lax.rsqrt(jnp.mean(v * v, axis=1, keepdims=True) + EPS)


def down(row):
    n = row.shape[1]
    parts = []
    for start in range(0, n, LANES):
        wide = jnp.broadcast_to(row[:, start : start + LANES], (LANES, LANES))
        parts.append(jnp.transpose(wide).astype(jnp.int16))
    return parts[0] if len(parts) == 1 else jnp.concatenate(parts, axis=0)


def picks(column, size):
    n = column.shape[0]
    lane = lax.broadcasted_iota(jnp.int32, (n, LANES), 1)
    one, zero = jnp.ones((n, LANES), half), jnp.zeros((n, LANES), half)
    parts = [
        jnp.where(column == (lane + start).astype(jnp.int16), one, zero)
        for start in range(0, size, LANES)
    ]
    return jnp.concatenate(parts, axis=1)


def members(row, size):
    n = row.shape[1]
    line = lax.broadcasted_iota(jnp.int32, (size, n), 0).astype(jnp.int16)
    entry = jnp.broadcast_to(row, (size, n)).astype(jnp.int16)
    return jnp.where(entry == line, jnp.ones((size, n), half), jnp.zeros((size, n), half))


def counts_of(pools, first, size):
    line = (lax.broadcasted_iota(jnp.int32, (size, LANES), 0) + first).astype(jnp.int16)
    one, zero = jnp.ones((size, LANES), half), jnp.zeros((size, LANES), half)
    total = zero
    for pool in pools:
        for r in range(pool.shape[0]):
            entry = jnp.broadcast_to(pool[r : r + 1, :], (size, LANES)).astype(jnp.int16)
            total = total + jnp.where(entry == line, one, zero)
    return times(total, jnp.ones((LANES, LANES), half))


def along_lanes(pool, first, lines):
    rows, n = pool.shape
    column = jnp.concatenate([down(pool[r : r + 1, :]) for r in range(rows)], axis=0)
    lane = lax.broadcasted_iota(jnp.int32, (rows * n, LANES), 1) + first
    one, zero = jnp.ones((rows * n, LANES), half), jnp.zeros((rows * n, LANES), half)
    out = []
    for r in range(lines):
        hits = jnp.where(column == (lane + r * LANES).astype(jnp.int16), one, zero)
        out.append(times(jnp.ones((8, rows * n), half), hits)[0:1, :])
    return jnp.concatenate(out, axis=0)


def first_part(degree, tile, lhs, wide, column, reach, before, extra):
    sources = wide.shape[0]
    for k in range(degree):
        lhs[k * tile : (k + 1) * tile, :] = picks(column(k), sources)
    sums = folded(times(lhs[...], wide[...])).reshape(degree, tile, -1)
    for k in range(degree):
        before[k][...] = sums[k] + reach + extra[k]


def second_part(degree, tile, hidden, edge_sum, receivers, weights):
    message = folded(times(side(hidden), weights[0]))
    message = (message * inverse_spread(message)).reshape(degree, tile, -1)
    total = edge_sum
    for k in range(degree):
        total = total + message[k]
    node = jnp.concatenate([side(receivers), side(total)], axis=1)
    rhs_node = jnp.concatenate([weights[1], weights[2]], axis=0)
    node_hidden = jnp.maximum(folded(times(node, rhs_node)), 0.0)
    update = folded(times(side(node_hidden), weights[3]))
    return receivers + update * inverse_spread(update)


def pack_first(edge_in, weights):
    w = edge_in.shape[1]
    weights[0] = packed(edge_in[0:w])
    weights[1] = packed(edge_in[w : 2 * w])


def pack_second(edge_out, node_in, node_out, weights):
    w = edge_out.shape[1]
    weights[0] = packed(centred_columns(edge_out[...]))
    weights[1] = packed(node_in[0:w])
    weights[2] = packed(node_in[w : 2 * w])
    weights[3] = packed(centred_columns(node_out[...]))


def with_halo(degree, tile, rows, margin, beyond, column, before):
    chosen = [picks(column(k) - jnp.int16(rows), 2 * margin) for k in range(degree)]
    sums = folded(times(jnp.concatenate(chosen, axis=0), beyond[...])).reshape(degree, tile, -1)
    parts = [jnp.maximum(sums[k] + before[k][...], 0.0) for k in range(degree)]
    return jnp.concatenate(parts, axis=0)


def halo_sources(left, right, sender, beyond):
    margin = left.shape[0]
    beyond[:margin, :] = side(folded(times(side(left[...]), sender)))
    beyond[margin:, :] = side(folded(times(side(right[...]), sender)))


def rotated(target, flip, part):
    return jnp.where(target < part, target + flip * part, target - flip * part)


def gather_halo(lists, nodes, to_next, to_previous):
    both = side(nodes[...])
    for i, out in enumerate((to_next, to_previous)):
        out[...] = folded(times(picks(down(lists[i : i + 1, :]), nodes.shape[0]), both))


def start_kernel(lists, nodes, senders, pool, edge_in, to_next, to_previous, kept_nodes, kept_senders, kept_pool, weights):
    gather_halo(lists, nodes, to_next, to_previous)
    kept_nodes[...] = nodes[...]
    kept_senders[...] = senders[...]
    kept_pool[...] = pool[...]
    pack_first(edge_in.at[0], weights)
    w = nodes.shape[1]
    weights[2] = packed(edge_in[0, 2 * w : 3 * w])


def fine_first_kernel(lines, flip, senders, nodes, pool, weights, edges, *refs):
    degree = edges.shape[0]
    before, refs = refs[:degree], refs[degree:]
    columns, refs = refs[:degree], refs[degree:]
    edge_sum, counts, wide, lhs, local, arrived = refs
    rows, _ = nodes.shape
    copies = [pltpu.make_async_copy(edges.at[k], local.at[k], arrived.at[k]) for k in range(degree)]
    for copy in copies:
        copy.start()
    wide[:rows, :] = side(folded(times(side(nodes[...]), weights[0])))
    wide[rows:, :] = weights[2]
    reach = folded(times(side(nodes[...]), weights[1]))
    part = lines * LANES
    height = counts.shape[0] // 2
    counts[...] = jnp.zeros_like(counts)
    counts[:lines, :] = along_lanes(pool, flip[0] * part, lines)
    counts[height : height + lines, :] = along_lanes(pool, (1 - flip[0]) * part, lines)
    for k in range(degree):
        columns[k][...] = jnp.concatenate(
            [down(senders[k : k + 1, start : start + LANES]) for start in range(0, rows, LANES)], axis=0
        )
        copies[k].wait()
        lhs[k % 2, :, :rows] = picks(columns[k][...], rows)
        lhs[k % 2, :, rows:] = side(local[k])
        before[k][...] = folded(times(lhs[k % 2], wide[...])) + reach
        edge_sum[...] = local[k] if k == 0 else edge_sum[...] + local[k]


def fine_second_kernel(degree, flip, pool, nodes, left, right, counts, first_weights, *refs):
    before, refs = refs[:degree], refs[degree:]
    columns, refs = refs[:degree], refs[degree:]
    edge_sum, edge_out, node_in, node_out, new, keep, send, beyond, weights, held, sent = refs
    rows, _ = nodes.shape
    margin = left.shape[0]
    halo_sources(left, right, first_weights[0], beyond)
    pack_second(edge_out.at[0], node_in.at[0], node_out.at[0], weights)
    hidden = with_halo(degree, rows, rows, margin, beyond, lambda k: columns[k][...], before)
    held[...] = second_part(degree, rows, hidden, edge_sum[...], nodes[...], weights)
    copy = pltpu.make_async_copy(held, new, sent)
    copy.start()
    both = side(held[...])
    height = counts.shape[0] // 2
    part = keep.shape[0] - height
    target = jnp.concatenate([pool[j : j + 1, :] for j in range(pool.shape[0])], axis=1)
    target = rotated(target, flip[0], part)
    send[:part, :] = folded(times(members(target - part, part), both))
    keep[:part, :] = folded(times(members(target, part), both))
    keep[part:, :] = counts[:height, :]
    send[part:, :] = counts[height:, :]
    copy.wait()


def window_kernel(
    flip, quarter_pool, fine_pool, quarter_edges, quarter_senders, coarse_senders, edge_in, edge_out, node_in, node_out, _,
    coarse_share, chosen, quarter_before, quarter_sum, quarter_columns, coarse_columns, fine_columns,
    quarter_first, quarter_second, coarse_first, coarse_second,
):
    w = edge_in.shape[2]
    block = coarse_share.shape[0]
    share = 1.0 / counts_of([quarter_pool[...]], 0, block)
    coarse_share[...] = share

    degree, rows, _ = quarter_before.shape
    rhs = packed(edge_in[1, 2 * w : 3 * w])
    total = None
    for k in range(degree):
        edge = quarter_edges[pl.ds(k, rows, stride=degree), :]
        total = edge if total is None else total + edge
        quarter_before[k] = folded(times(side(edge), rhs))
    quarter_sum[...] = total
    pack_first(edge_in.at[1], quarter_first)
    pack_second(edge_out.at[1], node_in.at[1], node_out.at[1], quarter_second)
    pack_first(edge_in.at[2], coarse_first)
    coarse_first[2] = packed(edge_in[2, 2 * w : 3 * w])
    pack_second(edge_out.at[2], node_in.at[2], node_out.at[2], coarse_second)

    for k in range(degree):
        for start in range(0, rows, LANES):
            quarter_columns[k, start : start + LANES, :] = down(quarter_senders[k : k + 1, start : start + LANES])
    for k in range(coarse_columns.shape[0]):
        for start in range(0, block, LANES):
            coarse_columns[k, start : start + LANES, :] = down(coarse_senders[k : k + 1, start : start + LANES])

    parent = [down(quarter_pool[r : r + 1, :]) for r in range(quarter_pool.shape[0])]
    parent = side(jnp.concatenate(parent, axis=0).astype(jnp.int32).astype(f32))
    for r in range(fine_pool.shape[0]):
        rows = slice(r * LANES, (r + 1) * LANES)
        column = down(fine_pool[r : r + 1, :])
        fine_columns[rows, :] = column
        named = folded(times(picks(column, parent.shape[0]), parent))
        chosen[rows, :] = picks(named.astype(jnp.int32).astype(jnp.int16), chosen.shape[1])


def mean_kernel(lines, mine, theirs, out):
    part = out.shape[0]
    counts = mine[part : part + lines, :] + theirs[part : part + lines, :]
    for r in range(lines):
        rows = slice(r * LANES, (r + 1) * LANES)
        share = 1.0 / jnp.transpose(jnp.broadcast_to(counts[r : r + 1, :], (LANES, LANES)))
        out[rows, :] = (mine[rows, :] + theirs[rows, :]) * share


def quarter_nodes_kernel(flip, mine, other, lists, nodes, to_next, to_previous):
    part = mine.shape[0]
    nodes[pl.ds(pl.multiple_of(flip[0] * part, part), part), :] = mine[...]
    nodes[pl.ds(pl.multiple_of((1 - flip[0]) * part, part), part), :] = other[...]
    gather_halo(lists, nodes, to_next, to_previous)


def quarter_first_kernel(tile, columns, nodes, mine, extra, weights, before, wide, lhs):
    degree, part, _ = before.shape
    wide[...] = side(folded(times(side(nodes[...]), weights[0])))
    for t in range(part // tile):
        span = slice(t * tile, (t + 1) * tile)
        reach = folded(times(side(mine[span, :]), weights[1]))
        first_part(
            degree, tile, lhs, wide, lambda k: columns[k, span, :], reach,
            [before.at[k, span, :] for k in range(degree)], extra.at[:, span, :],
        )


def quarter_second_kernel(
    flip, columns, pool, mine, left, right, before, edge_sum, first_weights, weights, new, keep, both, beyond,
):
    degree, part, _ = before.shape
    margin = left.shape[0]
    halo_sources(left, right, first_weights[0], beyond)
    hidden = with_halo(
        degree, part, 2 * part, margin, beyond, lambda k: columns[k], [before.at[k] for k in range(degree)]
    )
    updated = second_part(degree, part, hidden, edge_sum[...], mine[...], weights)
    new[...] = updated
    coarse_part = keep.shape[0]
    at = flip[0] * (part // LANES)
    target = jnp.concatenate([pool[pl.ds(at + j, 1), :] for j in range(part // LANES)], axis=1)
    target = rotated(target, flip[0], coarse_part)
    split = side(updated)
    both[:coarse_part, :] = folded(times(members(target - coarse_part, coarse_part), split))
    kept = folded(times(members(target, coarse_part), split))
    both[coarse_part:, :] = kept
    keep[...] = kept


def base_kernel(n_sub, place, columns, mine, other, fine_new, weights, *refs):
    pieces, refs = refs[:n_sub], refs[n_sub:]
    out, before, edge_sum, nodes, edges = refs
    part = mine.shape[0]
    piece = pieces[0].shape[0]
    for j in range(n_sub):
        at = jnp.bitwise_xor(place[0], j)
        edges[pl.ds(pl.multiple_of(at * piece, piece), piece), :] = pieces[j][...]
    degree, block, _ = before.shape
    total = None
    for k in range(degree):
        edge = edges[pl.ds(k, block, stride=degree), :]
        total = edge if total is None else total + edge
        before[k] = folded(times(side(edge), weights[2]))
    edge_sum[...] = total
    nodes[pl.ds(pl.multiple_of(place[1] * part, part), part), :] = mine[...]
    nodes[pl.ds(pl.multiple_of((1 - place[1]) * part, part), part), :] = other[...]
    both = side(nodes[...])
    out[...] = fine_new[...] + folded(times(picks(columns[...], both.shape[0]), both))


def coarse_kernel(n_patch, tile, place, *refs):
    mine, refs = refs[:n_patch], refs[n_patch:]
    other, refs = refs[:n_patch], refs[n_patch:]
    (columns, extra, edge_sum, chosen, base, first_weights, weights,
     out, nodes, wide, lhs, before, new, held, sent) = refs
    part, w = mine[0].shape
    block = 2 * part
    degree = extra.shape[0]
    for j in range(n_patch):
        at = lax.rem(place[0] + j, n_patch) * block
        nodes[pl.ds(pl.multiple_of(at + place[1] * part, part), part), :] = mine[j][...]
        nodes[pl.ds(pl.multiple_of(at + (1 - place[1]) * part, part), part), :] = other[j][...]
    wide[...] = side(folded(times(side(nodes[...]), first_weights[0])))
    for t in range(block // tile):
        span = slice(t * tile, (t + 1) * tile)
        receivers = nodes[pl.ds(pl.multiple_of(place[0] * block + t * tile, tile), tile), :]
        reach = folded(times(side(receivers), first_weights[1]))
        first_part(
            degree, tile, lhs, wide, lambda k: columns[k, span, :], reach,
            [before.at[k] for k in range(degree)], extra.at[:, span, :],
        )
        hidden = jnp.maximum(before[...], 0.0).reshape(degree * tile, w)
        new[span, :] = second_part(degree, tile, hidden, edge_sum[span, :], receivers, weights)
    both = side(new[...])
    steps = sent.shape[0]
    rows = out.shape[0] // steps
    copies = []
    for i in range(steps):
        span = slice(i * rows, (i + 1) * rows)
        held[span, :] = base[span, :] + folded(times(chosen[span, :], both))
        copies.append(pltpu.make_async_copy(held.at[span, :], out.at[span, :], sent.at[i]))
        copies[-1].start()
    for copy in copies:
        copy.wait()


def whole(*shape):
    return pl.BlockSpec(shape, lambda *_: (0,) * len(shape))


def shaped(*shape, dtype=f32):
    return jax.ShapeDtypeStruct(shape, dtype)


def run(kernel, grid, scalars, in_specs, operands, outs, out_specs, scratch, mega, flops):
    return pl.pallas_call(
        kernel,
        out_shape=outs,
        grid_spec=pltpu.PrefetchScalarGridSpec(
            num_scalar_prefetch=len(scalars), grid=grid, in_specs=in_specs, out_specs=out_specs,
            scratch_shapes=scratch,
        ),
        compiler_params=pltpu.CompilerParams(vmem_limit_bytes=mega * 1024 * 1024),
        cost_estimate=pl.CostEstimate(flops=flops, bytes_accessed=10**6, transcendentals=0),
    )(*scalars, *operands)


def passed(value, axis, steps):
    count = lax.axis_size(axis)
    return lax.ppermute(value, axis, [(s, (s + steps) % count) for s in range(count)])


def swapped(value, axis, bit):
    count = lax.axis_size(axis)
    return lax.ppermute(value, axis, [(s, s ^ bit) for s in range(count)])


def on_device(
    fine_nodes, fine_edges, fine_senders, fine_halo, fine_pool, quarter_edges, quarter_senders,
    quarter_halo, quarter_pool, coarse_edges, coarse_senders, edge_in, edge_out, node_in, node_out,
):
    n_sub, n_patch = lax.axis_size("sub"), lax.axis_size("patch")
    sub, patch = lax.axis_index("sub").astype(jnp.int32), lax.axis_index("patch").astype(jnp.int32)
    rows, degree, w = fine_edges.shape
    q_rows, q_degree, _ = quarter_edges.shape
    margin, q_margin = fine_halo.shape[1], quarter_halo.shape[1]
    piece, c_degree, _ = coarse_edges.shape
    total = coarse_senders.shape[0]
    block = total // n_patch
    part, c_part = q_rows // 2, block // 2
    tile = min(256, part)
    c_tile = min(256, block)
    lines = part // LANES
    height = -(-lines // 8) * 8
    core = sub % 2
    flip = core.reshape(1)
    sub_core = jnp.stack([sub, core])
    patch_core = jnp.stack([patch, core])
    layers = (edge_in, edge_out, node_in, node_out)
    layer_specs = [whole(*x.shape) for x in layers]
    in_hbm = pl.BlockSpec(memory_space=pl.ANY)
    pool_rows = fine_pool.reshape(rows // LANES, LANES)
    quarter_pool_rows = quarter_pool.reshape(q_rows // LANES, LANES)
    fine_senders, quarter_senders, coarse_senders = fine_senders.T, quarter_senders.T, coarse_senders.T
    own_edges = coarse_edges.reshape(piece * c_degree, w)
    hbm = lambda x: pltpu.with_memory_space_constraint(x, pltpu.HBM)
    mats = lambda n: (n, 2 * w, 2 * w)
    short = jnp.int16
    big = 16 if total <= 2048 else 48

    to_next, to_previous, nodes, senders, pool, fine_weights = run(
        start_kernel, (1,), (),
        [
            whole(2, margin), whole(rows, w), whole(degree, rows), whole(*pool_rows.shape),
            pl.BlockSpec((1, 3 * w, w), lambda i: (0, 0, 0)),
        ],
        (hbm(fine_halo), hbm(fine_nodes), hbm(fine_senders), hbm(pool_rows), hbm(edge_in)),
        (
            shaped(margin, w), shaped(margin, w), shaped(rows, w), shaped(degree, rows, dtype=jnp.int32),
            shaped(*pool_rows.shape, dtype=jnp.int32), shaped(*mats(3), dtype=half),
        ),
        [
            whole(margin, w), whole(margin, w), whole(rows, w), whole(degree, rows), whole(*pool_rows.shape),
            whole(*mats(3)),
        ],
        [], 8, 10**8,
    )
    left = passed(to_next, ("patch", "sub"), 1)
    right = passed(to_previous, ("patch", "sub"), -1)
    firsts = run(
        functools.partial(fine_first_kernel, lines), (1,), (flip,),
        [whole(degree, rows), whole(rows, w), whole(*pool_rows.shape), whole(*mats(3)), in_hbm],
        (senders, nodes, pool, fine_weights, hbm(fine_edges.transpose(1, 0, 2))),
        (
            *(shaped(rows, w),) * degree, *(shaped(rows, w, dtype=short),) * degree, shaped(rows, w),
            shaped(2 * height, w),
        ),
        [whole(rows, w)] * (2 * degree + 1) + [whole(2 * height, w)],
        [
            pltpu.VMEM((rows + 2 * w, 2 * w), half), pltpu.VMEM((2, rows, rows + 2 * w), half),
            pltpu.VMEM((degree, rows, w), f32), pltpu.SemaphoreType.DMA((degree,)),
        ],
        30, 8 * 10**9,
    )
    before, columns, (edge_sum, counts) = firsts[:degree], firsts[degree : 2 * degree], firsts[2 * degree :]
    fine_new, keep, send = run(
        functools.partial(fine_second_kernel, degree), (1,), (flip,),
        [
            whole(*pool_rows.shape), whole(rows, w), whole(margin, w), whole(margin, w), whole(2 * height, w),
            whole(*mats(3)), *[whole(rows, w)] * (2 * degree + 1), *layer_specs[1:],
        ],
        (pool, nodes, left, right, counts, fine_weights, *before, *columns, edge_sum, *layers[1:]),
        (pltpu.HBM((rows, w), f32), shaped(part + height, w), shaped(part + height, w)),
        [in_hbm, whole(part + height, w), whole(part + height, w)],
        [
            pltpu.VMEM((2 * margin, 2 * w), half), pltpu.VMEM(mats(4), half), pltpu.VMEM((rows, w), f32),
            pltpu.SemaphoreType.DMA,
        ],
        30, 4 * 10**9,
    )

    mine, theirs = keep, swapped(send, "sub", 1)
    bit = 2
    after = theirs
    while bit < n_sub:
        mine = mine + theirs
        theirs = swapped(mine, "sub", bit)
        after = mine if bit == 2 else after
        bit *= 2
    (coarse_share, chosen, quarter_before, quarter_sum, quarter_columns, coarse_columns, fine_columns,
     quarter_weights, quarter_later, coarse_weights, coarse_later) = run(
        window_kernel, (1,), (patch_core,),
        [
            whole(*quarter_pool_rows.shape), whole(*pool_rows.shape),
            pl.BlockSpec((part * q_degree, w), lambda i, place: (place[1], 0)),
            pl.BlockSpec((q_degree, part), lambda i, place: (0, place[1])),
            pl.BlockSpec((c_degree, block), lambda i, place: (0, place[0])), *layer_specs, in_hbm,
        ],
        (quarter_pool_rows, pool, quarter_edges.reshape(q_rows * q_degree, w), quarter_senders, coarse_senders,
         *layers, after),
        (
            shaped(block, w), shaped(rows, block, dtype=half), shaped(q_degree, part, w), shaped(part, w),
            shaped(q_degree, part, w, dtype=short), shaped(c_degree, block, w, dtype=short),
            shaped(rows, w, dtype=short), shaped(*mats(2), dtype=half), shaped(*mats(4), dtype=half),
            shaped(*mats(3), dtype=half), shaped(*mats(4), dtype=half),
        ),
        [
            whole(block, w), whole(rows, block), whole(q_degree, part, w), whole(part, w), whole(q_degree, part, w),
            whole(c_degree, block, w), whole(rows, w), whole(*mats(2)), whole(*mats(4)), whole(*mats(3)),
            whole(*mats(4)),
        ],
        [], 16, 10**9,
    )
    edge_pieces = [own_edges, swapped(own_edges, "sub", 1)]
    mine = run(
        functools.partial(mean_kernel, lines), (1,), (), [whole(part + height, w)] * 2, (mine, theirs),
        shaped(part, w), whole(part, w), [], 6, 10**7,
    )
    other = swapped(mine, "sub", 1)

    quarter_nodes, to_next, to_previous = run(
        quarter_nodes_kernel, (1,), (flip,), [whole(part, w), whole(part, w), whole(2, q_margin)],
        (mine, other, quarter_halo), (shaped(q_rows, w), shaped(q_margin, w), shaped(q_margin, w)),
        [whole(q_rows, w), whole(q_margin, w), whole(q_margin, w)], [], 8, 10**8,
    )
    left = passed(to_next, "patch", 1)
    right = passed(to_previous, "patch", -1)
    bit = 2
    while bit < n_sub:
        edge_pieces += [swapped(value, "sub", bit) for value in edge_pieces]
        bit *= 2
    quarter_first = run(
        functools.partial(quarter_first_kernel, tile), (1,), (),
        [whole(q_degree, part, w), whole(q_rows, w), whole(part, w), whole(q_degree, part, w), whole(*mats(2))],
        (quarter_columns, quarter_nodes, mine, quarter_before, quarter_weights),
        shaped(q_degree, part, w), whole(q_degree, part, w),
        [pltpu.VMEM((q_rows, 2 * w), half), pltpu.VMEM((q_degree * tile, q_rows), half)], 16, 3 * 10**9,
    )
    quarter_mine, keep, both = run(
        quarter_second_kernel, (1,), (flip,),
        [
            whole(q_degree, part, w), whole(*quarter_pool_rows.shape), whole(part, w), whole(q_margin, w),
            whole(q_margin, w), whole(q_degree, part, w), whole(part, w), whole(*mats(2)), whole(*mats(4)),
        ],
        (quarter_columns, quarter_pool_rows, mine, left, right, quarter_first, quarter_sum, quarter_weights,
         quarter_later),
        (shaped(part, w), shaped(c_part, w), shaped(block, w)),
        [whole(part, w), whole(c_part, w), whole(block, w)],
        [pltpu.VMEM((2 * q_margin, 2 * w), half)], 16, 2 * 10**9,
    )

    theirs = swapped(both, "sub", 1)
    share = lax.dynamic_slice_in_dim(coarse_share, core * c_part, c_part, 0)
    own = (keep + theirs[:c_part]) * share
    share = lax.dynamic_slice_in_dim(coarse_share, (1 - core) * c_part, c_part, 0)
    own_partner = (both[:c_part] + theirs[c_part:]) * share
    quarter_other = swapped(quarter_mine, "sub", 1)
    pieces = [own] + [passed(own, "patch", -j) for j in range(1, n_patch)]
    partner = [own_partner] + [swapped(pieces[j], "sub", 1) for j in range(1, n_patch)]
    base, coarse_before, coarse_sum = run(
        functools.partial(base_kernel, n_sub), (1,), (sub_core,),
        [
            whole(rows, w), whole(part, w), whole(part, w), whole(rows, w), whole(*mats(3)),
            *[whole(*own_edges.shape)] * n_sub,
        ],
        (fine_columns, quarter_mine, quarter_other, hbm(fine_new), coarse_weights, *edge_pieces),
        (shaped(rows, w), shaped(c_degree, block, w), shaped(block, w)),
        [whole(rows, w), whole(c_degree, block, w), whole(block, w)],
        [pltpu.VMEM((q_rows, w), f32), pltpu.VMEM((block * c_degree, w), f32)], 16, 10**9,
    )
    return run(
        functools.partial(coarse_kernel, n_patch, c_tile), (1,), (patch_core,),
        [
            *[whole(c_part, w)] * (2 * n_patch), whole(c_degree, block, w), whole(c_degree, block, w),
            whole(block, w), whole(rows, block), whole(rows, w), whole(*mats(3)), whole(*mats(4)),
        ],
        (*pieces, *partner, coarse_columns, coarse_before, coarse_sum, chosen, base, coarse_weights, coarse_later),
        shaped(rows, w), in_hbm,
        [
            pltpu.VMEM((total, w), f32), pltpu.VMEM((total, 2 * w), half),
            pltpu.VMEM((c_degree * c_tile, total), half), pltpu.VMEM((c_degree, c_tile, w), f32),
            pltpu.VMEM((block, w), f32), pltpu.VMEM((rows, w), f32), pltpu.SemaphoreType.DMA((4,)),
        ],
        big, 2 * 10**9,
    )


def solution(mesh):
    split = P(("groups", "patch", "sub"))
    patches = P(("groups", "patch"))
    return jax.shard_map(
        on_device,
        mesh=mesh,
        in_specs=(
            split, split, split, split, split, patches, patches, patches, patches, split, P("groups"),
            P(), P(), P(), P(),
        ),
        out_specs=split,
        check_vma=False,
    )
```

```python
import functools

import jax
import jax.numpy as jnp
from jax import lax
from jax.experimental import pallas as pl
from jax.experimental.pallas import tpu as pltpu
from jax.sharding import PartitionSpec as P


f32 = jnp.float32
half = jnp.bfloat16
LANES = 128
EPS = 1e-05


def side(x):
    high = x.astype(half)
    low = (x - high.astype(f32)).astype(half)
    return jnp.concatenate([high, low], axis=1)


def packed(w):
    row = side(w)
    return jnp.concatenate([row, row], axis=0)


def folded(y):
    w = y.shape[1] // 2
    return y[:, :w] + y[:, w:]


def times(a, b):
    return lax.dot_general(a, b, (((1,), (0,)), ((), ())), preferred_element_type=f32)


def centred_columns(w):
    return w - jnp.mean(w, axis=1, keepdims=True)


def inverse_spread(v):
    return lax.rsqrt(jnp.mean(v * v, axis=1, keepdims=True) + EPS)


def down(row):
    n = row.shape[1]
    parts = []
    for start in range(0, n, LANES):
        wide = jnp.broadcast_to(row[:, start : start + LANES], (LANES, LANES))
        parts.append(jnp.transpose(wide).astype(jnp.int16))
    return parts[0] if len(parts) == 1 else jnp.concatenate(parts, axis=0)


def picks(column, size):
    n = column.shape[0]
    lane = lax.broadcasted_iota(jnp.int32, (n, LANES), 1)
    one, zero = jnp.ones((n, LANES), half), jnp.zeros((n, LANES), half)
    parts = [
        jnp.where(column == (lane + start).astype(jnp.int16), one, zero)
        for start in range(0, size, LANES)
    ]
    return jnp.concatenate(parts, axis=1)


def members(row, size):
    n = row.shape[1]
    line = lax.broadcasted_iota(jnp.int32, (size, n), 0).astype(jnp.int16)
    entry = jnp.broadcast_to(row, (size, n)).astype(jnp.int16)
    return jnp.where(entry == line, jnp.ones((size, n), half), jnp.zeros((size, n), half))


def counts_of(pools, first, size):
    line = (lax.broadcasted_iota(jnp.int32, (size, LANES), 0) + first).astype(jnp.int16)
    one, zero = jnp.ones((size, LANES), half), jnp.zeros((size, LANES), half)
    total = zero
    for pool in pools:
        for r in range(pool.shape[0]):
            entry = jnp.broadcast_to(pool[r : r + 1, :], (size, LANES)).astype(jnp.int16)
            total = total + jnp.where(entry == line, one, zero)
    return times(total, jnp.ones((LANES, LANES), half))


def along_lanes(pool, first, lines):
    rows, n = pool.shape
    column = jnp.concatenate([down(pool[r : r + 1, :]) for r in range(rows)], axis=0)
    lane = (lax.broadcasted_iota(jnp.int32, (16, LANES), 1) + first).astype(jnp.int16)
    one, zero = jnp.ones((16, LANES), jnp.int16), jnp.zeros((16, LANES), jnp.int16)
    out = []
    for r in range(lines):
        name = lane + jnp.int16(r * LANES)
        hits = [jnp.where(column[i : i + 16, :] == name, one, zero) for i in range(0, rows * n, 16)]
        while len(hits) > 1:
            hits = [a + b for a, b in zip(hits[::2], hits[1::2])] + ([hits[-1]] if len(hits) % 2 else [])
        out.append(jnp.sum(hits[0].astype(jnp.int32).astype(f32), axis=0, keepdims=True))
    return jnp.concatenate(out, axis=0)


def first_part(degree, tile, wide, column, reach, before, extra):
    sources = wide.shape[0]
    operand = jnp.concatenate([picks(column(k), sources) for k in range(degree)], axis=0)
    sums = folded(times(operand, wide[...])).reshape(degree, tile, -1)
    for k in range(degree):
        before[k][...] = sums[k] + reach + extra[k]


def second_part(degree, tile, hidden, edge_sum, receivers, weights):
    message = folded(times(side(hidden), weights[0]))
    message = (message * inverse_spread(message)).reshape(degree, tile, -1)
    total = edge_sum
    for k in range(degree):
        total = total + message[k]
    node = jnp.concatenate([side(receivers), side(total)], axis=1)
    rhs_node = jnp.concatenate([weights[1], weights[2]], axis=0)
    node_hidden = jnp.maximum(folded(times(node, rhs_node)), 0.0)
    update = folded(times(side(node_hidden), weights[3]))
    return receivers + update * inverse_spread(update)


def pack_first(edge_in, weights):
    w = edge_in.shape[1]
    weights[0] = packed(edge_in[0:w])
    weights[1] = packed(edge_in[w : 2 * w])


def pack_second(edge_out, node_in, node_out, weights):
    w = edge_out.shape[1]
    weights[0] = packed(centred_columns(edge_out[...]))
    weights[1] = packed(node_in[0:w])
    weights[2] = packed(node_in[w : 2 * w])
    weights[3] = packed(centred_columns(node_out[...]))


def with_halo(degree, tile, rows, margin, beyond, column, before):
    chosen = [picks(column(k) - jnp.int16(rows), 2 * margin) for k in range(degree)]
    sums = folded(times(jnp.concatenate(chosen, axis=0), beyond[...])).reshape(degree, tile, -1)
    parts = [jnp.maximum(sums[k] + before[k][...], 0.0) for k in range(degree)]
    return jnp.concatenate(parts, axis=0)


def halo_sources(left, right, sender, beyond):
    margin = left.shape[0]
    beyond[:margin, :] = side(folded(times(side(left[...]), sender)))
    beyond[margin:, :] = side(folded(times(side(right[...]), sender)))


def rotated(target, flip, part):
    return jnp.where(target < part, target + flip * part, target - flip * part)


def gather_halo(lists, nodes, to_next, to_previous):
    both = side(nodes[...])
    for i, out in enumerate((to_next, to_previous)):
        out[...] = folded(times(picks(down(lists[i : i + 1, :]), nodes.shape[0]), both))


def start_kernel(lists, nodes, senders, pool, edge_in, edges, to_next, to_previous, kept_nodes, kept_senders, kept_pool, weights, *refs):
    slots, (kept_lists, kept_layer, arrived) = refs[:-3], refs[-3:]
    moves = [(lists, kept_lists), (nodes, kept_nodes), (edge_in.at[0], kept_layer), (senders, kept_senders), (pool, kept_pool)]
    moves += [(edges.at[k], slots[k]) for k in range(len(slots))]
    copies = [pltpu.make_async_copy(*move, arrived.at[i]) for i, move in enumerate(moves)]
    for copy in copies:
        copy.start()
    copies[0].wait()
    copies[1].wait()
    gather_halo(kept_lists, kept_nodes, to_next, to_previous)
    copies[2].wait()
    pack_first(kept_layer, weights)
    w = nodes.shape[1]
    weights[2] = packed(kept_layer[2 * w : 3 * w])
    for copy in copies[3:]:
        copy.wait()


def fine_first_kernel(ready, lines, flip, senders, nodes, pool, weights, edges, *refs):
    degree = edges.shape[0]
    here, refs = refs[:ready], refs[ready:]
    before, refs = refs[:degree], refs[degree:]
    edge_sum, counts, wide, local, arrived = refs
    rows, _ = nodes.shape
    copies = [pltpu.make_async_copy(edges.at[k], local.at[k - ready], arrived.at[k - ready]) for k in range(ready, degree)]
    for copy in copies:
        copy.start()
    wide[:rows, :] = side(folded(times(side(nodes[...]), weights[0])))
    wide[rows:, :] = weights[2]
    reach = folded(times(side(nodes[...]), weights[1]))
    part = lines * LANES
    height = counts.shape[0] // 2
    counts[...] = jnp.zeros_like(counts)
    counts[:lines, :] = along_lanes(pool, flip[0] * part, lines)
    counts[height : height + lines, :] = along_lanes(pool, (1 - flip[0]) * part, lines)
    for k in range(degree):
        if k == ready:
            for copy in copies:
                copy.wait()
        column = down(senders[k : k + 1, :])
        edge = here[k][...] if k < ready else local[k - ready]
        operand = jnp.concatenate([picks(column, rows), side(edge)], axis=1)
        before[k][...] = folded(times(operand, wide[...])) + reach
        edge_sum[...] = edge if k == 0 else edge_sum[...] + edge


def fine_second_kernel(flip, senders, pool, nodes, left, right, counts, *refs):
    degree = senders.shape[0]
    before, refs = refs[:degree], refs[degree:]
    edge_sum, edge_in, edge_out, node_in, node_out, new, keep, send, beyond, weights, held, sent = refs
    rows, w = nodes.shape
    margin = left.shape[0]
    halo_sources(left, right, packed(edge_in[0, 0:w]), beyond)
    pack_second(edge_out.at[0], node_in.at[0], node_out.at[0], weights)
    hidden = with_halo(degree, rows, rows, margin, beyond, lambda k: down(senders[k : k + 1, :]), before)
    held[...] = second_part(degree, rows, hidden, edge_sum[...], nodes[...], weights)
    copy = pltpu.make_async_copy(held, new, sent)
    copy.start()
    both = side(held[...])
    height = counts.shape[0] // 2
    part = keep.shape[0] - height
    target = jnp.concatenate([pool[j : j + 1, :] for j in range(pool.shape[0])], axis=1)
    target = rotated(target, flip[0], part)
    send[:part, :] = folded(times(members(target - part, part), both))
    keep[:part, :] = folded(times(members(target, part), both))
    keep[part:, :] = counts[:height, :]
    send[part:, :] = counts[height:, :]
    copy.wait()


def window_kernel(
    flip, quarter_pool, fine_pool, quarter_edges, coarse_senders, edge_in, edge_out, node_in, node_out, _,
    coarse_share, chosen, quarter_before, quarter_sum, coarse_columns,
    quarter_first, quarter_second, coarse_first, coarse_second,
):
    w = edge_in.shape[2]
    block = coarse_share.shape[0]
    share = 1.0 / counts_of([quarter_pool[...]], 0, block)
    coarse_share[...] = share

    degree, rows, _ = quarter_before.shape
    rhs = packed(edge_in[1, 2 * w : 3 * w])
    total = None
    for k in range(degree):
        edge = quarter_edges[pl.ds(k, rows, stride=degree), :]
        total = edge if total is None else total + edge
        quarter_before[k] = folded(times(side(edge), rhs))
    quarter_sum[...] = total
    pack_first(edge_in.at[1], quarter_first)
    pack_second(edge_out.at[1], node_in.at[1], node_out.at[1], quarter_second)
    pack_first(edge_in.at[2], coarse_first)
    coarse_first[2] = packed(edge_in[2, 2 * w : 3 * w])
    pack_second(edge_out.at[2], node_in.at[2], node_out.at[2], coarse_second)

    for k in range(coarse_columns.shape[0]):
        for start in range(0, block, LANES):
            coarse_columns[k, start : start + LANES, :] = down(coarse_senders[k : k + 1, start : start + LANES])

    parent = [down(quarter_pool[r : r + 1, :]) for r in range(quarter_pool.shape[0])]
    parent = side(jnp.concatenate(parent, axis=0).astype(jnp.int32).astype(f32))
    for r in range(fine_pool.shape[0]):
        rows = slice(r * LANES, (r + 1) * LANES)
        column = down(fine_pool[r : r + 1, :])
        named = folded(times(picks(column, parent.shape[0]), parent))
        chosen[rows, :] = picks(named.astype(jnp.int32).astype(jnp.int16), chosen.shape[1])


def mean_kernel(lines, mine, theirs, out):
    part = out.shape[0]
    counts = mine[part : part + lines, :] + theirs[part : part + lines, :]
    for r in range(lines):
        rows = slice(r * LANES, (r + 1) * LANES)
        share = 1.0 / jnp.transpose(jnp.broadcast_to(counts[r : r + 1, :], (LANES, LANES)))
        out[rows, :] = (mine[rows, :] + theirs[rows, :]) * share


def quarter_nodes_kernel(flip, mine, other, lists, nodes, to_next, to_previous):
    part = mine.shape[0]
    nodes[pl.ds(pl.multiple_of(flip[0] * part, part), part), :] = mine[...]
    nodes[pl.ds(pl.multiple_of((1 - flip[0]) * part, part), part), :] = other[...]
    gather_halo(lists, nodes, to_next, to_previous)


def quarter_first_kernel(tile, senders, nodes, extra, weights, before, wide):
    degree, rows, _ = before.shape
    wide[...] = side(folded(times(side(nodes[...]), weights[0])))
    for t in range(rows // tile):
        span = slice(t * tile, (t + 1) * tile)
        reach = folded(times(side(nodes[span, :]), weights[1]))
        first_part(
            degree, tile, wide, lambda k: down(senders[k : k + 1, span]), reach,
            [before.at[k, span, :] for k in range(degree)], extra.at[:, span, :],
        )


def quarter_second_kernel(
    flip, senders, pool, nodes, left, right, before, edge_sum, share, first_weights, weights, new, own, partner, beyond,
):
    degree, rows, _ = before.shape
    margin = left.shape[0]
    halo_sources(left, right, first_weights[0], beyond)
    hidden = with_halo(
        degree, rows, rows, margin, beyond, lambda k: down(senders[k : k + 1, :]),
        [before.at[k] for k in range(degree)],
    )
    updated = second_part(degree, rows, hidden, edge_sum[...], nodes[...], weights)
    new[...] = updated
    part = own.shape[0]
    target = jnp.concatenate([pool[j : j + 1, :] for j in range(pool.shape[0])], axis=1)
    target = rotated(target, flip[0], part)
    split = side(updated)
    first = pl.multiple_of(flip[0] * part, part)
    second = pl.multiple_of((1 - flip[0]) * part, part)
    own[...] = folded(times(members(target, part), split)) * share[pl.ds(first, part), :]
    partner[...] = folded(times(members(target - part, part), split)) * share[pl.ds(second, part), :]


def base_kernel(pool, quarter, fine_new, out):
    both = side(quarter[...])
    column = jnp.concatenate([down(pool[r : r + 1, :]) for r in range(pool.shape[0])], axis=0)
    out[...] = fine_new[...] + folded(times(picks(column, both.shape[0]), both))


def coarse_kernel(n_patch, tile, place, *refs):
    mine, refs = refs[:n_patch], refs[n_patch:]
    other, refs = refs[:n_patch], refs[n_patch:]
    (columns, chosen, base, first_weights, weights), refs = refs[:5], refs[5:]
    pieces, (out, nodes, edges, wide, new, held, sent) = refs[:-7], refs[-7:]
    part, w = mine[0].shape
    block = 2 * part
    piece = pieces[0].shape[0]
    degree = columns.shape[0]
    sources = nodes.shape[0]
    for j, source in enumerate(pieces):
        at = jnp.bitwise_xor(place[2], j)
        edges[pl.ds(pl.multiple_of(at * piece, piece), piece), :] = source[...]
    for j in range(n_patch):
        at = lax.rem(place[0] + j, n_patch) * block
        nodes[pl.ds(pl.multiple_of(at + place[1] * part, part), part), :] = mine[j][...]
        nodes[pl.ds(pl.multiple_of(at + (1 - place[1]) * part, part), part), :] = other[j][...]
    wide[:sources, :] = side(folded(times(side(nodes[...]), first_weights[0])))
    wide[sources:, :] = first_weights[2]
    for t in range(block // tile):
        span = slice(t * tile, (t + 1) * tile)
        receivers = nodes[pl.ds(pl.multiple_of(place[0] * block + t * tile, tile), tile), :]
        reach = folded(times(side(receivers), first_weights[1]))
        edge = [edges[pl.ds(t * tile * degree + k, tile, stride=degree), :] for k in range(degree)]
        operand = [jnp.concatenate([picks(columns[k, span, :], sources), side(edge[k])], axis=1) for k in range(degree)]
        sums = folded(times(jnp.concatenate(operand, axis=0), wide[...])).reshape(degree, tile, w)
        hidden = jnp.maximum(sums + reach[None], 0.0).reshape(degree * tile, w)
        total = edge[0]
        for k in range(1, degree):
            total = total + edge[k]
        new[span, :] = second_part(degree, tile, hidden, total, receivers, weights)
    both = side(new[...])
    steps = sent.shape[0]
    rows = out.shape[0] // steps
    copies = []
    for i in range(steps):
        span = slice(i * rows, (i + 1) * rows)
        held[span, :] = base[span, :] + folded(times(chosen[span, :], both))
        copies.append(pltpu.make_async_copy(held.at[span, :], out.at[span, :], sent.at[i]))
        copies[-1].start()
    for copy in copies:
        copy.wait()


def whole(*shape):
    return pl.BlockSpec(shape, lambda *_: (0,) * len(shape))


def shaped(*shape, dtype=f32):
    return jax.ShapeDtypeStruct(shape, dtype)


def run(kernel, grid, scalars, in_specs, operands, outs, out_specs, scratch, mega, flops):
    return pl.pallas_call(
        kernel,
        out_shape=outs,
        grid_spec=pltpu.PrefetchScalarGridSpec(
            num_scalar_prefetch=len(scalars), grid=grid, in_specs=in_specs, out_specs=out_specs,
            scratch_shapes=scratch,
        ),
        compiler_params=pltpu.CompilerParams(vmem_limit_bytes=mega * 1024 * 1024),
        cost_estimate=pl.CostEstimate(flops=flops, bytes_accessed=10**6, transcendentals=0),
    )(*scalars, *operands)


def passed(value, axis, steps):
    count = lax.axis_size(axis)
    return lax.ppermute(value, axis, [(s, (s + steps) % count) for s in range(count)])


def swapped(value, axis, bit):
    count = lax.axis_size(axis)
    return lax.ppermute(value, axis, [(s, s ^ bit) for s in range(count)])


def on_device(
    fine_nodes, fine_edges, fine_senders, fine_halo, fine_pool, quarter_edges, quarter_senders,
    quarter_halo, quarter_pool, coarse_edges, coarse_senders, edge_in, edge_out, node_in, node_out,
):
    n_sub, n_patch = lax.axis_size("sub"), lax.axis_size("patch")
    sub, patch = lax.axis_index("sub").astype(jnp.int32), lax.axis_index("patch").astype(jnp.int32)
    rows, degree, w = fine_edges.shape
    q_rows, q_degree, _ = quarter_edges.shape
    margin, q_margin = fine_halo.shape[1], quarter_halo.shape[1]
    piece, c_degree, _ = coarse_edges.shape
    total = coarse_senders.shape[0]
    block = total // n_patch
    part, c_part = q_rows // 2, block // 2
    tile = min(512, q_rows)
    c_tile = min(256, block)
    lines = part // LANES
    height = -(-lines // 8) * 8
    core = sub % 2
    flip = core.reshape(1)
    patch_core = jnp.stack([patch, core])
    layers = (edge_in, edge_out, node_in, node_out)
    layer_specs = [whole(*x.shape) for x in layers]
    in_hbm, in_vmem = pl.BlockSpec(memory_space=pl.ANY), pl.BlockSpec(memory_space=pltpu.VMEM)
    pool_rows = fine_pool.reshape(rows // LANES, LANES)
    quarter_pool_rows = quarter_pool.reshape(q_rows // LANES, LANES)
    fine_senders, quarter_senders, coarse_senders = fine_senders.T, quarter_senders.T, coarse_senders.T
    own_edges = coarse_edges.reshape(piece * c_degree, w)
    hbm = lambda x: pltpu.with_memory_space_constraint(x, pltpu.HBM)
    mats = lambda n: (n, 2 * w, 2 * w)
    short = jnp.int16
    big = 16 if total <= 2048 else 48

    ready = min(2, degree - 1)
    edges = hbm(fine_edges.transpose(1, 0, 2))
    to_next, to_previous, nodes, senders, pool, fine_weights, *here = run(
        start_kernel, (1,), (), [in_hbm] * 6,
        (hbm(fine_halo), hbm(fine_nodes), hbm(fine_senders), hbm(pool_rows), hbm(edge_in), edges),
        (
            shaped(margin, w), shaped(margin, w), shaped(rows, w), shaped(degree, rows, dtype=jnp.int32),
            shaped(*pool_rows.shape, dtype=jnp.int32), shaped(*mats(3), dtype=half), *(shaped(rows, w),) * ready,
        ),
        [
            whole(margin, w), whole(margin, w), in_vmem, in_vmem, in_vmem, whole(*mats(3)), *[in_vmem] * ready,
        ],
        [pltpu.VMEM((2, margin), jnp.int32), pltpu.VMEM((3 * w, w), f32), pltpu.SemaphoreType.DMA((ready + 5,))],
        8, 10**8,
    )
    left = passed(to_next, ("patch", "sub"), 1)
    right = passed(to_previous, ("patch", "sub"), -1)
    firsts = run(
        functools.partial(fine_first_kernel, ready, lines), (1,), (flip,),
        [whole(degree, rows), whole(rows, w), whole(*pool_rows.shape), whole(*mats(3)), in_hbm, *[whole(rows, w)] * ready],
        (senders, nodes, pool, fine_weights, edges, *here),
        (*(shaped(rows, w),) * (degree + 1), shaped(2 * height, w)),
        [whole(rows, w)] * (degree + 1) + [whole(2 * height, w)],
        [
            pltpu.VMEM((rows + 2 * w, 2 * w), half),
            pltpu.VMEM((degree - ready, rows, w), f32), pltpu.SemaphoreType.DMA((degree - ready,)),
        ],
        30, 8 * 10**9,
    )
    *before, edge_sum, counts = firsts
    fine_new, keep, send = run(
        fine_second_kernel, (1,), (flip,),
        [
            whole(degree, rows), whole(*pool_rows.shape), whole(rows, w), whole(margin, w), whole(margin, w),
            whole(2 * height, w), *[whole(rows, w)] * (degree + 1), *layer_specs,
        ],
        (fine_senders, pool_rows, fine_nodes, left, right, counts, *before, edge_sum, *layers),
        (pltpu.HBM((rows, w), f32), shaped(part + height, w), shaped(part + height, w)),
        [in_hbm, whole(part + height, w), whole(part + height, w)],
        [
            pltpu.VMEM((2 * margin, 2 * w), half), pltpu.VMEM(mats(4), half), pltpu.VMEM((rows, w), f32),
            pltpu.SemaphoreType.DMA,
        ],
        30, 4 * 10**9,
    )

    mine, theirs = keep, swapped(send, "sub", 1)
    bit = 2
    after = theirs
    while bit < n_sub:
        mine = mine + theirs
        theirs = swapped(mine, "sub", bit)
        after = mine if bit == 2 else after
        bit *= 2
    (coarse_share, chosen, quarter_before, quarter_sum, coarse_columns,
     quarter_weights, quarter_later, coarse_weights, coarse_later) = run(
        window_kernel, (1,), (patch_core,),
        [
            whole(*quarter_pool_rows.shape), whole(*pool_rows.shape),
            whole(q_rows * q_degree, w),
            pl.BlockSpec((c_degree, block), lambda i, place: (0, place[0])), *layer_specs, in_hbm,
        ],
        (quarter_pool_rows, pool_rows, quarter_edges.reshape(q_rows * q_degree, w), coarse_senders,
         *layers, after),
        (
            shaped(block, w), shaped(rows, block, dtype=half), shaped(q_degree, q_rows, w), shaped(q_rows, w),
            shaped(c_degree, block, w, dtype=short), shaped(*mats(2), dtype=half), shaped(*mats(4), dtype=half),
            shaped(*mats(3), dtype=half), shaped(*mats(4), dtype=half),
        ),
        [
            whole(block, w), whole(rows, block), whole(q_degree, q_rows, w), whole(q_rows, w),
            whole(c_degree, block, w), whole(*mats(2)), whole(*mats(4)), whole(*mats(3)),
            whole(*mats(4)),
        ],
        [], 16, 10**9,
    )
    mine = run(
        functools.partial(mean_kernel, lines), (1,), (), [whole(part + height, w)] * 2, (mine, theirs),
        shaped(part, w), whole(part, w), [], 6, 10**7,
    )
    other = swapped(mine, "sub", 1)

    quarter_nodes, to_next, to_previous = run(
        quarter_nodes_kernel, (1,), (flip,), [whole(part, w), whole(part, w), whole(2, q_margin)],
        (mine, other, quarter_halo), (shaped(q_rows, w), shaped(q_margin, w), shaped(q_margin, w)),
        [whole(q_rows, w), whole(q_margin, w), whole(q_margin, w)], [], 8, 10**8,
    )
    left = passed(to_next, "patch", 1)
    right = passed(to_previous, "patch", -1)
    across = [own_edges]
    bit = 2
    while bit < n_sub:
        across += [swapped(value, "sub", bit) for value in across]
        bit *= 2
    edge_pieces = []
    for value in across:
        edge_pieces += [value, swapped(value, "sub", 1)]
    quarter_first = run(
        functools.partial(quarter_first_kernel, tile), (1,), (),
        [whole(q_degree, q_rows), whole(q_rows, w), whole(q_degree, q_rows, w), whole(*mats(2))],
        (quarter_senders, quarter_nodes, quarter_before, quarter_weights),
        shaped(q_degree, q_rows, w), whole(q_degree, q_rows, w), [pltpu.VMEM((q_rows, 2 * w), half)], 20, 3 * 10**9,
    )
    quarter_new, own, own_partner = run(
        quarter_second_kernel, (1,), (flip,),
        [
            whole(q_degree, q_rows), whole(*quarter_pool_rows.shape), whole(q_rows, w), whole(q_margin, w),
            whole(q_margin, w), whole(q_degree, q_rows, w), whole(q_rows, w), whole(block, w), whole(*mats(2)),
            whole(*mats(4)),
        ],
        (quarter_senders, quarter_pool_rows, quarter_nodes, left, right, quarter_first, quarter_sum, coarse_share,
         quarter_weights, quarter_later),
        (shaped(q_rows, w), shaped(c_part, w), shaped(c_part, w)),
        [whole(q_rows, w), whole(c_part, w), whole(c_part, w)],
        [pltpu.VMEM((2 * q_margin, 2 * w), half)], 20, 2 * 10**9,
    )

    pieces = [own] + [passed(own, "patch", -j) for j in range(1, n_patch)]
    partner = [own_partner] + [swapped(pieces[j], "sub", 1) for j in range(1, n_patch)]
    base = run(
        base_kernel, (1,), (), [whole(*pool_rows.shape), whole(q_rows, w), whole(rows, w)],
        (pool_rows, quarter_new, hbm(fine_new)), shaped(rows, w), whole(rows, w), [], 16, 10**9,
    )
    return run(
        functools.partial(coarse_kernel, n_patch, c_tile), (1,), (jnp.stack([patch, core, sub]),),
        [
            *[whole(c_part, w)] * (2 * n_patch), whole(c_degree, block, w), whole(rows, block), whole(rows, w),
            whole(*mats(3)), whole(*mats(4)), *[whole(*own_edges.shape)] * n_sub,
        ],
        (*pieces, *partner, coarse_columns, chosen, base, coarse_weights, coarse_later, *edge_pieces),
        shaped(rows, w), in_hbm,
        [
            pltpu.VMEM((total, w), f32), pltpu.VMEM((block * c_degree, w), f32),
            pltpu.VMEM((total + 2 * w, 2 * w), half), pltpu.VMEM((block, w), f32), pltpu.VMEM((rows, w), f32),
            pltpu.SemaphoreType.DMA((4,)),
        ],
        big, 2 * 10**9,
    )


def solution(mesh):
    split = P(("groups", "patch", "sub"))
    patches = P(("groups", "patch"))
    return jax.shard_map(
        on_device,
        mesh=mesh,
        in_specs=(
            split, split, split, split, split, patches, patches, patches, patches, split, P("groups"),
            P(), P(), P(), P(),
        ),
        out_specs=split,
        check_vma=False,
    )
```

```python
import functools

import jax
import jax.numpy as jnp
from jax import lax
from jax.experimental import pallas as pl
from jax.experimental.pallas import tpu as pltpu
from jax.sharding import PartitionSpec as P


f32 = jnp.float32
half = jnp.bfloat16
LANES = 128
EPS = 1e-05


def side(x):
    high = x.astype(half)
    low = (x - high.astype(f32)).astype(half)
    return jnp.concatenate([high, low], axis=1)


def packed(w):
    row = side(w)
    return jnp.concatenate([row, row], axis=0)


def folded(y):
    w = y.shape[1] // 2
    return y[:, :w] + y[:, w:]


def times(a, b):
    return lax.dot_general(a, b, (((1,), (0,)), ((), ())), preferred_element_type=f32)


def centred_columns(w):
    return w - jnp.mean(w, axis=1, keepdims=True)


def inverse_spread(v):
    return lax.rsqrt(jnp.mean(v * v, axis=1, keepdims=True) + EPS)


def down(row):
    n = row.shape[1]
    parts = []
    for start in range(0, n, LANES):
        wide = jnp.broadcast_to(row[:, start : start + LANES], (LANES, LANES))
        parts.append(jnp.transpose(wide).astype(jnp.int16))
    return parts[0] if len(parts) == 1 else jnp.concatenate(parts, axis=0)


def picks(column, size):
    n = column.shape[0]
    lane = lax.broadcasted_iota(jnp.int32, (n, LANES), 1)
    one, zero = jnp.ones((n, LANES), half), jnp.zeros((n, LANES), half)
    parts = [
        jnp.where(column == (lane + start).astype(jnp.int16), one, zero)
        for start in range(0, size, LANES)
    ]
    return jnp.concatenate(parts, axis=1)


def members(row, size):
    n = row.shape[1]
    line = lax.broadcasted_iota(jnp.int32, (size, n), 0).astype(jnp.int16)
    entry = jnp.broadcast_to(row, (size, n)).astype(jnp.int16)
    return jnp.where(entry == line, jnp.ones((size, n), half), jnp.zeros((size, n), half))


def counts_of(pools, first, size):
    line = (lax.broadcasted_iota(jnp.int32, (size, LANES), 0) + first).astype(jnp.int16)
    one, zero = jnp.ones((size, LANES), half), jnp.zeros((size, LANES), half)
    total = zero
    for pool in pools:
        for r in range(pool.shape[0]):
            entry = jnp.broadcast_to(pool[r : r + 1, :], (size, LANES)).astype(jnp.int16)
            total = total + jnp.where(entry == line, one, zero)
    return times(total, jnp.ones((LANES, LANES), half))


def along_lanes(pool, first, lines):
    rows, n = pool.shape
    column = jnp.concatenate([down(pool[r : r + 1, :]) for r in range(rows)], axis=0)
    lane = (lax.broadcasted_iota(jnp.int32, (16, LANES), 1) + first).astype(jnp.int16)
    one, zero = jnp.ones((16, LANES), jnp.int16), jnp.zeros((16, LANES), jnp.int16)
    out = []
    for r in range(lines):
        name = lane + jnp.int16(r * LANES)
        hits = [jnp.where(column[i : i + 16, :] == name, one, zero) for i in range(0, rows * n, 16)]
        while len(hits) > 1:
            hits = [a + b for a, b in zip(hits[::2], hits[1::2])] + ([hits[-1]] if len(hits) % 2 else [])
        out.append(jnp.sum(hits[0].astype(jnp.int32).astype(f32), axis=0, keepdims=True))
    return jnp.concatenate(out, axis=0)


def first_part(degree, tile, wide, column, reach, before, extra):
    sources = wide.shape[0]
    operand = jnp.concatenate([picks(column(k), sources) for k in range(degree)], axis=0)
    sums = folded(times(operand, wide[...])).reshape(degree, tile, -1)
    for k in range(degree):
        before[k][...] = sums[k] + reach + extra[k]


def second_part(degree, tile, hidden, edge_sum, receivers, weights):
    message = folded(times(side(hidden), weights[0]))
    message = (message * inverse_spread(message)).reshape(degree, tile, -1)
    total = edge_sum
    for k in range(degree):
        total = total + message[k]
    node = jnp.concatenate([side(receivers), side(total)], axis=1)
    rhs_node = jnp.concatenate([weights[1], weights[2]], axis=0)
    node_hidden = jnp.maximum(folded(times(node, rhs_node)), 0.0)
    update = folded(times(side(node_hidden), weights[3]))
    return receivers + update * inverse_spread(update)


def pack_first(edge_in, weights):
    w = edge_in.shape[1]
    weights[0] = packed(edge_in[0:w])
    weights[1] = packed(edge_in[w : 2 * w])


def pack_second(edge_out, node_in, node_out, weights):
    w = edge_out.shape[1]
    weights[0] = packed(centred_columns(edge_out[...]))
    weights[1] = packed(node_in[0:w])
    weights[2] = packed(node_in[w : 2 * w])
    weights[3] = packed(centred_columns(node_out[...]))


def with_halo(degree, tile, rows, margin, beyond, column, before):
    chosen = [picks(column(k) - jnp.int16(rows), 2 * margin) for k in range(degree)]
    sums = folded(times(jnp.concatenate(chosen, axis=0), beyond[...])).reshape(degree, tile, -1)
    parts = [jnp.maximum(sums[k] + before[k][...], 0.0) for k in range(degree)]
    return jnp.concatenate(parts, axis=0)


def halo_sources(left, right, sender, beyond):
    margin = left.shape[0]
    beyond[:margin, :] = side(folded(times(side(left[...]), sender)))
    beyond[margin:, :] = side(folded(times(side(right[...]), sender)))


def rotated(target, flip, part):
    return jnp.where(target < part, target + flip * part, target - flip * part)


def gather_halo(lists, nodes, to_next, to_previous):
    both = side(nodes[...])
    for i, out in enumerate((to_next, to_previous)):
        out[...] = folded(times(picks(down(lists[i : i + 1, :]), nodes.shape[0]), both))


def start_kernel(lists, nodes, senders, pool, edge_in, edges, to_next, to_previous, kept_nodes, kept_senders, kept_pool, weights, *refs):
    slots, (kept_lists, kept_layer, arrived) = refs[:-3], refs[-3:]
    moves = [(lists, kept_lists), (nodes, kept_nodes), (edge_in.at[0], kept_layer), (senders, kept_senders), (pool, kept_pool)]
    moves += [(edges.at[k], slots[k]) for k in range(len(slots))]
    copies = [pltpu.make_async_copy(*move, arrived.at[i]) for i, move in enumerate(moves)]
    for copy in copies:
        copy.start()
    copies[0].wait()
    copies[1].wait()
    gather_halo(kept_lists, kept_nodes, to_next, to_previous)
    copies[2].wait()
    pack_first(kept_layer, weights)
    w = nodes.shape[1]
    weights[2] = packed(kept_layer[2 * w : 3 * w])
    for copy in copies[3:]:
        copy.wait()


def fine_first_kernel(ready, lines, flip, senders, nodes, pool, weights, edges, *refs):
    degree = edges.shape[0]
    here, refs = refs[:ready], refs[ready:]
    before, refs = refs[:degree], refs[degree:]
    edge_sum, counts, wide, local, arrived = refs
    rows, _ = nodes.shape
    copies = [pltpu.make_async_copy(edges.at[k], local.at[k - ready], arrived.at[k - ready]) for k in range(ready, degree)]
    for copy in copies:
        copy.start()
    wide[:rows, :] = side(folded(times(side(nodes[...]), weights[0])))
    wide[rows:, :] = weights[2]
    reach = folded(times(side(nodes[...]), weights[1]))
    part = lines * LANES
    height = counts.shape[0] // 2
    counts[...] = jnp.zeros_like(counts)
    counts[:lines, :] = along_lanes(pool, flip[0] * part, lines)
    counts[height : height + lines, :] = along_lanes(pool, (1 - flip[0]) * part, lines)
    for k in range(degree):
        if k == ready:
            for copy in copies:
                copy.wait()
        column = down(senders[k : k + 1, :])
        edge = here[k][...] if k < ready else local[k - ready]
        operand = jnp.concatenate([picks(column, rows), side(edge)], axis=1)
        before[k][...] = folded(times(operand, wide[...])) + reach
        edge_sum[...] = edge if k == 0 else edge_sum[...] + edge


def fine_second_kernel(flip, senders, pool, nodes, left, right, counts, *refs):
    degree = senders.shape[0]
    before, refs = refs[:degree], refs[degree:]
    edge_sum, edge_in, edge_out, node_in, node_out, new, keep, send, beyond, weights, held, sent = refs
    rows, w = nodes.shape
    margin = left.shape[0]
    halo_sources(left, right, packed(edge_in[0, 0:w]), beyond)
    pack_second(edge_out.at[0], node_in.at[0], node_out.at[0], weights)
    hidden = with_halo(degree, rows, rows, margin, beyond, lambda k: down(senders[k : k + 1, :]), before)
    held[...] = second_part(degree, rows, hidden, edge_sum[...], nodes[...], weights)
    copy = pltpu.make_async_copy(held, new, sent)
    copy.start()
    both = side(held[...])
    height = counts.shape[0] // 2
    part = keep.shape[0] - height
    target = jnp.concatenate([pool[j : j + 1, :] for j in range(pool.shape[0])], axis=1)
    target = rotated(target, flip[0], part)
    send[:part, :] = folded(times(members(target - part, part), both))
    keep[:part, :] = folded(times(members(target, part), both))
    keep[part:, :] = counts[:height, :]
    send[part:, :] = counts[height:, :]
    copy.wait()


def window_kernel(
    flip, quarter_pool, fine_pool, quarter_edges, coarse_senders, edge_in, edge_out, node_in, node_out, _,
    coarse_share, chosen, quarter_before, quarter_sum, coarse_columns,
    quarter_first, quarter_second, coarse_first, coarse_second,
):
    w = edge_in.shape[2]
    block = coarse_share.shape[0]
    share = 1.0 / counts_of([quarter_pool[...]], 0, block)
    coarse_share[...] = share

    degree, rows, _ = quarter_before.shape
    rhs = packed(edge_in[1, 2 * w : 3 * w])
    total = None
    for k in range(degree):
        edge = quarter_edges[pl.ds(k, rows, stride=degree), :]
        total = edge if total is None else total + edge
        quarter_before[k] = folded(times(side(edge), rhs))
    quarter_sum[...] = total
    pack_first(edge_in.at[1], quarter_first)
    pack_second(edge_out.at[1], node_in.at[1], node_out.at[1], quarter_second)
    pack_first(edge_in.at[2], coarse_first)
    coarse_first[2] = packed(edge_in[2, 2 * w : 3 * w])
    pack_second(edge_out.at[2], node_in.at[2], node_out.at[2], coarse_second)

    for k in range(coarse_columns.shape[0]):
        for start in range(0, block, LANES):
            coarse_columns[k, start : start + LANES, :] = down(coarse_senders[k : k + 1, start : start + LANES])

    parent = [down(quarter_pool[r : r + 1, :]) for r in range(quarter_pool.shape[0])]
    parent = side(jnp.concatenate(parent, axis=0).astype(jnp.int32).astype(f32))
    for r in range(fine_pool.shape[0]):
        rows = slice(r * LANES, (r + 1) * LANES)
        column = down(fine_pool[r : r + 1, :])
        named = folded(times(picks(column, parent.shape[0]), parent))
        chosen[rows, :] = picks(named.astype(jnp.int32).astype(jnp.int16), chosen.shape[1])


def mean_kernel(lines, total, out):
    part = out.shape[0]
    counts = total[part : part + lines, :]
    for r in range(lines):
        rows = slice(r * LANES, (r + 1) * LANES)
        share = 1.0 / jnp.transpose(jnp.broadcast_to(counts[r : r + 1, :], (LANES, LANES)))
        out[rows, :] = total[rows, :] * share


def quarter_nodes_kernel(flip, mine, other, lists, nodes, to_next, to_previous):
    part = mine.shape[0]
    nodes[pl.ds(pl.multiple_of(flip[0] * part, part), part), :] = mine[...]
    nodes[pl.ds(pl.multiple_of((1 - flip[0]) * part, part), part), :] = other[...]
    gather_halo(lists, nodes, to_next, to_previous)


def quarter_first_kernel(tile, senders, nodes, extra, weights, before, wide):
    degree, rows, _ = before.shape
    wide[...] = side(folded(times(side(nodes[...]), weights[0])))
    for t in range(rows // tile):
        span = slice(t * tile, (t + 1) * tile)
        reach = folded(times(side(nodes[span, :]), weights[1]))
        first_part(
            degree, tile, wide, lambda k: down(senders[k : k + 1, span]), reach,
            [before.at[k, span, :] for k in range(degree)], extra.at[:, span, :],
        )


def quarter_second_kernel(
    flip, senders, pool, nodes, left, right, before, edge_sum, share, first_weights, weights, new, own, partner, beyond,
):
    degree, rows, _ = before.shape
    margin = left.shape[0]
    halo_sources(left, right, first_weights[0], beyond)
    hidden = with_halo(
        degree, rows, rows, margin, beyond, lambda k: down(senders[k : k + 1, :]),
        [before.at[k] for k in range(degree)],
    )
    updated = second_part(degree, rows, hidden, edge_sum[...], nodes[...], weights)
    new[...] = updated
    part = own.shape[0]
    target = jnp.concatenate([pool[j : j + 1, :] for j in range(pool.shape[0])], axis=1)
    target = rotated(target, flip[0], part)
    split = side(updated)
    first = pl.multiple_of(flip[0] * part, part)
    second = pl.multiple_of((1 - flip[0]) * part, part)
    own[...] = folded(times(members(target, part), split)) * share[pl.ds(first, part), :]
    partner[...] = folded(times(members(target - part, part), split)) * share[pl.ds(second, part), :]


def base_kernel(pool, quarter, fine_new, out):
    both = side(quarter[...])
    column = jnp.concatenate([down(pool[r : r + 1, :]) for r in range(pool.shape[0])], axis=0)
    out[...] = fine_new[...] + folded(times(picks(column, both.shape[0]), both))


def coarse_kernel(n_patch, tile, place, *refs):
    mine, refs = refs[:n_patch], refs[n_patch:]
    other, refs = refs[:n_patch], refs[n_patch:]
    (columns, chosen, base, first_weights, weights), refs = refs[:5], refs[5:]
    pieces, (out, nodes, edges, wide, new, held, sent) = refs[:-7], refs[-7:]
    part, w = mine[0].shape
    block = 2 * part
    piece = pieces[0].shape[0]
    degree = columns.shape[0]
    sources = nodes.shape[0]
    for j, source in enumerate(pieces):
        at = jnp.bitwise_xor(place[2], j)
        edges[pl.ds(pl.multiple_of(at * piece, piece), piece), :] = source[...]
    for j in range(n_patch):
        at = lax.rem(place[0] + j, n_patch) * block
        nodes[pl.ds(pl.multiple_of(at + place[1] * part, part), part), :] = mine[j][...]
        nodes[pl.ds(pl.multiple_of(at + (1 - place[1]) * part, part), part), :] = other[j][...]
    wide[:sources, :] = side(folded(times(side(nodes[...]), first_weights[0])))
    wide[sources:, :] = first_weights[2]
    for t in range(block // tile):
        span = slice(t * tile, (t + 1) * tile)
        receivers = nodes[pl.ds(pl.multiple_of(place[0] * block + t * tile, tile), tile), :]
        reach = folded(times(side(receivers), first_weights[1]))
        edge = [edges[pl.ds(t * tile * degree + k, tile, stride=degree), :] for k in range(degree)]
        operand = [jnp.concatenate([picks(columns[k, span, :], sources), side(edge[k])], axis=1) for k in range(degree)]
        sums = folded(times(jnp.concatenate(operand, axis=0), wide[...])).reshape(degree, tile, w)
        hidden = jnp.maximum(sums + reach[None], 0.0).reshape(degree * tile, w)
        total = edge[0]
        for k in range(1, degree):
            total = total + edge[k]
        new[span, :] = second_part(degree, tile, hidden, total, receivers, weights)
    both = side(new[...])
    steps = sent.shape[0]
    rows = out.shape[0] // steps
    copies = []
    for i in range(steps):
        span = slice(i * rows, (i + 1) * rows)
        held[span, :] = base[span, :] + folded(times(chosen[span, :], both))
        copies.append(pltpu.make_async_copy(held.at[span, :], out.at[span, :], sent.at[i]))
        copies[-1].start()
    for copy in copies:
        copy.wait()


def whole(*shape):
    return pl.BlockSpec(shape, lambda *_: (0,) * len(shape))


def shaped(*shape, dtype=f32):
    return jax.ShapeDtypeStruct(shape, dtype)


def run(kernel, grid, scalars, in_specs, operands, outs, out_specs, scratch, mega, flops):
    return pl.pallas_call(
        kernel,
        out_shape=outs,
        grid_spec=pltpu.PrefetchScalarGridSpec(
            num_scalar_prefetch=len(scalars), grid=grid, in_specs=in_specs, out_specs=out_specs,
            scratch_shapes=scratch,
        ),
        compiler_params=pltpu.CompilerParams(vmem_limit_bytes=mega * 1024 * 1024),
        cost_estimate=pl.CostEstimate(flops=flops, bytes_accessed=10**6, transcendentals=0),
    )(*scalars, *operands)


def passed(value, axis, steps):
    count = lax.axis_size(axis)
    return lax.ppermute(value, axis, [(s, (s + steps) % count) for s in range(count)])


def swapped(value, axis, bit):
    count = lax.axis_size(axis)
    return lax.ppermute(value, axis, [(s, s ^ bit) for s in range(count)])


def on_device(
    fine_nodes, fine_edges, fine_senders, fine_halo, fine_pool, quarter_edges, quarter_senders,
    quarter_halo, quarter_pool, coarse_edges, coarse_senders, edge_in, edge_out, node_in, node_out,
):
    n_sub, n_patch = lax.axis_size("sub"), lax.axis_size("patch")
    sub, patch = lax.axis_index("sub").astype(jnp.int32), lax.axis_index("patch").astype(jnp.int32)
    rows, degree, w = fine_edges.shape
    q_rows, q_degree, _ = quarter_edges.shape
    margin, q_margin = fine_halo.shape[1], quarter_halo.shape[1]
    piece, c_degree, _ = coarse_edges.shape
    total = coarse_senders.shape[0]
    block = total // n_patch
    part, c_part = q_rows // 2, block // 2
    tile = min(512, q_rows)
    c_tile = min(256, block)
    lines = part // LANES
    height = -(-lines // 8) * 8
    core = sub % 2
    flip = core.reshape(1)
    patch_core = jnp.stack([patch, core])
    layers = (edge_in, edge_out, node_in, node_out)
    layer_specs = [whole(*x.shape) for x in layers]
    in_hbm, in_vmem = pl.BlockSpec(memory_space=pl.ANY), pl.BlockSpec(memory_space=pltpu.VMEM)
    pool_rows = fine_pool.reshape(rows // LANES, LANES)
    quarter_pool_rows = quarter_pool.reshape(q_rows // LANES, LANES)
    fine_senders, quarter_senders, coarse_senders = fine_senders.T, quarter_senders.T, coarse_senders.T
    own_edges = coarse_edges.reshape(piece * c_degree, w)
    hbm = lambda x: pltpu.with_memory_space_constraint(x, pltpu.HBM)
    mats = lambda n: (n, 2 * w, 2 * w)
    short = jnp.int16
    big = 16 if total <= 2048 else 48

    ready = min(2, degree - 1)
    edges = hbm(fine_edges.transpose(1, 0, 2))
    to_next, to_previous, nodes, senders, pool, fine_weights, *here = run(
        start_kernel, (1,), (), [in_hbm] * 6,
        (hbm(fine_halo), hbm(fine_nodes), hbm(fine_senders), hbm(pool_rows), hbm(edge_in), edges),
        (
            shaped(margin, w), shaped(margin, w), shaped(rows, w), shaped(degree, rows, dtype=jnp.int32),
            shaped(*pool_rows.shape, dtype=jnp.int32), shaped(*mats(3), dtype=half), *(shaped(rows, w),) * ready,
        ),
        [
            whole(margin, w), whole(margin, w), in_vmem, in_vmem, in_vmem, whole(*mats(3)), *[in_vmem] * ready,
        ],
        [pltpu.VMEM((2, margin), jnp.int32), pltpu.VMEM((3 * w, w), f32), pltpu.SemaphoreType.DMA((ready + 5,))],
        8, 10**8,
    )
    left = passed(to_next, ("patch", "sub"), 1)
    right = passed(to_previous, ("patch", "sub"), -1)
    firsts = run(
        functools.partial(fine_first_kernel, ready, lines), (1,), (flip,),
        [whole(degree, rows), whole(rows, w), whole(*pool_rows.shape), whole(*mats(3)), in_hbm, *[whole(rows, w)] * ready],
        (senders, nodes, pool, fine_weights, edges, *here),
        (*(shaped(rows, w),) * (degree + 1), shaped(2 * height, w)),
        [whole(rows, w)] * (degree + 1) + [whole(2 * height, w)],
        [
            pltpu.VMEM((rows + 2 * w, 2 * w), half),
            pltpu.VMEM((degree - ready, rows, w), f32), pltpu.SemaphoreType.DMA((degree - ready,)),
        ],
        30, 8 * 10**9,
    )
    *before, edge_sum, counts = firsts
    fine_new, keep, send = run(
        fine_second_kernel, (1,), (flip,),
        [
            whole(degree, rows), whole(*pool_rows.shape), whole(rows, w), whole(margin, w), whole(margin, w),
            whole(2 * height, w), *[whole(rows, w)] * (degree + 1), *layer_specs,
        ],
        (fine_senders, pool_rows, fine_nodes, left, right, counts, *before, edge_sum, *layers),
        (pltpu.HBM((rows, w), f32), shaped(part + height, w), shaped(part + height, w)),
        [in_hbm, whole(part + height, w), whole(part + height, w)],
        [
            pltpu.VMEM((2 * margin, 2 * w), half), pltpu.VMEM(mats(4), half), pltpu.VMEM((rows, w), f32),
            pltpu.SemaphoreType.DMA,
        ],
        30, 4 * 10**9,
    )

    mine, theirs = keep, swapped(send, "sub", 1)
    bit = 2
    after = theirs
    while bit < n_sub:
        mine = mine + theirs
        theirs = swapped(mine, "sub", bit)
        after = mine if bit == 2 else after
        bit *= 2
    (coarse_share, chosen, quarter_before, quarter_sum, coarse_columns,
     quarter_weights, quarter_later, coarse_weights, coarse_later) = run(
        window_kernel, (1,), (patch_core,),
        [
            whole(*quarter_pool_rows.shape), whole(*pool_rows.shape),
            whole(q_rows * q_degree, w),
            pl.BlockSpec((c_degree, block), lambda i, place: (0, place[0])), *layer_specs, in_hbm,
        ],
        (quarter_pool_rows, pool_rows, quarter_edges.reshape(q_rows * q_degree, w), coarse_senders,
         *[hbm(x) for x in layers], after),
        (
            shaped(block, w), shaped(rows, block, dtype=half), shaped(q_degree, q_rows, w), shaped(q_rows, w),
            shaped(c_degree, block, w, dtype=short), shaped(*mats(2), dtype=half), shaped(*mats(4), dtype=half),
            shaped(*mats(3), dtype=half), shaped(*mats(4), dtype=half),
        ),
        [
            whole(block, w), whole(rows, block), whole(q_degree, q_rows, w), whole(q_rows, w),
            whole(c_degree, block, w), whole(*mats(2)), whole(*mats(4)), whole(*mats(3)),
            whole(*mats(4)),
        ],
        [], 16, 10**9,
    )
    mine = run(
        functools.partial(mean_kernel, lines), (1,), (), [whole(part + height, w)], (mine + theirs,),
        shaped(part, w), whole(part, w), [], 6, 10**7,
    )
    other = swapped(mine, "sub", 1)

    quarter_nodes, to_next, to_previous = run(
        quarter_nodes_kernel, (1,), (flip,), [whole(part, w), whole(part, w), whole(2, q_margin)],
        (mine, other, quarter_halo), (shaped(q_rows, w), shaped(q_margin, w), shaped(q_margin, w)),
        [whole(q_rows, w), whole(q_margin, w), whole(q_margin, w)], [], 8, 10**8,
    )
    left = passed(to_next, "patch", 1)
    right = passed(to_previous, "patch", -1)
    across = [own_edges]
    bit = 2
    while bit < n_sub:
        across += [swapped(value, "sub", bit) for value in across]
        bit *= 2
    edge_pieces = []
    for value in across:
        edge_pieces += [value, swapped(value, "sub", 1)]
    quarter_first = run(
        functools.partial(quarter_first_kernel, tile), (1,), (),
        [whole(q_degree, q_rows), whole(q_rows, w), whole(q_degree, q_rows, w), whole(*mats(2))],
        (quarter_senders, quarter_nodes, quarter_before, quarter_weights),
        shaped(q_degree, q_rows, w), whole(q_degree, q_rows, w), [pltpu.VMEM((q_rows, 2 * w), half)], 20, 3 * 10**9,
    )
    quarter_new, own, own_partner = run(
        quarter_second_kernel, (1,), (flip,),
        [
            whole(q_degree, q_rows), whole(*quarter_pool_rows.shape), whole(q_rows, w), whole(q_margin, w),
            whole(q_margin, w), whole(q_degree, q_rows, w), whole(q_rows, w), whole(block, w), whole(*mats(2)),
            whole(*mats(4)),
        ],
        (quarter_senders, quarter_pool_rows, quarter_nodes, left, right, quarter_first, quarter_sum, coarse_share,
         quarter_weights, quarter_later),
        (shaped(q_rows, w), shaped(c_part, w), shaped(c_part, w)),
        [whole(q_rows, w), whole(c_part, w), whole(c_part, w)],
        [pltpu.VMEM((2 * q_margin, 2 * w), half)], 20, 2 * 10**9,
    )

    pieces = [own] + [passed(own, "patch", -j) for j in range(1, n_patch)]
    partner = [own_partner] + [swapped(pieces[j], "sub", 1) for j in range(1, n_patch)]
    base = run(
        base_kernel, (1,), (), [whole(*pool_rows.shape), whole(q_rows, w), whole(rows, w)],
        (pool_rows, quarter_new, hbm(fine_new)), shaped(rows, w), whole(rows, w), [], 16, 10**9,
    )
    return run(
        functools.partial(coarse_kernel, n_patch, c_tile), (1,), (jnp.stack([patch, core, sub]),),
        [
            *[whole(c_part, w)] * (2 * n_patch), whole(c_degree, block, w), whole(rows, block), whole(rows, w),
            whole(*mats(3)), whole(*mats(4)), *[whole(*own_edges.shape)] * n_sub,
        ],
        (*pieces, *partner, coarse_columns, chosen, base, coarse_weights, coarse_later, *edge_pieces),
        shaped(rows, w), in_hbm,
        [
            pltpu.VMEM((total, w), f32), pltpu.VMEM((block * c_degree, w), f32),
            pltpu.VMEM((total + 2 * w, 2 * w), half), pltpu.VMEM((block, w), f32), pltpu.VMEM((rows, w), f32),
            pltpu.SemaphoreType.DMA((4,)),
        ],
        big, 2 * 10**9,
    )


def solution(mesh):
    split = P(("groups", "patch", "sub"))
    patches = P(("groups", "patch"))
    return jax.shard_map(
        on_device,
        mesh=mesh,
        in_specs=(
            split, split, split, split, split, patches, patches, patches, patches, split, P("groups"),
            P(), P(), P(), P(),
        ),
        out_specs=split,
        check_vma=False,
    )
```

```python
import functools

import jax
import jax.numpy as jnp
from jax import lax
from jax.experimental import pallas as pl
from jax.experimental.pallas import tpu as pltpu
from jax.sharding import PartitionSpec as P


f32 = jnp.float32
half = jnp.bfloat16
LANES = 128
EPS = 1e-05


def side(x):
    high = x.astype(half)
    low = (x - high.astype(f32)).astype(half)
    return jnp.concatenate([high, low], axis=1)


def packed(w):
    row = side(w)
    return jnp.concatenate([row, row], axis=0)


def folded(y):
    w = y.shape[1] // 2
    return y[:, :w] + y[:, w:]


def times(a, b):
    return lax.dot_general(a, b, (((1,), (0,)), ((), ())), preferred_element_type=f32)


def centred_columns(w):
    return w - jnp.mean(w, axis=1, keepdims=True)


def inverse_spread(v):
    return lax.rsqrt(jnp.mean(v * v, axis=1, keepdims=True) + EPS)


def down(row):
    n = row.shape[1]
    parts = []
    for start in range(0, n, LANES):
        wide = jnp.broadcast_to(row[:, start : start + LANES], (LANES, LANES))
        parts.append(jnp.transpose(wide).astype(jnp.int16))
    return parts[0] if len(parts) == 1 else jnp.concatenate(parts, axis=0)


def picks(column, size):
    n = column.shape[0]
    lane = lax.broadcasted_iota(jnp.int32, (n, LANES), 1)
    one, zero = jnp.ones((n, LANES), half), jnp.zeros((n, LANES), half)
    parts = [
        jnp.where(column == (lane + start).astype(jnp.int16), one, zero)
        for start in range(0, size, LANES)
    ]
    return jnp.concatenate(parts, axis=1)


def members(row, size):
    n = row.shape[1]
    line = lax.broadcasted_iota(jnp.int32, (size, n), 0).astype(jnp.int16)
    entry = jnp.broadcast_to(row, (size, n)).astype(jnp.int16)
    return jnp.where(entry == line, jnp.ones((size, n), half), jnp.zeros((size, n), half))


def counts_of(pools, first, size):
    line = (lax.broadcasted_iota(jnp.int32, (size, LANES), 0) + first).astype(jnp.int16)
    one, zero = jnp.ones((size, LANES), half), jnp.zeros((size, LANES), half)
    total = zero
    for pool in pools:
        for r in range(pool.shape[0]):
            entry = jnp.broadcast_to(pool[r : r + 1, :], (size, LANES)).astype(jnp.int16)
            total = total + jnp.where(entry == line, one, zero)
    return times(total, jnp.ones((LANES, LANES), half))


def along_lanes(pool, first, lines):
    rows, n = pool.shape
    column = jnp.concatenate([down(pool[r : r + 1, :]) for r in range(rows)], axis=0)
    lane = (lax.broadcasted_iota(jnp.int32, (16, LANES), 1) + first).astype(jnp.int16)
    one, zero = jnp.ones((16, LANES), jnp.int16), jnp.zeros((16, LANES), jnp.int16)
    out = []
    for r in range(lines):
        name = lane + jnp.int16(r * LANES)
        hits = [jnp.where(column[i : i + 16, :] == name, one, zero) for i in range(0, rows * n, 16)]
        while len(hits) > 1:
            hits = [a + b for a, b in zip(hits[::2], hits[1::2])] + ([hits[-1]] if len(hits) % 2 else [])
        out.append(jnp.sum(hits[0].astype(jnp.int32).astype(f32), axis=0, keepdims=True))
    return jnp.concatenate(out, axis=0)


def first_part(degree, tile, wide, column, reach, before, extra):
    sources = wide.shape[0]
    operand = jnp.concatenate([picks(column(k), sources) for k in range(degree)], axis=0)
    sums = folded(times(operand, wide[...])).reshape(degree, tile, -1)
    for k in range(degree):
        before[k][...] = sums[k] + reach + extra[k]


def second_part(degree, tile, hidden, edge_sum, receivers, weights):
    message = folded(times(side(hidden), weights[0]))
    message = (message * inverse_spread(message)).reshape(degree, tile, -1)
    total = edge_sum
    for k in range(degree):
        total = total + message[k]
    node = jnp.concatenate([side(receivers), side(total)], axis=1)
    rhs_node = jnp.concatenate([weights[1], weights[2]], axis=0)
    node_hidden = jnp.maximum(folded(times(node, rhs_node)), 0.0)
    update = folded(times(side(node_hidden), weights[3]))
    return receivers + update * inverse_spread(update)


def pack_first(edge_in, weights):
    w = edge_in.shape[1]
    weights[0] = packed(edge_in[0:w])
    weights[1] = packed(edge_in[w : 2 * w])


def pack_second(edge_out, node_in, node_out, weights):
    w = edge_out.shape[1]
    weights[0] = packed(centred_columns(edge_out[...]))
    weights[1] = packed(node_in[0:w])
    weights[2] = packed(node_in[w : 2 * w])
    weights[3] = packed(centred_columns(node_out[...]))


def with_halo(degree, tile, rows, margin, beyond, column, before):
    chosen = [picks(column(k) - jnp.int16(rows), 2 * margin) for k in range(degree)]
    sums = folded(times(jnp.concatenate(chosen, axis=0), beyond[...])).reshape(degree, tile, -1)
    parts = [jnp.maximum(sums[k] + before[k][...], 0.0) for k in range(degree)]
    return jnp.concatenate(parts, axis=0)


def halo_sources(left, right, sender, beyond):
    margin = left.shape[0]
    beyond[:margin, :] = side(folded(times(side(left[...]), sender)))
    beyond[margin:, :] = side(folded(times(side(right[...]), sender)))


def rotated(target, flip, part):
    return jnp.where(target < part, target + flip * part, target - flip * part)


def gather_halo(lists, nodes, to_next, to_previous):
    both = side(nodes[...])
    for i, out in enumerate((to_next, to_previous)):
        out[...] = folded(times(picks(down(lists[i : i + 1, :]), nodes.shape[0]), both))


def start_kernel(lists, nodes, senders, pool, edge_in, edges, to_next, to_previous, kept_nodes, kept_senders, kept_pool, weights, *refs):
    slots, (kept_lists, kept_layer, arrived) = refs[:-3], refs[-3:]
    moves = [(lists, kept_lists), (nodes, kept_nodes), (edge_in.at[0], kept_layer), (senders, kept_senders), (pool, kept_pool)]
    moves += [(edges.at[k], slots[k]) for k in range(len(slots))]
    copies = [pltpu.make_async_copy(*move, arrived.at[i]) for i, move in enumerate(moves)]
    for copy in copies:
        copy.start()
    copies[0].wait()
    copies[1].wait()
    gather_halo(kept_lists, kept_nodes, to_next, to_previous)
    copies[2].wait()
    pack_first(kept_layer, weights)
    w = nodes.shape[1]
    weights[2] = packed(kept_layer[2 * w : 3 * w])
    for copy in copies[3:]:
        copy.wait()


def fine_first_kernel(ready, lines, flip, senders, nodes, pool, weights, edges, *refs):
    degree = edges.shape[0]
    here, refs = refs[:ready], refs[ready:]
    before, refs = refs[:degree], refs[degree:]
    edge_sum, counts, wide, local, arrived = refs
    rows, _ = nodes.shape
    copies = [pltpu.make_async_copy(edges.at[k], local.at[k - ready], arrived.at[k - ready]) for k in range(ready, degree)]
    for copy in copies:
        copy.start()
    wide[:rows, :] = side(folded(times(side(nodes[...]), weights[0])))
    wide[rows:, :] = weights[2]
    reach = folded(times(side(nodes[...]), weights[1]))
    part = lines * LANES
    height = counts.shape[0] // 2
    counts[...] = jnp.zeros_like(counts)
    counts[:lines, :] = along_lanes(pool, flip[0] * part, lines)
    counts[height : height + lines, :] = along_lanes(pool, (1 - flip[0]) * part, lines)
    for k in range(degree):
        if k in (ready, ready + 2):
            for copy in copies[:2] if k == ready else copies[2:]:
                copy.wait()
        column = down(senders[k : k + 1, :])
        edge = here[k][...] if k < ready else local[k - ready]
        operand = jnp.concatenate([picks(column, rows), side(edge)], axis=1)
        before[k][...] = folded(times(operand, wide[...])) + reach
        edge_sum[...] = edge if k == 0 else edge_sum[...] + edge


def fine_second_kernel(flip, senders, pool, nodes, left, right, counts, *refs):
    degree = senders.shape[0]
    before, refs = refs[:degree], refs[degree:]
    edge_sum, edge_in, edge_out, node_in, node_out, new, keep, send, beyond, weights, held, sent = refs
    rows, w = nodes.shape
    margin = left.shape[0]
    halo_sources(left, right, packed(edge_in[0, 0:w]), beyond)
    pack_second(edge_out.at[0], node_in.at[0], node_out.at[0], weights)
    hidden = with_halo(degree, rows, rows, margin, beyond, lambda k: down(senders[k : k + 1, :]), before)
    held[...] = second_part(degree, rows, hidden, edge_sum[...], nodes[...], weights)
    copy = pltpu.make_async_copy(held, new, sent)
    copy.start()
    both = side(held[...])
    height = counts.shape[0] // 2
    part = keep.shape[0] - height
    target = jnp.concatenate([pool[j : j + 1, :] for j in range(pool.shape[0])], axis=1)
    target = rotated(target, flip[0], part)
    send[:part, :] = folded(times(members(target - part, part), both))
    keep[:part, :] = folded(times(members(target, part), both))
    keep[part:, :] = counts[:height, :]
    send[part:, :] = counts[height:, :]
    copy.wait()


def window_kernel(
    flip, quarter_pool, fine_pool, quarter_edges, coarse_senders, edge_in, edge_out, node_in, node_out, _,
    coarse_share, chosen, quarter_before, quarter_sum, coarse_columns,
    quarter_first, quarter_second, coarse_first, coarse_second,
):
    w = edge_in.shape[2]
    block = coarse_share.shape[0]
    share = 1.0 / counts_of([quarter_pool[...]], 0, block)
    coarse_share[...] = share

    degree, rows, _ = quarter_before.shape
    rhs = packed(edge_in[1, 2 * w : 3 * w])
    total = None
    for k in range(degree):
        edge = quarter_edges[pl.ds(k, rows, stride=degree), :]
        total = edge if total is None else total + edge
        quarter_before[k] = folded(times(side(edge), rhs))
    quarter_sum[...] = total
    pack_first(edge_in.at[1], quarter_first)
    pack_second(edge_out.at[1], node_in.at[1], node_out.at[1], quarter_second)
    pack_first(edge_in.at[2], coarse_first)
    coarse_first[2] = packed(edge_in[2, 2 * w : 3 * w])
    pack_second(edge_out.at[2], node_in.at[2], node_out.at[2], coarse_second)

    for k in range(coarse_columns.shape[0]):
        for start in range(0, block, LANES):
            coarse_columns[k, start : start + LANES, :] = down(coarse_senders[k : k + 1, start : start + LANES])

    parent = [down(quarter_pool[r : r + 1, :]) for r in range(quarter_pool.shape[0])]
    parent = side(jnp.concatenate(parent, axis=0).astype(jnp.int32).astype(f32))
    for r in range(fine_pool.shape[0]):
        rows = slice(r * LANES, (r + 1) * LANES)
        column = down(fine_pool[r : r + 1, :])
        named = folded(times(picks(column, parent.shape[0]), parent))
        chosen[rows, :] = picks(named.astype(jnp.int32).astype(jnp.int16), chosen.shape[1])


def mean_kernel(lines, total, out):
    part = out.shape[0]
    counts = total[part : part + lines, :]
    for r in range(lines):
        rows = slice(r * LANES, (r + 1) * LANES)
        share = 1.0 / jnp.transpose(jnp.broadcast_to(counts[r : r + 1, :], (LANES, LANES)))
        out[rows, :] = total[rows, :] * share


def quarter_nodes_kernel(flip, mine, other, lists, nodes, to_next, to_previous):
    part = mine.shape[0]
    nodes[pl.ds(pl.multiple_of(flip[0] * part, part), part), :] = mine[...]
    nodes[pl.ds(pl.multiple_of((1 - flip[0]) * part, part), part), :] = other[...]
    gather_halo(lists, nodes, to_next, to_previous)


def quarter_first_kernel(tile, senders, nodes, extra, weights, before, wide):
    degree, rows, _ = before.shape
    wide[...] = side(folded(times(side(nodes[...]), weights[0])))
    for t in range(rows // tile):
        span = slice(t * tile, (t + 1) * tile)
        reach = folded(times(side(nodes[span, :]), weights[1]))
        first_part(
            degree, tile, wide, lambda k: down(senders[k : k + 1, span]), reach,
            [before.at[k, span, :] for k in range(degree)], extra.at[:, span, :],
        )


def quarter_second_kernel(
    flip, senders, pool, nodes, left, right, before, edge_sum, share, first_weights, weights, new, own, partner, beyond,
):
    degree, rows, _ = before.shape
    margin = left.shape[0]
    halo_sources(left, right, first_weights[0], beyond)
    hidden = with_halo(
        degree, rows, rows, margin, beyond, lambda k: down(senders[k : k + 1, :]),
        [before.at[k] for k in range(degree)],
    )
    updated = second_part(degree, rows, hidden, edge_sum[...], nodes[...], weights)
    new[...] = updated
    part = own.shape[0]
    target = jnp.concatenate([pool[j : j + 1, :] for j in range(pool.shape[0])], axis=1)
    target = rotated(target, flip[0], part)
    split = side(updated)
    first = pl.multiple_of(flip[0] * part, part)
    second = pl.multiple_of((1 - flip[0]) * part, part)
    own[...] = folded(times(members(target, part), split)) * share[pl.ds(first, part), :]
    partner[...] = folded(times(members(target - part, part), split)) * share[pl.ds(second, part), :]


def base_kernel(pool, quarter, fine_new, out):
    both = side(quarter[...])
    column = jnp.concatenate([down(pool[r : r + 1, :]) for r in range(pool.shape[0])], axis=0)
    out[...] = fine_new[...] + folded(times(picks(column, both.shape[0]), both))


def coarse_first_kernel(place, own, partner, columns, first_weights, *refs):
    pieces, (before, edge_sum, nodes, edges, wide) = refs[:-5], refs[-5:]
    part, w = own.shape
    block = 2 * part
    piece = pieces[0].shape[0]
    degree = columns.shape[0]
    for j, source in enumerate(pieces):
        at = jnp.bitwise_xor(place[2], j)
        edges[pl.ds(pl.multiple_of(at * piece, piece), piece), :] = source[...]
    nodes[pl.ds(pl.multiple_of(place[1] * part, part), part), :] = own[...]
    nodes[pl.ds(pl.multiple_of((1 - place[1]) * part, part), part), :] = partner[...]
    both = side(nodes[...])
    wide[:block, :] = side(folded(times(both, first_weights[0])))
    wide[block:, :] = first_weights[2]
    reach = folded(times(both, first_weights[1]))
    first = (place[0] * block).astype(jnp.int16)
    edge = [edges[pl.ds(k, block, stride=degree), :] for k in range(degree)]
    operand = [jnp.concatenate([picks(columns[k] - first, block), side(edge[k])], axis=1) for k in range(degree)]
    sums = folded(times(jnp.concatenate(operand, axis=0), wide[...])).reshape(degree, block, w)
    total = edge[0]
    for k in range(1, degree):
        total = total + edge[k]
    edge_sum[...] = total
    for k in range(degree):
        before[k] = sums[k] + reach


def coarse_kernel(n_patch, place, own, own_partner, *refs):
    mine, refs = refs[: n_patch - 1], refs[n_patch - 1 :]
    other, refs = refs[: n_patch - 1], refs[n_patch - 1 :]
    columns, chosen, base, before, edge_sum, first_weights, weights, out, nodes, receivers, wide, new, held, sent = refs
    part, w = own.shape
    block = 2 * part
    degree = columns.shape[0]
    sources = nodes.shape[0]
    for j in range(n_patch - 1):
        nodes[pl.ds(pl.multiple_of(j * block + place[1] * part, part), part), :] = mine[j][...]
        nodes[pl.ds(pl.multiple_of(j * block + (1 - place[1]) * part, part), part), :] = other[j][...]
    receivers[pl.ds(pl.multiple_of(place[1] * part, part), part), :] = own[...]
    receivers[pl.ds(pl.multiple_of((1 - place[1]) * part, part), part), :] = own_partner[...]
    wide[...] = side(folded(times(side(nodes[...]), first_weights[0])))
    first = ((place[0] + 1) * block).astype(jnp.int16)
    column = columns[...] - first
    column = jnp.where(column < 0, column + jnp.int16(n_patch * block), column)
    operand = jnp.concatenate([picks(column[k], sources) for k in range(degree)], axis=0)
    hidden = jnp.maximum(folded(times(operand, wide[...])) + before[...].reshape(degree * block, w), 0.0)
    new[...] = second_part(degree, block, hidden, edge_sum[...], receivers[...], weights)
    both = side(new[...])
    steps = sent.shape[0]
    rows = out.shape[0] // steps
    copies = []
    for i in range(steps):
        span = slice(i * rows, (i + 1) * rows)
        held[span, :] = base[span, :] + folded(times(chosen[span, :], both))
        copies.append(pltpu.make_async_copy(held.at[span, :], out.at[span, :], sent.at[i]))
        copies[-1].start()
    for copy in copies:
        copy.wait()


def whole(*shape):
    return pl.BlockSpec(shape, lambda *_: (0,) * len(shape))


def shaped(*shape, dtype=f32):
    return jax.ShapeDtypeStruct(shape, dtype)


def run(kernel, grid, scalars, in_specs, operands, outs, out_specs, scratch, mega, flops):
    return pl.pallas_call(
        kernel,
        out_shape=outs,
        grid_spec=pltpu.PrefetchScalarGridSpec(
            num_scalar_prefetch=len(scalars), grid=grid, in_specs=in_specs, out_specs=out_specs,
            scratch_shapes=scratch,
        ),
        compiler_params=pltpu.CompilerParams(vmem_limit_bytes=mega * 1024 * 1024),
        cost_estimate=pl.CostEstimate(flops=flops, bytes_accessed=10**6, transcendentals=0),
    )(*scalars, *operands)


def passed(value, axis, steps):
    count = lax.axis_size(axis)
    return lax.ppermute(value, axis, [(s, (s + steps) % count) for s in range(count)])


def swapped(value, axis, bit):
    count = lax.axis_size(axis)
    return lax.ppermute(value, axis, [(s, s ^ bit) for s in range(count)])


def on_device(
    fine_nodes, fine_edges, fine_senders, fine_halo, fine_pool, quarter_edges, quarter_senders,
    quarter_halo, quarter_pool, coarse_edges, coarse_senders, edge_in, edge_out, node_in, node_out,
):
    n_sub, n_patch = lax.axis_size("sub"), lax.axis_size("patch")
    sub, patch = lax.axis_index("sub").astype(jnp.int32), lax.axis_index("patch").astype(jnp.int32)
    rows, degree, w = fine_edges.shape
    q_rows, q_degree, _ = quarter_edges.shape
    margin, q_margin = fine_halo.shape[1], quarter_halo.shape[1]
    piece, c_degree, _ = coarse_edges.shape
    total = coarse_senders.shape[0]
    block = total // n_patch
    part, c_part = q_rows // 2, block // 2
    tile = min(512, q_rows)
    lines = part // LANES
    height = -(-lines // 8) * 8
    core = sub % 2
    flip = core.reshape(1)
    patch_core = jnp.stack([patch, core])
    layers = (edge_in, edge_out, node_in, node_out)
    layer_specs = [whole(*x.shape) for x in layers]
    in_hbm, in_vmem = pl.BlockSpec(memory_space=pl.ANY), pl.BlockSpec(memory_space=pltpu.VMEM)
    pool_rows = fine_pool.reshape(rows // LANES, LANES)
    quarter_pool_rows = quarter_pool.reshape(q_rows // LANES, LANES)
    fine_senders, quarter_senders, coarse_senders = fine_senders.T, quarter_senders.T, coarse_senders.T
    own_edges = coarse_edges.reshape(piece * c_degree, w)
    hbm = lambda x: pltpu.with_memory_space_constraint(x, pltpu.HBM)
    mats = lambda n: (n, 2 * w, 2 * w)
    short = jnp.int16
    big = 16 if total <= 2048 else 48

    ready = min(2, degree - 1)
    edges = hbm(fine_edges.transpose(1, 0, 2))
    to_next, to_previous, nodes, senders, pool, fine_weights, *here = run(
        start_kernel, (1,), (), [in_hbm] * 6,
        (hbm(fine_halo), hbm(fine_nodes), hbm(fine_senders), hbm(pool_rows), hbm(edge_in), edges),
        (
            shaped(margin, w), shaped(margin, w), shaped(rows, w), shaped(degree, rows, dtype=jnp.int32),
            shaped(*pool_rows.shape, dtype=jnp.int32), shaped(*mats(3), dtype=half), *(shaped(rows, w),) * ready,
        ),
        [
            whole(margin, w), whole(margin, w), in_vmem, in_vmem, in_vmem, whole(*mats(3)), *[in_vmem] * ready,
        ],
        [pltpu.VMEM((2, margin), jnp.int32), pltpu.VMEM((3 * w, w), f32), pltpu.SemaphoreType.DMA((ready + 5,))],
        8, 10**8,
    )
    left = passed(to_next, ("patch", "sub"), 1)
    right = passed(to_previous, ("patch", "sub"), -1)
    firsts = run(
        functools.partial(fine_first_kernel, ready, lines), (1,), (flip,),
        [whole(degree, rows), whole(rows, w), whole(*pool_rows.shape), whole(*mats(3)), in_hbm, *[whole(rows, w)] * ready],
        (senders, nodes, pool, fine_weights, edges, *here),
        (*(shaped(rows, w),) * (degree + 1), shaped(2 * height, w)),
        [whole(rows, w)] * (degree + 1) + [whole(2 * height, w)],
        [
            pltpu.VMEM((rows + 2 * w, 2 * w), half),
            pltpu.VMEM((degree - ready, rows, w), f32), pltpu.SemaphoreType.DMA((degree - ready,)),
        ],
        30, 8 * 10**9,
    )
    *before, edge_sum, counts = firsts
    fine_new, keep, send = run(
        fine_second_kernel, (1,), (flip,),
        [
            whole(degree, rows), whole(*pool_rows.shape), whole(rows, w), whole(margin, w), whole(margin, w),
            whole(2 * height, w), *[whole(rows, w)] * (degree + 1), *layer_specs,
        ],
        (fine_senders, pool_rows, fine_nodes, left, right, counts, *before, edge_sum, *layers),
        (pltpu.HBM((rows, w), f32), shaped(part + height, w), shaped(part + height, w)),
        [in_hbm, whole(part + height, w), whole(part + height, w)],
        [
            pltpu.VMEM((2 * margin, 2 * w), half), pltpu.VMEM(mats(4), half), pltpu.VMEM((rows, w), f32),
            pltpu.SemaphoreType.DMA,
        ],
        30, 4 * 10**9,
    )

    mine, theirs = keep, swapped(send, "sub", 1)
    bit = 2
    after = theirs
    while bit < n_sub:
        mine = mine + theirs
        theirs = swapped(mine, "sub", bit)
        after = mine if bit == 2 else after
        bit *= 2
    (coarse_share, chosen, quarter_before, quarter_sum, coarse_columns,
     quarter_weights, quarter_later, coarse_weights, coarse_later) = run(
        window_kernel, (1,), (patch_core,),
        [
            whole(*quarter_pool_rows.shape), whole(*pool_rows.shape),
            whole(q_rows * q_degree, w),
            pl.BlockSpec((c_degree, block), lambda i, place: (0, place[0])), *layer_specs, in_hbm,
        ],
        (quarter_pool_rows, pool_rows, quarter_edges.reshape(q_rows * q_degree, w), coarse_senders,
         *[hbm(x) for x in layers], after),
        (
            shaped(block, w), shaped(rows, block, dtype=half), shaped(q_degree, q_rows, w), shaped(q_rows, w),
            shaped(c_degree, block, w, dtype=short), shaped(*mats(2), dtype=half), shaped(*mats(4), dtype=half),
            shaped(*mats(3), dtype=half), shaped(*mats(4), dtype=half),
        ),
        [
            whole(block, w), whole(rows, block), whole(q_degree, q_rows, w), whole(q_rows, w),
            whole(c_degree, block, w), whole(*mats(2)), whole(*mats(4)), whole(*mats(3)),
            whole(*mats(4)),
        ],
        [], 16, 10**9,
    )
    mine = run(
        functools.partial(mean_kernel, lines), (1,), (), [whole(part + height, w)], (mine + theirs,),
        shaped(part, w), whole(part, w), [], 6, 10**7,
    )
    other = swapped(mine, "sub", 1)

    quarter_nodes, to_next, to_previous = run(
        quarter_nodes_kernel, (1,), (flip,), [whole(part, w), whole(part, w), whole(2, q_margin)],
        (mine, other, quarter_halo), (shaped(q_rows, w), shaped(q_margin, w), shaped(q_margin, w)),
        [whole(q_rows, w), whole(q_margin, w), whole(q_margin, w)], [], 8, 10**8,
    )
    left = passed(to_next, "patch", 1)
    right = passed(to_previous, "patch", -1)
    across = [own_edges]
    bit = 2
    while bit < n_sub:
        across += [swapped(value, "sub", bit) for value in across]
        bit *= 2
    edge_pieces = []
    for value in across:
        edge_pieces += [value, swapped(value, "sub", 1)]
    quarter_first = run(
        functools.partial(quarter_first_kernel, tile), (1,), (),
        [whole(q_degree, q_rows), whole(q_rows, w), whole(q_degree, q_rows, w), whole(*mats(2))],
        (quarter_senders, quarter_nodes, quarter_before, quarter_weights),
        shaped(q_degree, q_rows, w), whole(q_degree, q_rows, w), [pltpu.VMEM((q_rows, 2 * w), half)], 20, 3 * 10**9,
    )
    quarter_new, own, own_partner = run(
        quarter_second_kernel, (1,), (flip,),
        [
            whole(q_degree, q_rows), whole(*quarter_pool_rows.shape), whole(q_rows, w), whole(q_margin, w),
            whole(q_margin, w), whole(q_degree, q_rows, w), whole(q_rows, w), whole(block, w), whole(*mats(2)),
            whole(*mats(4)),
        ],
        (quarter_senders, quarter_pool_rows, quarter_nodes, left, right, quarter_first, quarter_sum, coarse_share,
         quarter_weights, quarter_later),
        (shaped(q_rows, w), shaped(c_part, w), shaped(c_part, w)),
        [whole(q_rows, w), whole(c_part, w), whole(c_part, w)],
        [pltpu.VMEM((2 * q_margin, 2 * w), half)], 20, 2 * 10**9,
    )

    pieces = [own] + [passed(own, "patch", -j) for j in range(1, n_patch)]
    partner = [own_partner] + [swapped(pieces[j], "sub", 1) for j in range(1, n_patch)]
    base = run(
        base_kernel, (1,), (), [whole(*pool_rows.shape), whole(q_rows, w), whole(rows, w)],
        (pool_rows, quarter_new, hbm(fine_new)), shaped(rows, w), whole(rows, w), [], 16, 10**9,
    )
    place = jnp.stack([patch, core, sub])
    before, edge_sum = run(
        coarse_first_kernel, (1,), (place,),
        [
            whole(c_part, w), whole(c_part, w), whole(c_degree, block, w), whole(*mats(3)),
            *[whole(*own_edges.shape)] * n_sub,
        ],
        (own, own_partner, coarse_columns, coarse_weights, *edge_pieces),
        (shaped(c_degree, block, w), shaped(block, w)), [whole(c_degree, block, w), whole(block, w)],
        [
            pltpu.VMEM((block, w), f32), pltpu.VMEM((block * c_degree, w), f32),
            pltpu.VMEM((block + 2 * w, 2 * w), half),
        ],
        16, 10**9,
    )
    return run(
        functools.partial(coarse_kernel, n_patch), (1,), (place,),
        [
            *[whole(c_part, w)] * (2 * n_patch), whole(c_degree, block, w), whole(rows, block), whole(rows, w),
            whole(c_degree, block, w), whole(block, w), whole(*mats(3)), whole(*mats(4)),
        ],
        (own, own_partner, *pieces[1:], *partner[1:], coarse_columns, chosen, base, before, edge_sum, coarse_weights,
         coarse_later),
        shaped(rows, w), in_hbm,
        [
            pltpu.VMEM((total - block, w), f32), pltpu.VMEM((block, w), f32),
            pltpu.VMEM((total - block, 2 * w), half), pltpu.VMEM((block, w), f32), pltpu.VMEM((rows, w), f32),
            pltpu.SemaphoreType.DMA((4,)),
        ],
        big, 2 * 10**9,
    )


def solution(mesh):
    split = P(("groups", "patch", "sub"))
    patches = P(("groups", "patch"))
    return jax.shard_map(
        on_device,
        mesh=mesh,
        in_specs=(
            split, split, split, split, split, patches, patches, patches, patches, split, P("groups"),
            P(), P(), P(), P(),
        ),
        out_specs=split,
        check_vma=False,
    )
```

```python
import functools

import jax
import jax.numpy as jnp
from jax import lax
from jax.experimental import pallas as pl
from jax.experimental.pallas import tpu as pltpu
from jax.sharding import PartitionSpec as P


f32 = jnp.float32
half = jnp.bfloat16
LANES = 128
EPS = 1e-05


def side(x):
    high = x.astype(half)
    low = (x - high.astype(f32)).astype(half)
    return jnp.concatenate([high, low], axis=1)


def packed(w):
    row = side(w)
    return jnp.concatenate([row, row], axis=0)


def folded(y):
    w = y.shape[1] // 2
    return y[:, :w] + y[:, w:]


def times(a, b):
    return lax.dot_general(a, b, (((1,), (0,)), ((), ())), preferred_element_type=f32)


def centred_columns(w):
    return w - jnp.mean(w, axis=1, keepdims=True)


def inverse_spread(v):
    return lax.rsqrt(jnp.mean(v * v, axis=1, keepdims=True) + EPS)


def down(row):
    n = row.shape[1]
    parts = []
    for start in range(0, n, LANES):
        wide = jnp.broadcast_to(row[:, start : start + LANES], (LANES, LANES))
        parts.append(jnp.transpose(wide).astype(jnp.int16))
    return parts[0] if len(parts) == 1 else jnp.concatenate(parts, axis=0)


def picks(column, size):
    n = column.shape[0]
    lane = lax.broadcasted_iota(jnp.int32, (n, LANES), 1)
    one, zero = jnp.ones((n, LANES), half), jnp.zeros((n, LANES), half)
    parts = [
        jnp.where(column == (lane + start).astype(jnp.int16), one, zero)
        for start in range(0, size, LANES)
    ]
    return jnp.concatenate(parts, axis=1)


def members(row, size):
    n = row.shape[1]
    line = lax.broadcasted_iota(jnp.int32, (size, n), 0).astype(jnp.int16)
    entry = jnp.broadcast_to(row, (size, n)).astype(jnp.int16)
    return jnp.where(entry == line, jnp.ones((size, n), half), jnp.zeros((size, n), half))


def counts_of(pools, first, size):
    line = (lax.broadcasted_iota(jnp.int32, (size, LANES), 0) + first).astype(jnp.int16)
    one, zero = jnp.ones((size, LANES), half), jnp.zeros((size, LANES), half)
    total = zero
    for pool in pools:
        for r in range(pool.shape[0]):
            entry = jnp.broadcast_to(pool[r : r + 1, :], (size, LANES)).astype(jnp.int16)
            total = total + jnp.where(entry == line, one, zero)
    return times(total, jnp.ones((LANES, LANES), half))


def along_lanes(pool, first, lines):
    rows, n = pool.shape
    column = jnp.concatenate([down(pool[r : r + 1, :]) for r in range(rows)], axis=0)
    lane = (lax.broadcasted_iota(jnp.int32, (16, LANES), 1) + first).astype(jnp.int16)
    one, zero = jnp.ones((16, LANES), jnp.int16), jnp.zeros((16, LANES), jnp.int16)
    out = []
    for r in range(lines):
        name = lane + jnp.int16(r * LANES)
        hits = [jnp.where(column[i : i + 16, :] == name, one, zero) for i in range(0, rows * n, 16)]
        while len(hits) > 1:
            hits = [a + b for a, b in zip(hits[::2], hits[1::2])] + ([hits[-1]] if len(hits) % 2 else [])
        out.append(jnp.sum(hits[0].astype(jnp.int32).astype(f32), axis=0, keepdims=True))
    return jnp.concatenate(out, axis=0)


def first_part(degree, tile, wide, column, reach, before, extra):
    sources = wide.shape[0]
    operand = jnp.concatenate([picks(column(k), sources) for k in range(degree)], axis=0)
    sums = folded(times(operand, wide[...])).reshape(degree, tile, -1)
    for k in range(degree):
        before[k][...] = sums[k] + reach + extra[k]


def second_part(degree, tile, hidden, edge_sum, receivers, weights):
    message = folded(times(side(hidden), weights[0]))
    message = (message * inverse_spread(message)).reshape(degree, tile, -1)
    total = edge_sum
    for k in range(degree):
        total = total + message[k]
    node = jnp.concatenate([side(receivers), side(total)], axis=1)
    rhs_node = jnp.concatenate([weights[1], weights[2]], axis=0)
    node_hidden = jnp.maximum(folded(times(node, rhs_node)), 0.0)
    update = folded(times(side(node_hidden), weights[3]))
    return receivers + update * inverse_spread(update)


def pack_first(edge_in, weights):
    w = edge_in.shape[1]
    weights[0] = packed(edge_in[0:w])
    weights[1] = packed(edge_in[w : 2 * w])


def pack_second(edge_out, node_in, node_out, weights):
    w = edge_out.shape[1]
    weights[0] = packed(centred_columns(edge_out[...]))
    weights[1] = packed(node_in[0:w])
    weights[2] = packed(node_in[w : 2 * w])
    weights[3] = packed(centred_columns(node_out[...]))


def with_halo(degree, tile, rows, margin, beyond, column, before):
    chosen = [picks(column(k) - jnp.int16(rows), 2 * margin) for k in range(degree)]
    sums = folded(times(jnp.concatenate(chosen, axis=0), beyond[...])).reshape(degree, tile, -1)
    parts = [jnp.maximum(sums[k] + before[k][...], 0.0) for k in range(degree)]
    return jnp.concatenate(parts, axis=0)


def halo_sources(left, right, sender, beyond):
    margin = left.shape[0]
    beyond[:margin, :] = side(folded(times(side(left[...]), sender)))
    beyond[margin:, :] = side(folded(times(side(right[...]), sender)))


def rotated(target, flip, part):
    return jnp.where(target < part, target + flip * part, target - flip * part)


def gather_halo(lists, nodes, to_next, to_previous):
    both = side(nodes[...])
    for i, out in enumerate((to_next, to_previous)):
        out[...] = folded(times(picks(down(lists[i : i + 1, :]), nodes.shape[0]), both))


def start_kernel(lists, nodes, senders, pool, edge_in, edges, to_next, to_previous, kept_nodes, kept_senders, kept_pool, weights, *refs):
    slots, (kept_lists, kept_layer, arrived) = refs[:-3], refs[-3:]
    moves = [(lists, kept_lists), (nodes, kept_nodes), (edge_in.at[0], kept_layer), (senders, kept_senders), (pool, kept_pool)]
    moves += [(edges.at[k], slots[k]) for k in range(len(slots))]
    copies = [pltpu.make_async_copy(*move, arrived.at[i]) for i, move in enumerate(moves)]
    for copy in copies:
        copy.start()
    copies[0].wait()
    copies[1].wait()
    gather_halo(kept_lists, kept_nodes, to_next, to_previous)
    copies[2].wait()
    pack_first(kept_layer, weights)
    w = nodes.shape[1]
    weights[2] = packed(kept_layer[2 * w : 3 * w])
    for copy in copies[3:]:
        copy.wait()


def fine_first_kernel(ready, lines, flip, senders, nodes, pool, weights, edges, *refs):
    degree = edges.shape[0]
    here, refs = refs[:ready], refs[ready:]
    before, refs = refs[:degree], refs[degree:]
    edge_sum, counts, wide, local, arrived = refs
    rows, _ = nodes.shape
    copies = [pltpu.make_async_copy(edges.at[k], local.at[k - ready], arrived.at[k - ready]) for k in range(ready, degree)]
    for copy in copies:
        copy.start()
    wide[:rows, :] = side(folded(times(side(nodes[...]), weights[0])))
    wide[rows:, :] = weights[2]
    reach = folded(times(side(nodes[...]), weights[1]))
    part = lines * LANES
    height = counts.shape[0] // 2
    counts[...] = jnp.zeros_like(counts)
    counts[:lines, :] = along_lanes(pool, flip[0] * part, lines)
    counts[height : height + lines, :] = along_lanes(pool, (1 - flip[0]) * part, lines)
    for k in range(degree):
        if k in (ready, ready + 2):
            for copy in copies[:2] if k == ready else copies[2:]:
                copy.wait()
        column = down(senders[k : k + 1, :])
        edge = here[k][...] if k < ready else local[k - ready]
        operand = jnp.concatenate([picks(column, rows), side(edge)], axis=1)
        before[k][...] = folded(times(operand, wide[...])) + reach
        edge_sum[...] = edge if k == 0 else edge_sum[...] + edge


def fine_second_kernel(flip, senders, pool, nodes, left, right, counts, *refs):
    degree = senders.shape[0]
    before, refs = refs[:degree], refs[degree:]
    edge_sum, edge_in, edge_out, node_in, node_out, new, keep, send, beyond, weights, held, sent = refs
    rows, w = nodes.shape
    margin = left.shape[0]
    halo_sources(left, right, packed(edge_in[0, 0:w]), beyond)
    pack_second(edge_out.at[0], node_in.at[0], node_out.at[0], weights)
    hidden = with_halo(degree, rows, rows, margin, beyond, lambda k: down(senders[k : k + 1, :]), before)
    held[...] = second_part(degree, rows, hidden, edge_sum[...], nodes[...], weights)
    copy = pltpu.make_async_copy(held, new, sent)
    copy.start()
    both = side(held[...])
    height = counts.shape[0] // 2
    part = keep.shape[0] - height
    target = jnp.concatenate([pool[j : j + 1, :] for j in range(pool.shape[0])], axis=1)
    target = rotated(target, flip[0], part)
    send[:part, :] = folded(times(members(target - part, part), both))
    keep[:part, :] = folded(times(members(target, part), both))
    keep[part:, :] = counts[:height, :]
    send[part:, :] = counts[height:, :]
    copy.wait()


def window_kernel(
    flip, quarter_pool, fine_pool, quarter_edges, coarse_senders, edge_in, edge_out, node_in, node_out, _,
    coarse_share, chosen, quarter_before, quarter_sum, coarse_columns,
    quarter_first, quarter_second, coarse_first, coarse_second,
):
    w = edge_in.shape[2]
    block = coarse_share.shape[0]
    share = 1.0 / counts_of([quarter_pool[...]], 0, block)
    coarse_share[...] = share

    degree, rows, _ = quarter_before.shape
    rhs = packed(edge_in[1, 2 * w : 3 * w])
    total = None
    for k in range(degree):
        edge = quarter_edges[pl.ds(k, rows, stride=degree), :]
        total = edge if total is None else total + edge
        quarter_before[k] = folded(times(side(edge), rhs))
    quarter_sum[...] = total
    pack_first(edge_in.at[1], quarter_first)
    pack_second(edge_out.at[1], node_in.at[1], node_out.at[1], quarter_second)
    pack_first(edge_in.at[2], coarse_first)
    coarse_first[2] = packed(edge_in[2, 2 * w : 3 * w])
    pack_second(edge_out.at[2], node_in.at[2], node_out.at[2], coarse_second)

    for k in range(coarse_columns.shape[0]):
        for start in range(0, block, LANES):
            coarse_columns[k, start : start + LANES, :] = down(coarse_senders[k : k + 1, start : start + LANES])

    parent = [down(quarter_pool[r : r + 1, :]) for r in range(quarter_pool.shape[0])]
    parent = side(jnp.concatenate(parent, axis=0).astype(jnp.int32).astype(f32))
    for r in range(fine_pool.shape[0]):
        rows = slice(r * LANES, (r + 1) * LANES)
        column = down(fine_pool[r : r + 1, :])
        named = folded(times(picks(column, parent.shape[0]), parent))
        chosen[rows, :] = picks(named.astype(jnp.int32).astype(jnp.int16), chosen.shape[1])


def mean_kernel(lines, total, out):
    part = out.shape[0]
    counts = total[part : part + lines, :]
    for r in range(lines):
        rows = slice(r * LANES, (r + 1) * LANES)
        share = 1.0 / jnp.transpose(jnp.broadcast_to(counts[r : r + 1, :], (LANES, LANES)))
        out[rows, :] = total[rows, :] * share


def quarter_nodes_kernel(flip, mine, other, lists, nodes, to_next, to_previous):
    part = mine.shape[0]
    nodes[pl.ds(pl.multiple_of(flip[0] * part, part), part), :] = mine[...]
    nodes[pl.ds(pl.multiple_of((1 - flip[0]) * part, part), part), :] = other[...]
    gather_halo(lists, nodes, to_next, to_previous)


def quarter_first_kernel(tile, senders, nodes, extra, weights, before, wide):
    degree, rows, _ = before.shape
    wide[...] = side(folded(times(side(nodes[...]), weights[0])))
    for t in range(rows // tile):
        span = slice(t * tile, (t + 1) * tile)
        reach = folded(times(side(nodes[span, :]), weights[1]))
        first_part(
            degree, tile, wide, lambda k: down(senders[k : k + 1, span]), reach,
            [before.at[k, span, :] for k in range(degree)], extra.at[:, span, :],
        )


def quarter_second_kernel(
    flip, senders, pool, nodes, left, right, before, edge_sum, share, first_weights, weights, new, own, beyond,
):
    degree, rows, _ = before.shape
    margin = left.shape[0]
    halo_sources(left, right, first_weights[0], beyond)
    hidden = with_halo(
        degree, rows, rows, margin, beyond, lambda k: down(senders[k : k + 1, :]),
        [before.at[k] for k in range(degree)],
    )
    updated = second_part(degree, rows, hidden, edge_sum[...], nodes[...], weights)
    new[...] = updated
    part = own.shape[0]
    target = jnp.concatenate([pool[j : j + 1, :] for j in range(pool.shape[0])], axis=1)
    target = rotated(target, flip[0], part)
    split = side(updated)
    first = pl.multiple_of(flip[0] * part, part)
    own[...] = folded(times(members(target, part), split)) * share[pl.ds(first, part), :]


def base_kernel(flip, pool, quarter_pool, quarter, share, fine_new, out, partner):
    both = side(quarter[...])
    part = partner.shape[0]
    target = jnp.concatenate([quarter_pool[j : j + 1, :] for j in range(quarter_pool.shape[0])], axis=1)
    target = rotated(target, flip[0], part) - part
    second = pl.multiple_of((1 - flip[0]) * part, part)
    partner[...] = folded(times(members(target, part), both)) * share[pl.ds(second, part), :]
    column = jnp.concatenate([down(pool[r : r + 1, :]) for r in range(pool.shape[0])], axis=0)
    out[...] = fine_new[...] + folded(times(picks(column, both.shape[0]), both))


def coarse_first_kernel(place, own, partner, columns, first_weights, *refs):
    pieces, (before, edge_sum, nodes, edges, wide) = refs[:-5], refs[-5:]
    part, w = own.shape
    block = 2 * part
    piece = pieces[0].shape[0]
    degree = columns.shape[0]
    for j, source in enumerate(pieces):
        at = jnp.bitwise_xor(place[2], j)
        edges[pl.ds(pl.multiple_of(at * piece, piece), piece), :] = source[...]
    nodes[pl.ds(pl.multiple_of(place[1] * part, part), part), :] = own[...]
    nodes[pl.ds(pl.multiple_of((1 - place[1]) * part, part), part), :] = partner[...]
    both = side(nodes[...])
    wide[:block, :] = side(folded(times(both, first_weights[0])))
    wide[block:, :] = first_weights[2]
    reach = folded(times(both, first_weights[1]))
    first = (place[0] * block).astype(jnp.int16)
    edge = [edges[pl.ds(k, block, stride=degree), :] for k in range(degree)]
    operand = [jnp.concatenate([picks(columns[k] - first, block), side(edge[k])], axis=1) for k in range(degree)]
    sums = folded(times(jnp.concatenate(operand, axis=0), wide[...])).reshape(degree, block, w)
    total = edge[0]
    for k in range(1, degree):
        total = total + edge[k]
    edge_sum[...] = total
    for k in range(degree):
        before[k] = sums[k] + reach


def coarse_kernel(n_patch, place, own, own_partner, *refs):
    mine, refs = refs[: n_patch - 1], refs[n_patch - 1 :]
    other, refs = refs[: n_patch - 1], refs[n_patch - 1 :]
    columns, chosen, base, before, edge_sum, first_weights, weights, out, nodes, receivers, wide, new, held, sent = refs
    part, w = own.shape
    block = 2 * part
    degree = columns.shape[0]
    sources = nodes.shape[0]
    for j in range(n_patch - 1):
        nodes[pl.ds(pl.multiple_of(j * block + place[1] * part, part), part), :] = mine[j][...]
        nodes[pl.ds(pl.multiple_of(j * block + (1 - place[1]) * part, part), part), :] = other[j][...]
    receivers[pl.ds(pl.multiple_of(place[1] * part, part), part), :] = own[...]
    receivers[pl.ds(pl.multiple_of((1 - place[1]) * part, part), part), :] = own_partner[...]
    wide[...] = side(folded(times(side(nodes[...]), first_weights[0])))
    first = ((place[0] + 1) * block).astype(jnp.int16)
    column = columns[...] - first
    column = jnp.where(column < 0, column + jnp.int16(n_patch * block), column)
    operand = jnp.concatenate([picks(column[k], sources) for k in range(degree)], axis=0)
    hidden = jnp.maximum(folded(times(operand, wide[...])) + before[...].reshape(degree * block, w), 0.0)
    new[...] = second_part(degree, block, hidden, edge_sum[...], receivers[...], weights)
    both = side(new[...])
    steps = sent.shape[0]
    rows = out.shape[0] // steps
    copies = []
    for i in range(steps):
        span = slice(i * rows, (i + 1) * rows)
        held[span, :] = base[span, :] + folded(times(chosen[span, :], both))
        copies.append(pltpu.make_async_copy(held.at[span, :], out.at[span, :], sent.at[i]))
        copies[-1].start()
    for copy in copies:
        copy.wait()


def whole(*shape):
    return pl.BlockSpec(shape, lambda *_: (0,) * len(shape))


def shaped(*shape, dtype=f32):
    return jax.ShapeDtypeStruct(shape, dtype)


def run(kernel, grid, scalars, in_specs, operands, outs, out_specs, scratch, mega, flops):
    return pl.pallas_call(
        kernel,
        out_shape=outs,
        grid_spec=pltpu.PrefetchScalarGridSpec(
            num_scalar_prefetch=len(scalars), grid=grid, in_specs=in_specs, out_specs=out_specs,
            scratch_shapes=scratch,
        ),
        compiler_params=pltpu.CompilerParams(vmem_limit_bytes=mega * 1024 * 1024),
        cost_estimate=pl.CostEstimate(flops=flops, bytes_accessed=10**6, transcendentals=0),
    )(*scalars, *operands)


def passed(value, axis, steps):
    count = lax.axis_size(axis)
    return lax.ppermute(value, axis, [(s, (s + steps) % count) for s in range(count)])


def swapped(value, axis, bit):
    count = lax.axis_size(axis)
    return lax.ppermute(value, axis, [(s, s ^ bit) for s in range(count)])


def on_device(
    fine_nodes, fine_edges, fine_senders, fine_halo, fine_pool, quarter_edges, quarter_senders,
    quarter_halo, quarter_pool, coarse_edges, coarse_senders, edge_in, edge_out, node_in, node_out,
):
    n_sub, n_patch = lax.axis_size("sub"), lax.axis_size("patch")
    sub, patch = lax.axis_index("sub").astype(jnp.int32), lax.axis_index("patch").astype(jnp.int32)
    rows, degree, w = fine_edges.shape
    q_rows, q_degree, _ = quarter_edges.shape
    margin, q_margin = fine_halo.shape[1], quarter_halo.shape[1]
    piece, c_degree, _ = coarse_edges.shape
    total = coarse_senders.shape[0]
    block = total // n_patch
    part, c_part = q_rows // 2, block // 2
    tile = min(1024, q_rows)
    lines = part // LANES
    height = -(-lines // 8) * 8
    core = sub % 2
    flip = core.reshape(1)
    patch_core = jnp.stack([patch, core])
    layers = (edge_in, edge_out, node_in, node_out)
    layer_specs = [whole(*x.shape) for x in layers]
    in_hbm, in_vmem = pl.BlockSpec(memory_space=pl.ANY), pl.BlockSpec(memory_space=pltpu.VMEM)
    pool_rows = fine_pool.reshape(rows // LANES, LANES)
    quarter_pool_rows = quarter_pool.reshape(q_rows // LANES, LANES)
    fine_senders, quarter_senders, coarse_senders = fine_senders.T, quarter_senders.T, coarse_senders.T
    own_edges = coarse_edges.reshape(piece * c_degree, w)
    hbm = lambda x: pltpu.with_memory_space_constraint(x, pltpu.HBM)
    mats = lambda n: (n, 2 * w, 2 * w)
    short = jnp.int16
    big = 16 if total <= 2048 else 48

    ready = min(2, degree - 1)
    edges = hbm(fine_edges.transpose(1, 0, 2))
    to_next, to_previous, nodes, senders, pool, fine_weights, *here = run(
        start_kernel, (1,), (), [in_hbm] * 6,
        (hbm(fine_halo), hbm(fine_nodes), hbm(fine_senders), hbm(pool_rows), hbm(edge_in), edges),
        (
            shaped(margin, w), shaped(margin, w), shaped(rows, w), shaped(degree, rows, dtype=jnp.int32),
            shaped(*pool_rows.shape, dtype=jnp.int32), shaped(*mats(3), dtype=half), *(shaped(rows, w),) * ready,
        ),
        [
            whole(margin, w), whole(margin, w), in_vmem, in_vmem, in_vmem, whole(*mats(3)), *[in_vmem] * ready,
        ],
        [pltpu.VMEM((2, margin), jnp.int32), pltpu.VMEM((3 * w, w), f32), pltpu.SemaphoreType.DMA((ready + 5,))],
        8, 10**8,
    )
    left = passed(to_next, ("patch", "sub"), 1)
    right = passed(to_previous, ("patch", "sub"), -1)
    firsts = run(
        functools.partial(fine_first_kernel, ready, lines), (1,), (flip,),
        [whole(degree, rows), whole(rows, w), whole(*pool_rows.shape), whole(*mats(3)), in_hbm, *[whole(rows, w)] * ready],
        (senders, nodes, pool, fine_weights, edges, *here),
        (*(shaped(rows, w),) * (degree + 1), shaped(2 * height, w)),
        [whole(rows, w)] * (degree + 1) + [whole(2 * height, w)],
        [
            pltpu.VMEM((rows + 2 * w, 2 * w), half),
            pltpu.VMEM((degree - ready, rows, w), f32), pltpu.SemaphoreType.DMA((degree - ready,)),
        ],
        30, 8 * 10**9,
    )
    *before, edge_sum, counts = firsts
    fine_new, keep, send = run(
        fine_second_kernel, (1,), (flip,),
        [
            whole(degree, rows), whole(*pool_rows.shape), whole(rows, w), whole(margin, w), whole(margin, w),
            whole(2 * height, w), *[whole(rows, w)] * (degree + 1), *layer_specs,
        ],
        (fine_senders, pool_rows, fine_nodes, left, right, counts, *before, edge_sum, *layers),
        (pltpu.HBM((rows, w), f32), shaped(part + height, w), shaped(part + height, w)),
        [in_hbm, whole(part + height, w), whole(part + height, w)],
        [
            pltpu.VMEM((2 * margin, 2 * w), half), pltpu.VMEM(mats(4), half), pltpu.VMEM((rows, w), f32),
            pltpu.SemaphoreType.DMA,
        ],
        30, 4 * 10**9,
    )

    mine, theirs = keep, swapped(send, "sub", 1)
    bit = 2
    after = theirs
    while bit < n_sub:
        mine = mine + theirs
        theirs = swapped(mine, "sub", bit)
        after = mine if bit == 2 else after
        bit *= 2
    (coarse_share, chosen, quarter_before, quarter_sum, coarse_columns,
     quarter_weights, quarter_later, coarse_weights, coarse_later) = run(
        window_kernel, (1,), (patch_core,),
        [
            whole(*quarter_pool_rows.shape), whole(*pool_rows.shape),
            whole(q_rows * q_degree, w),
            pl.BlockSpec((c_degree, block), lambda i, place: (0, place[0])), *layer_specs, in_hbm,
        ],
        (quarter_pool_rows, pool_rows, quarter_edges.reshape(q_rows * q_degree, w), coarse_senders,
         *[hbm(x) for x in layers], after),
        (
            shaped(block, w), shaped(rows, block, dtype=half), shaped(q_degree, q_rows, w), shaped(q_rows, w),
            shaped(c_degree, block, w, dtype=short), shaped(*mats(2), dtype=half), shaped(*mats(4), dtype=half),
            shaped(*mats(3), dtype=half), shaped(*mats(4), dtype=half),
        ),
        [
            whole(block, w), whole(rows, block), whole(q_degree, q_rows, w), whole(q_rows, w),
            whole(c_degree, block, w), whole(*mats(2)), whole(*mats(4)), whole(*mats(3)),
            whole(*mats(4)),
        ],
        [], 16, 10**9,
    )
    mine = run(
        functools.partial(mean_kernel, lines), (1,), (), [whole(part + height, w)], (mine + theirs,),
        shaped(part, w), whole(part, w), [], 6, 10**7,
    )
    other = swapped(mine, "sub", 1)

    quarter_nodes, to_next, to_previous = run(
        quarter_nodes_kernel, (1,), (flip,), [whole(part, w), whole(part, w), whole(2, q_margin)],
        (mine, other, quarter_halo), (shaped(q_rows, w), shaped(q_margin, w), shaped(q_margin, w)),
        [whole(q_rows, w), whole(q_margin, w), whole(q_margin, w)], [], 8, 10**8,
    )
    left = passed(to_next, "patch", 1)
    right = passed(to_previous, "patch", -1)
    across = [own_edges]
    bit = 2
    while bit < n_sub:
        across += [swapped(value, "sub", bit) for value in across]
        bit *= 2
    edge_pieces = []
    for value in across:
        edge_pieces += [value, swapped(value, "sub", 1)]
    quarter_first = run(
        functools.partial(quarter_first_kernel, tile), (1,), (),
        [whole(q_degree, q_rows), whole(q_rows, w), whole(q_degree, q_rows, w), whole(*mats(2))],
        (quarter_senders, quarter_nodes, quarter_before, quarter_weights),
        shaped(q_degree, q_rows, w), whole(q_degree, q_rows, w), [pltpu.VMEM((q_rows, 2 * w), half)], 20, 3 * 10**9,
    )
    quarter_new, own = run(
        quarter_second_kernel, (1,), (flip,),
        [
            whole(q_degree, q_rows), whole(*quarter_pool_rows.shape), whole(q_rows, w), whole(q_margin, w),
            whole(q_margin, w), whole(q_degree, q_rows, w), whole(q_rows, w), whole(block, w), whole(*mats(2)),
            whole(*mats(4)),
        ],
        (quarter_senders, quarter_pool_rows, quarter_nodes, left, right, quarter_first, quarter_sum, coarse_share,
         quarter_weights, quarter_later),
        (shaped(q_rows, w), shaped(c_part, w)), [whole(q_rows, w), whole(c_part, w)],
        [pltpu.VMEM((2 * q_margin, 2 * w), half)], 20, 2 * 10**9,
    )

    pieces = [own] + [passed(own, "patch", -j) for j in range(1, n_patch)]
    partner = [swapped(pieces[j], "sub", 1) for j in range(1, n_patch)]
    base, own_partner = run(
        base_kernel, (1,), (flip,),
        [whole(*pool_rows.shape), whole(*quarter_pool_rows.shape), whole(q_rows, w), whole(block, w), whole(rows, w)],
        (pool_rows, quarter_pool_rows, quarter_new, coarse_share, hbm(fine_new)), (shaped(rows, w), shaped(c_part, w)),
        [whole(rows, w), whole(c_part, w)], [], 16, 10**9,
    )
    place = jnp.stack([patch, core, sub])
    before, edge_sum = run(
        coarse_first_kernel, (1,), (place,),
        [
            whole(c_part, w), whole(c_part, w), whole(c_degree, block, w), whole(*mats(3)),
            *[whole(*own_edges.shape)] * n_sub,
        ],
        (own, own_partner, coarse_columns, coarse_weights, *edge_pieces),
        (shaped(c_degree, block, w), shaped(block, w)), [whole(c_degree, block, w), whole(block, w)],
        [
            pltpu.VMEM((block, w), f32), pltpu.VMEM((block * c_degree, w), f32),
            pltpu.VMEM((block + 2 * w, 2 * w), half),
        ],
        16, 10**9,
    )
    return run(
        functools.partial(coarse_kernel, n_patch), (1,), (place,),
        [
            *[whole(c_part, w)] * (2 * n_patch), whole(c_degree, block, w), whole(rows, block), whole(rows, w),
            whole(c_degree, block, w), whole(block, w), whole(*mats(3)), whole(*mats(4)),
        ],
        (own, own_partner, *pieces[1:], *partner, coarse_columns, chosen, base, before, edge_sum, coarse_weights,
         coarse_later),
        shaped(rows, w), in_hbm,
        [
            pltpu.VMEM((total - block, w), f32), pltpu.VMEM((block, w), f32),
            pltpu.VMEM((total - block, 2 * w), half), pltpu.VMEM((block, w), f32), pltpu.VMEM((rows, w), f32),
            pltpu.SemaphoreType.DMA((4,)),
        ],
        big, 2 * 10**9,
    )


def solution(mesh):
    split = P(("groups", "patch", "sub"))
    patches = P(("groups", "patch"))
    return jax.shard_map(
        on_device,
        mesh=mesh,
        in_specs=(
            split, split, split, split, split, patches, patches, patches, patches, split, P("groups"),
            P(), P(), P(), P(),
        ),
        out_specs=split,
        check_vma=False,
    )
```
